256 devices in a mesh: dp: 2 (over core), order: 16 (over z_lo, y), ens: 8 (over z_hi, x).
Axes of the slice: x: 4, y: 4, z: 8 (z_hi: 2, z_lo: 4; z = z_hi * 4 + z_lo), core: 2. Of those that a mesh axis runs over, the one named last changes fastest.
Arguments:
- fourier: bfloat16 [2, 16, 320, 40960], P('dp', 'ens', 'order'), may hold values from -20 to 20
- analysis: bfloat16 [320, 320, 320], P(None, 'order'), may hold values from -0.3125 to 0.3125
- target: bfloat16 [2, 320, 40960], P('dp', 'ens', 'order'), may hold values from -6 to 6
- band_ids: int32 [320, 320], P('ens', 'order'), may hold values from 0 to 15, as said below
- partners: int32 [16, 4], replicated, may hold values from 0 to 15, as said below
- band_cotangent: float32 [2, 16], replicated, may hold values from 0.5 to 4
Outputs:
- grad_fourier: bfloat16 [2, 16, 320, 40960], P('dp', 'ens', 'order')
- grad_analysis: float32 [320, 320, 320], P(('dp', 'ens'), 'order')
- loss_bands: float32 [16], replicated
The draws below stay inside these ranges and needn't reach their ends.
Inputs may be any that keep to these rules, and one draw needn't show every extreme that they name: band_ids[l,m] depends on l only, never falls as l grows, starts at 0 and takes every band from 0 to 15. `partners`: each row names 4 different members, none equal to the row's own member.
All inputs are finite; a program needn't handle non-finite values.
Results may differ from the reference program's by a relative error of at most 0.0085.
Values may be sent and summed in bfloat16 or wider, within the bound.
No kernel may reach another device: no remote copies, remote signals or barrier semaphores. Data moves between devices by JAX's collectives and lax.ppermute only.
A program may use at most 128 MiB of HBM per device.

```python
import math
import jax
import jax.numpy as jnp
from jax import lax

MEMBERS = 16
NLAT = 320
L = 320
C = 64
NBANDS = 16
PARTNERS = 4
MM = 320
B = 2


def blocked_factor(key, count, low):
    block = max(count // 16, 1)
    groups = (count + block - 1) // block
    first, second = jax.random.split(key, 2)
    coarse = jnp.exp(jax.random.uniform(first, (groups,), jnp.float32, math.log(low), 0.0))
    rough = jax.random.uniform(second, (count,), jnp.float32, 0.7, 1.4)
    return jnp.repeat(coarse, block)[:count] * rough


def draw_fourier(key, part):
    first, second, third, fourth, fifth, sixth = jax.random.split(key, 6)
    shape = (B, MEMBERS, NLAT, MM * 2 * C)
    channel_scale = jnp.exp(jax.random.uniform(second, (C,), jnp.float32, 0.0, math.log(10.0)))
    row_scale = jnp.exp(jax.random.uniform(third, (NLAT,), jnp.float32, 0.0, math.log(10.0)))
    scale = row_scale[:, None, None] * channel_scale[None, None, :] / 3.0
    scale = jnp.broadcast_to(scale, (NLAT, MM * 2, C)).reshape(NLAT, MM * 2 * C)
    order_spread = blocked_factor(fifth, MM, 0.1)
    row_spread = blocked_factor(sixth, NLAT, 0.3)
    spread = row_spread[:, None, None] * order_spread[None, :, None]
    spread = jnp.broadcast_to(spread, (NLAT, MM, 2 * C)).reshape(NLAT, MM * 2 * C)
    common = jax.random.normal(fourth, (B, 1, NLAT, MM * 2 * C), jnp.float32)
    individual = jax.random.normal(first, shape, jnp.float32)
    base = 0.5 * common + spread[None, None] * individual
    values = jnp.clip(base, -6.0, 6.0) * scale[None, None]
    return jnp.clip(values, -20.0, 20.0).astype(jnp.bfloat16)


def draw_band_ids(key, part):
    shuffled = jax.random.permutation(key, L - 1)[:NBANDS - 1] + 1
    cuts = jnp.sort(shuffled)
    degrees = jnp.arange(L, dtype=jnp.int32)
    band = jnp.sum((degrees[:, None] >= cuts[None, :]).astype(jnp.int32), axis=1)
    return jnp.broadcast_to(band[:, None], (L, MM)).astype(jnp.int32)


def draw_partners(key, part):
    scores = jax.random.randint(key, (MEMBERS, MEMBERS - 1), 0, 1 << 20) * MEMBERS + jnp.arange(MEMBERS - 1, dtype=jnp.int32)[None, :]
    picks = jnp.argsort(scores, axis=1)[:, :PARTNERS] + 1
    return ((jnp.arange(MEMBERS, dtype=jnp.int32)[:, None] + picks) % MEMBERS).astype(jnp.int32)


def steps_of(own_key, dims, shards, least, high):
    def one(dim, parts):
        heights = jax.random.uniform(jax.random.fold_in(jax.random.fold_in(own_key, 6), dim), (parts,), jnp.float32, least / len(shards), high / len(shards))
        return jnp.repeat(jnp.exp(heights), dims[dim] // parts).reshape((-1,) + (1,) * (len(dims) - dim - 1))

    gain = one(*shards[0])
    for cut in shards[1:]:
        gain = gain * one(*cut)
    return gain


def centred(key, dims, deviation, limit, cuts=(), held_as=jnp.bfloat16):
    entries = deviation * jax.random.normal(key, dims, jnp.float32)
    if cuts:
        entries = entries * steps_of(key, dims, cuts, -0.22, 0.18)
    return jnp.clip(entries, -limit, limit).astype(held_as)


def setup_inputs(seed: int = 0) -> dict:
    splits = jax.random.split(jax.random.key(seed), 7)
    fourier = draw_fourier(jax.random.fold_in(splits[6], 71), 0)
    analysis = centred(splits[1], (NLAT, MM, L), NLAT ** -0.5, 0.3125, ((1, 16),))
    target = centred(splits[2], (B, L, MM * 2 * C), 1.0, 6.0, ((0, 2), (1, 8), (2, 16)))
    band_ids = draw_band_ids(jax.random.fold_in(splits[6], 71), 0)
    partners = draw_partners(jax.random.fold_in(splits[6], 71), 0)
    band_cotangent = jnp.clip(jnp.exp(jax.random.uniform(splits[5], (B, NBANDS), jnp.float32, math.log(0.5), math.log(4.0))), 0.5, 4.0)
    return {"fourier": fourier, "analysis": analysis, "target": target, "band_ids": band_ids, "partners": partners, "band_cotangent": band_cotangent}


HIGHEST = lax.Precision.HIGHEST
EPSILON = 1e-06
WEIGHT_RATIO = 1.0 / 64.0

def band_terms(grams, partners, cotangent):
    diagonal_part = jnp.diagonal(grams, axis1=2, axis2=3)
    squared = diagonal_part[..., :, None] + diagonal_part[..., None, :] - 2.0 * grams
    distance = jnp.sqrt(squared + EPSILON)
    member_ids = jnp.arange(MEMBERS, dtype=jnp.int32)
    counts = lax.optimization_barrier(jnp.sum((partners[:, :, None] == member_ids[None, None, :]).astype(jnp.float32), axis=1))
    obs_dist = distance[:, :, :MEMBERS, MEMBERS]
    pair_dist = distance[:, :, :MEMBERS, :MEMBERS]
    scores = lax.optimization_barrier(jnp.mean(obs_dist, axis=-1)) - lax.optimization_barrier(jnp.sum(counts * pair_dist, axis=(-2, -1))) / (2.0 * MEMBERS * PARTNERS)
    scaled = cotangent * (16.0 * MEMBERS * NLAT)
    symmetric = counts + counts.T
    obs_weight = scaled[..., None] / (MEMBERS * obs_dist)
    pair_weight = scaled[..., None, None] * symmetric / (2.0 * MEMBERS * PARTNERS * pair_dist)
    identity = jnp.eye(MEMBERS, dtype=jnp.float32)
    member_part = pair_weight + identity * (obs_weight - lax.optimization_barrier(jnp.sum(pair_weight, axis=-1)))[..., None]
    mixing = jnp.concatenate([member_part, -obs_weight[..., None]], axis=-1)
    return (scores, mixing)

def reference(fourier, analysis, target, band_ids, partners, band_cotangent):
    width = 2 * C
    grid = fourier.reshape(B, MEMBERS, NLAT, MM, width)
    observed_all = target.reshape(B, L, MM, width)
    degrees = jnp.arange(L, dtype=jnp.int32)
    band_range = jnp.arange(NBANDS, dtype=jnp.int32)
    order_range = jnp.arange(MM, dtype=jnp.int32)

    def stacked_at(order):
        grid_m = lax.dynamic_index_in_dim(grid, order, 3, keepdims=False)
        weight_m = lax.dynamic_index_in_dim(analysis, order, 1, keepdims=False)
        spec = jnp.einsum('bitq,tl->bilq', grid_m.astype(jnp.float32), weight_m.astype(jnp.float32), precision=HIGHEST)
        keep = degrees >= order
        spec = jnp.where(keep[None, None, :, None], spec, 0.0).astype(jnp.bfloat16)
        observed = lax.dynamic_index_in_dim(observed_all, order, 2, keepdims=False)
        observed = jnp.where(keep[None, :, None], observed, jnp.zeros((), jnp.bfloat16))
        stacked = jnp.concatenate([spec, observed[:, None]], axis=1)
        column = lax.dynamic_index_in_dim(band_ids, order, 1, keepdims=False)
        one_hot = (column[:, None] == band_range[None, :]).astype(jnp.float32)
        return (grid_m, weight_m, stacked, one_hot)

    def gram_step(total, order):
        grid_m, weight_m, stacked, one_hot = stacked_at(order)
        values = stacked.astype(jnp.float32)
        terms = jnp.einsum('bilq,bjlq->bijl', values, values, precision=HIGHEST)
        return (total + jnp.einsum('bijl,lk->bkij', terms, one_hot, precision=HIGHEST), None)
    start = jnp.zeros((B, NBANDS, MEMBERS + 1, MEMBERS + 1), jnp.float32)
    grams, unused = lax.scan(gram_step, start, order_range)
    scores, mixing = band_terms(grams, partners, band_cotangent)
    loss_bands = lax.optimization_barrier(jnp.sum(band_cotangent * scores, axis=0))

    def grad_step(order):
        grid_m, weight_m, stacked, one_hot = stacked_at(order)
        spread = jnp.einsum('lk,bkij->blij', one_hot, mixing, precision=HIGHEST)
        grad_spec = jnp.einsum('blij,bjlq->bilq', spread, stacked.astype(jnp.float32), precision=HIGHEST).astype(jnp.bfloat16)
        grad_values = grad_spec.astype(jnp.float32)
        grid_grad = jnp.einsum('bilq,tl->bitq', grad_values, weight_m.astype(jnp.float32), precision=HIGHEST).astype(jnp.bfloat16)
        weight_grad = jnp.einsum('bitq,bilq->tl', grid_m.astype(jnp.float32), grad_values, precision=HIGHEST) * WEIGHT_RATIO
        return (grid_grad, weight_grad)
    grid_grads, weight_grads = lax.map(grad_step, order_range)
    grad_fourier = jnp.transpose(grid_grads, (1, 2, 3, 0, 4)).reshape(B, MEMBERS, NLAT, MM * width)
    grad_analysis = jnp.transpose(weight_grads, (1, 0, 2))
    return (grad_fourier, grad_analysis, loss_bands)
```

```python
import jax
import jax.numpy as jnp
import numpy as np
from jax import lax
from jax.experimental import pallas as pl
from jax.experimental.pallas import tpu as pltpu
from jax.sharding import Mesh
from jax.sharding import PartitionSpec as P

MEMBERS = 16
NLAT = 320
L = 320
NBANDS = 16
PARTNERS = 4
JJ = MEMBERS + 1
ORDER = ("order_0", "order_1")
ENS = ("ens_0", "ens_1")
DP_ENS = ("dp", "ens_0", "ens_1")
EVERY = ORDER + ENS
EPSILON = 1e-06
WEIGHT_RATIO = 1.0 / 64.0
BF = jnp.bfloat16
F32 = jnp.float32
GROUP = 16
NGROUPS = L // GROUP
WIDE = 384
VMEM_LIMIT = 56 * 1024 * 1024


def selections():
    full = np.zeros((NLAT, 640), np.float32)
    half = np.zeros((2, NLAT, WIDE), np.float32)
    for t in range(NLAT):
        full[t, 2 * t : 2 * t + 2] = 1.0
        o, rest = divmod(t, 20)
        h, s = divmod(rest, 10)
        half[h, t, 24 * o + 2 * s : 24 * o + 2 * s + 2] = 1.0
    return full, half


FULL, HALF = selections()


def dot(a, b, ca=1, cb=0):
    return lax.dot_general(a, b, (((ca,), (cb,)), ((), ())), preferred_element_type=F32)


def iota(shape, dim):
    return lax.broadcasted_iota(jnp.int32, shape, dim)


def swap_halves(x):
    return pltpu.roll(x, 64, x.ndim - 1)


def split2(x):
    high = x.astype(BF)
    return high, (x - high.astype(F32)).astype(BF)


def split3(x):
    high = x.astype(BF)
    rest = x - high.astype(F32)
    mid = rest.astype(BF)
    return high, mid, (rest - mid.astype(F32)).astype(BF)


def pack_kernel(x_ref, o_ref):
    for p in range(4):
        for b in range(2):
            for s in range(2):
                o_ref[2 * p + b, 20 * s : 20 * s + 20] = x_ref[:, 5 * p + 3 * b + s]
        m = 5 * p + 2
        first = x_ref[0:10, m].astype(F32)
        second = x_ref[10:20, m].astype(F32)
        low = iota(first.shape, 2) < 64
        zeros = jnp.zeros((2, 2, 128), BF)
        o_ref[2 * p, 40:50] = jnp.where(low, first, swap_halves(second)).astype(BF)
        o_ref[2 * p + 1, 40:50] = jnp.where(low, swap_halves(first), second).astype(BF)
        o_ref[2 * p, 50:52] = zeros
        o_ref[2 * p + 1, 50:52] = zeros


def unpack_kernel(y_ref, x_ref):
    for p in range(4):
        for b in range(2):
            for s in range(2):
                x_ref[:, 5 * p + 3 * b + s] = y_ref[2 * p + b, 20 * s : 20 * s + 20]
        m = 5 * p + 2
        first = y_ref[2 * p, 40:50].astype(F32)
        second = y_ref[2 * p + 1, 40:50].astype(F32)
        low = iota(first.shape, 2) < 64
        x_ref[0:10, m] = jnp.where(low, first, swap_halves(second)).astype(BF)
        x_ref[10:20, m] = jnp.where(low, swap_halves(first), second).astype(BF)


def pack(x):
    return pl.pallas_call(
        pack_kernel,
        grid=(16,),
        out_shape=jax.ShapeDtypeStruct((128, 52, 2, 128), BF),
        in_specs=[pl.BlockSpec((20, 20, 2, 128), lambda o: (0, o, 0, 0))],
        out_specs=pl.BlockSpec((8, 52, 2, 128), lambda o: (o, 0, 0, 0)),
        name="pack",
    )(x)


def unpack(y):
    return pl.pallas_call(
        unpack_kernel,
        grid=(16,),
        out_shape=jax.ShapeDtypeStruct((20, 320, 2, 128), BF),
        in_specs=[pl.BlockSpec((8, 52, 2, 128), lambda o: (o, 0, 0, 0))],
        out_specs=pl.BlockSpec((20, 20, 2, 128), lambda o: (0, o, 0, 0)),
        name="unpack",
    )(y)


def target_kernel(t_ref, band_ref, o_ref):
    bands = jnp.broadcast_to(band_ref[:, 0:1].astype(F32), (40, 128))
    low = iota((40, 128), 1) < 64
    for p in range(4):
        middle = t_ref[:, 640 * p + 256 : 640 * p + 384].astype(F32)
        for b in range(2):
            start = 640 * p + WIDE * b
            o_ref[2 * p + b, :, 0:256] = t_ref[:, start : start + 256]
            part = middle if b == 0 else swap_halves(middle)
            o_ref[2 * p + b, :, 256:384] = jnp.where(low, part, bands).astype(BF)


def target_blocks(target, bands):
    return pl.pallas_call(
        target_kernel,
        out_shape=jax.ShapeDtypeStruct((8, 40, WIDE), BF),
        in_specs=[pl.BlockSpec(memory_space=pltpu.VMEM)] * 2,
        out_specs=pl.BlockSpec(memory_space=pltpu.VMEM),
        name="target_blocks",
    )(target, bands)


def own_orders(place_ref):
    ens = place_ref[1]
    pair = ens // 2
    odd = ens % 2
    first = 5 * pair + 3 * odd
    return first, first + 1, 5 * pair + 2


def fetch_orders(place_ref, analysis_ref, own_ref, sem):
    copies = [
        pltpu.make_async_copy(analysis_ref.at[m], own_ref.at[k], sem.at[k])
        for k, m in enumerate(own_orders(place_ref))
    ]
    for copy in copies:
        copy.start()
    for copy in copies:
        copy.wait()


def rows_of(rows_ref, e, start, count):
    block = rows_ref[:, e, start : start + count, :].astype(F32)
    return block.reshape(16 * count, 128).astype(BF)


def two_rows_of(rows_ref, g, start, count):
    return jnp.concatenate(
        [rows_of(rows_ref, 2 * g + k, start, count) for k in range(2)], axis=1
    )


def spectra_kernel(
    place_ref, analysis_ref, rows_ref, target_ref, full_ref, half_ref,
    stacked_ref, grams_ref, own_ref, to_full_ref, to_half_ref, terms_ref, sem,
):
    fetch_orders(place_ref, analysis_ref, own_ref, sem)
    orders = own_orders(place_ref)
    base = place_ref[0] * 20
    for slot in range(2):
        spread = dot(own_ref[slot], full_ref[...], 0, 0)
        member = iota(spread.shape, 1) % 2
        for i in range(2):
            to_full_ref[slot, i] = jnp.where(member == i, spread, 0.0).astype(BF)
    for h in range(2):
        spread = dot(own_ref[2], half_ref[h], 0, 0)
        member = iota(spread.shape, 1) % 2
        for i in range(2):
            to_half_ref[h, i] = jnp.where(member == i, spread, 0.0).astype(BF)
    degree = iota((L, 256), 0)
    low = iota((L, 128), 1) < 64

    def transform(g, carry):
        for slot in range(2):
            values = two_rows_of(rows_ref, g, 40 * slot, 40)
            keep = degree >= base + orders[slot]
            for i in range(2):
                spec = dot(to_full_ref[slot, i], values)
                spec = jnp.where(keep, spec, 0.0).astype(BF)
                for k in range(2):
                    stacked_ref[4 * g + 2 * k + i, :, 128 * slot : 128 * slot + 128] = spec[
                        :, 128 * k : 128 * k + 128
                    ]
        values = two_rows_of(rows_ref, g, 80, 24)
        keep = (degree >= base + orders[2])[:, :128] & low
        for i in range(2):
            first = dot(to_half_ref[0, i], values)
            second = dot(to_half_ref[1, i], values)
            for k in range(2):
                spec = first[:, 128 * k : 128 * k + 128] + swap_halves(
                    second[:, 128 * k : 128 * k + 128]
                )
                stacked_ref[4 * g + 2 * k + i, :, 256:384] = jnp.where(keep, spec, 0.0).astype(BF)
        return carry

    lax.fori_loop(0, 4, transform, 0)

    degree_wide = iota((L, WIDE), 0)
    lane_wide = iota((L, WIDE), 1)
    own_order = jnp.where(
        lane_wide < 128, orders[0], jnp.where(lane_wide < 256, orders[1], orders[2])
    )
    keep = (degree_wide >= base + own_order) & (lane_wide < 320)
    stacked_ref[MEMBERS] = jnp.where(keep, target_ref[...].astype(F32), 0.0).astype(BF)

    size = JJ * GROUP
    same = (iota((size, size), 0) & 15) == (iota((size, size), 1) & 15)
    gather = ((iota((size, 128), 0) >> 4) == iota((size, 128), 1)).astype(F32).astype(BF)

    def gram(g, carry):
        start = pl.multiple_of(g * GROUP, GROUP)
        block = stacked_ref[:, pl.ds(start, GROUP), :].reshape(size, WIDE)
        products = jnp.where(same, dot(block, block, 1, 1), 0.0)
        high, mid, low_part = split3(products)
        sums = dot(high, gather) + dot(mid, gather) + dot(low_part, gather)
        terms_ref[:, pl.ds(start, GROUP), :] = sums.reshape(JJ, GROUP, 128)
        return carry

    lax.fori_loop(0, NGROUPS, gram, 0)

    bands = target_ref[:, 256:384].astype(F32)
    column = jnp.broadcast_to(bands[:, 64:65], (L, 128))
    one_hot = (column == iota((L, 128), 1).astype(F32)).astype(F32).astype(BF)
    blocks = [jnp.zeros((NBANDS, 128), F32) for _ in range(3)]
    for i in range(JJ):
        parts = split3(terms_ref[i])
        total = sum(dot(one_hot, part, 0, 0) for part in parts)[:NBANDS]
        shift = JJ * (i % 7)
        blocks[i // 7] = blocks[i // 7] + (pltpu.roll(total, shift, 1) if shift else total)
    for n in range(3):
        grams_ref[NBANDS * n : NBANDS * n + NBANDS, :] = blocks[n]


def spectra(place, analysis, rows, target, full, half):
    vmem = pl.BlockSpec(memory_space=pltpu.VMEM)
    return pl.pallas_call(
        spectra_kernel,
        out_shape=[
            jax.ShapeDtypeStruct((JJ, L, WIDE), BF),
            jax.ShapeDtypeStruct((3 * NBANDS, 128), F32),
        ],
        in_specs=[
            pl.BlockSpec(memory_space=pltpu.SMEM),
            pl.BlockSpec(memory_space=pl.ANY),
            vmem, vmem, vmem, vmem,
        ],
        out_specs=[vmem, vmem],
        scratch_shapes=[
            pltpu.VMEM((3, NLAT, L), BF),
            pltpu.VMEM((2, 2, L, 640), BF),
            pltpu.VMEM((2, 2, L, WIDE), BF),
            pltpu.VMEM((JJ, L, 128), F32),
            pltpu.SemaphoreType.DMA((3,)),
        ],
        compiler_params=pltpu.CompilerParams(vmem_limit_bytes=VMEM_LIMIT),
        name="spectra",
    )(place, analysis, rows, target, full, half)


def gradient_kernel(
    place_ref, analysis_ref, rows_ref, stacked_ref, target_ref, grams_ref, counts_ref,
    symmetric_ref, cotangent_ref, full_ref, half_ref,
    back_ref, weight_ref, loss_ref,
    own_ref, from_full_ref, from_half_ref, grad_ref, full_sum_ref, half_sum_ref, sem,
):
    fetch_orders(place_ref, analysis_ref, own_ref, sem)
    grams = jnp.sum(grams_ref[...], axis=0)
    lane = iota((NBANDS, 128), 1)
    inside = lane < MEMBERS
    rows = []
    own_power = jnp.zeros((NBANDS, 128), F32)
    for i in range(JJ):
        shift = JJ * (i % 7)
        block = grams[NBANDS * (i // 7) : NBANDS * (i // 7) + NBANDS]
        block = pltpu.roll(block, 128 - shift, 1) if shift else block
        rows.append(jnp.where(lane < JJ, block, 0.0))
        own_power = own_power + jnp.where(lane == i, rows[i], 0.0)
    cotangent = cotangent_ref[...]
    scaled = cotangent * (16.0 * MEMBERS * NLAT)
    mixing = []
    score = jnp.zeros((NBANDS, 128), F32)
    for i in range(MEMBERS):
        squared = rows[i][:, i : i + 1] + own_power - 2.0 * rows[i]
        distance = jnp.sqrt(jnp.maximum(squared, 0.0) + EPSILON)
        observed = distance[:, MEMBERS : MEMBERS + 1]
        pairs = jnp.where(inside, counts_ref[i : i + 1, :] * distance, 0.0)
        score = score + observed / MEMBERS - jnp.sum(pairs, axis=1, keepdims=True) / (
            2.0 * MEMBERS * PARTNERS
        )
        observed_weight = scaled[:, :1] / (MEMBERS * observed)
        pair_weight = scaled * symmetric_ref[i : i + 1, :] / (2.0 * MEMBERS * PARTNERS * distance)
        pair_weight = jnp.where(inside, pair_weight, 0.0)
        own = observed_weight - jnp.sum(pair_weight, axis=1, keepdims=True)
        row = pair_weight + jnp.where(lane == i, own, 0.0)
        mixing.append(row + jnp.where(lane == MEMBERS, -observed_weight, 0.0))
    loss_ref[...] = score * cotangent

    size = MEMBERS * GROUP
    wide = JJ * GROUP
    widen = (iota((128, wide), 0) == (iota((128, wide), 1) >> 4)).astype(F32).astype(BF)
    mix_high, mix_low = split2(jnp.concatenate(mixing, axis=0))
    mix_high = dot(mix_high, widen).astype(BF)
    mix_low = dot(mix_low, widen).astype(BF)
    same_member = (iota((size, size), 0) >> 4) == (iota((size, size), 1) >> 4)
    band_of_column = (iota((size, size), 1) & 15).astype(F32)
    same_degree = (iota((size, wide), 0) & 15) == (iota((size, wide), 1) & 15)

    def mix(g, carry):
        start = pl.multiple_of(g * GROUP, GROUP)
        bands = target_ref[pl.ds(start, GROUP), 256:384].astype(F32)[:, 64:65]
        column = jnp.concatenate([jnp.broadcast_to(bands, (GROUP, size))] * MEMBERS, axis=0)
        pick = (same_member & (column == band_of_column)).astype(F32).astype(BF)
        block = stacked_ref[:, pl.ds(start, GROUP), :].reshape(wide, WIDE)
        high = jnp.where(same_degree, dot(pick, mix_high), 0.0).astype(BF)
        low = jnp.where(same_degree, dot(pick, mix_low), 0.0).astype(BF)
        grad = dot(high, block) + dot(low, block)
        grad_ref[:, pl.ds(start, GROUP), :] = grad.astype(BF).reshape(MEMBERS, GROUP, WIDE)
        return carry

    lax.fori_loop(0, NGROUPS, mix, 0)

    for slot in range(2):
        spread = dot(full_ref[...], own_ref[slot], 0, 0)
        member = iota(spread.shape, 0) % 2
        for i in range(2):
            from_full_ref[slot, i] = jnp.where(member == i, spread, 0.0).astype(BF)
    for h in range(2):
        spread = dot(half_ref[h], own_ref[2], 0, 0)
        member = iota(spread.shape, 0) % 2
        for i in range(2):
            from_half_ref[h, i] = jnp.where(member == i, spread, 0.0).astype(BF)
    full_sum_ref[...] = jnp.zeros_like(full_sum_ref)
    half_sum_ref[...] = jnp.zeros_like(half_sum_ref)

    def grads_of(g, i, slot):
        lanes = slice(128 * slot, 128 * slot + 128)
        return [grad_ref[4 * g + 2 * k + i, :, lanes] for k in range(2)]

    def inverse(g, carry):
        for slot in range(2):
            grads = [jnp.concatenate(grads_of(g, i, slot), axis=1) for i in range(2)]
            back = dot(from_full_ref[slot, 0], grads[0]) + dot(from_full_ref[slot, 1], grads[1])
            for k in range(2):
                part = back[:, 128 * k : 128 * k + 128].reshape(16, 40, 128)
                back_ref[:, 2 * g + k, 40 * slot : 40 * slot + 40, :] = part.astype(BF)
            values = two_rows_of(rows_ref, g, 40 * slot, 40)
            member = iota((640, L), 0) % 2
            terms = jnp.where(member == 0, dot(values, grads[0], 1, 1), dot(values, grads[1], 1, 1))
            full_sum_ref[slot] += terms
        pieces = [grads_of(g, i, 2) for i in range(2)]
        grads = [jnp.concatenate(pieces[i], axis=1) for i in range(2)]
        swapped = [
            jnp.concatenate([swap_halves(piece.astype(F32)).astype(BF) for piece in pieces[i]], axis=1)
            for i in range(2)
        ]
        first = dot(from_half_ref[0, 0], grads[0]) + dot(from_half_ref[0, 1], grads[1])
        second = dot(from_half_ref[1, 0], swapped[0]) + dot(from_half_ref[1, 1], swapped[1])
        back = first + second
        for k in range(2):
            part = back[:, 128 * k : 128 * k + 128].reshape(16, 24, 128)
            back_ref[:, 2 * g + k, 80:104, :] = part.astype(BF)
        values = two_rows_of(rows_ref, g, 80, 24)
        member = iota((WIDE, L), 0) % 2
        for h, sides in enumerate((grads, swapped)):
            half_sum_ref[h] += jnp.where(
                member == 0, dot(values, sides[0], 1, 1), dot(values, sides[1], 1, 1)
            )
        return carry

    lax.fori_loop(0, 4, inverse, 0)

    for slot in range(3):
        if slot < 2:
            parts = split2(full_sum_ref[slot])
            weight = dot(full_ref[...], parts[0]) + dot(full_ref[...], parts[1])
        else:
            weight = jnp.zeros((NLAT, L), F32)
            for h in range(2):
                parts = split2(half_sum_ref[h])
                weight = weight + dot(half_ref[h], parts[0]) + dot(half_ref[h], parts[1])
        weight = weight * WEIGHT_RATIO
        for c in range(16):
            weight_ref[c, slot] = weight[20 * c : 20 * c + 20].astype(BF)


def gradient(place, analysis, rows, stacked, target, grams, counts, symmetric, cotangent, full, half):
    vmem = pl.BlockSpec(memory_space=pltpu.VMEM)
    return pl.pallas_call(
        gradient_kernel,
        out_shape=[
            jax.ShapeDtypeStruct((16, 8, 104, 128), BF),
            jax.ShapeDtypeStruct((16, 3, 20, L), BF),
            jax.ShapeDtypeStruct((NBANDS, 128), F32),
        ],
        in_specs=[
            pl.BlockSpec(memory_space=pltpu.SMEM),
            pl.BlockSpec(memory_space=pl.ANY),
        ]
        + [vmem] * 9,
        out_specs=[vmem] * 3,
        scratch_shapes=[
            pltpu.VMEM((3, NLAT, L), BF),
            pltpu.VMEM((2, 2, 640, L), BF),
            pltpu.VMEM((2, 2, WIDE, L), BF),
            pltpu.VMEM((MEMBERS, L, WIDE), BF),
            pltpu.VMEM((2, 640, L), F32),
            pltpu.VMEM((2, WIDE, L), F32),
            pltpu.SemaphoreType.DMA((3,)),
        ],
        compiler_params=pltpu.CompilerParams(vmem_limit_bytes=VMEM_LIMIT),
        name="gradient",
    )(place, analysis, rows, stacked, target, grams, counts, symmetric, cotangent, full, half)


def finish_kernel(r_ref, o_ref):
    def both(e, slot):
        return r_ref[e, slot].astype(F32) + r_ref[8 + e, slot].astype(F32)

    for p in range(4):
        for b in range(2):
            for s in range(2):
                o_ref[:, 5 * p + 3 * b + s, :] = both(2 * p + b, s)
        o_ref[:, 5 * p + 2, :] = both(2 * p, 2) + both(2 * p + 1, 2)


def finish(received):
    return pl.pallas_call(
        finish_kernel,
        out_shape=jax.ShapeDtypeStruct((20, 20, L), F32),
        in_specs=[pl.BlockSpec(memory_space=pltpu.VMEM)],
        out_specs=pl.BlockSpec(memory_space=pltpu.VMEM),
        name="finish",
    )(received)


def exchange(x, axes):
    return lax.all_to_all(x, axes, split_axis=0, concat_axis=0, tiled=True)


def body(fourier, analysis, target, band_ids, partners, band_cotangent):
    place = jnp.stack([lax.axis_index(ORDER), lax.axis_index(ENS)]).astype(jnp.int32)
    full = jnp.asarray(FULL, BF)
    half = jnp.asarray(HALF, BF)
    by_order = jnp.transpose(analysis, (1, 0, 2))
    native = jnp.transpose(fourier[0].reshape(2, 20, 320, 128), (1, 2, 0, 3))
    blocks = target_blocks(target[0], band_ids)
    observed = exchange(blocks, ENS).reshape(L, WIDE)
    received = exchange(pack(native), EVERY)
    rows = received.reshape(128, 104, 128).reshape(16, 8, 104, 128)
    stacked, grams = spectra(place, by_order, rows, observed, full, half)
    grams = exchange(jnp.broadcast_to(grams, (16, *grams.shape)), ORDER).sum(axis=0)
    grams = exchange(jnp.broadcast_to(grams, (8, *grams.shape)), ENS)
    member_ids = jnp.arange(128, dtype=jnp.int32)
    counts = jnp.sum((partners[:, :, None] == member_ids[None, None, :]).astype(F32), axis=1)
    square = counts[:, :MEMBERS]
    symmetric = jnp.pad(square + square.T, ((0, 0), (0, 128 - MEMBERS)))
    cotangent = lax.dynamic_slice_in_dim(band_cotangent, lax.axis_index("dp"), 1, 0)[0]
    cotangent = jnp.broadcast_to(cotangent[:, None], (NBANDS, 128))
    back, weight, loss = gradient(
        place, by_order, rows, stacked, observed, grams, counts, symmetric, cotangent, full, half
    )
    loss_bands = lax.psum(loss[:, 0], "dp")
    returned = exchange(back.reshape(128, 104, 128).reshape(128, 52, 2, 128), EVERY)
    grad_analysis = finish(exchange(weight, DP_ENS))
    native_grad = unpack(returned)
    grad_fourier = jnp.transpose(native_grad, (2, 0, 1, 3)).reshape(1, 2, 20, 40960)
    return (grad_fourier, grad_analysis, loss_bands)


def solution(mesh):
    torus = Mesh(
        mesh.devices.reshape(mesh.shape["dp"], 4, 4, 2, 4),
        ("dp", "order_0", "order_1", "ens_0", "ens_1"),
    )
    in_specs = (
        P("dp", ENS, ORDER, None),
        P(None, ORDER, None),
        P("dp", ENS, ORDER),
        P(ENS, ORDER),
        P(),
        P(),
    )
    out_specs = (P("dp", ENS, ORDER, None), P(DP_ENS, ORDER, None), P())
    return jax.shard_map(body, mesh=torus, in_specs=in_specs, out_specs=out_specs, check_vma=False)
```

```python
import functools

import jax
import jax.numpy as jnp
import numpy as np
from jax import lax
from jax.experimental import pallas as pl
from jax.experimental.pallas import tpu as pltpu
from jax.sharding import Mesh
from jax.sharding import PartitionSpec as P

MEMBERS = 16
NLAT = 320
L = 320
NBANDS = 16
PARTNERS = 4
JJ = MEMBERS + 1
ORDER = ("order_0", "order_1")
ENS = ("ens_0", "ens_1")
DP_ENS = ("dp", "ens_0", "ens_1")
EVERY = ORDER + ENS
EPSILON = 1e-06
WEIGHT_RATIO = 1.0 / 64.0
BF = jnp.bfloat16
F32 = jnp.float32
GROUP = 16
NGROUPS = L // GROUP
WIDE = 384
VMEM_LIMIT = 48 * 1024 * 1024
VMEM = pl.BlockSpec(memory_space=pltpu.VMEM)
SMEM = pl.BlockSpec(memory_space=pltpu.SMEM)
ANY = pl.BlockSpec(memory_space=pl.ANY)


def selections():
    full = np.zeros((NLAT, 640), np.float32)
    half = np.zeros((2, NLAT, WIDE), np.float32)
    for t in range(NLAT):
        full[t, 2 * t : 2 * t + 2] = 1.0
        o, rest = divmod(t, 20)
        h, s = divmod(rest, 10)
        half[h, t, 24 * o + 2 * s : 24 * o + 2 * s + 2] = 1.0
    return full, half


def orderings():
    whole = np.zeros((320, 320), np.float32)
    half = np.zeros((2, 96, 160), np.float32)
    for t in range(20):
        h, s = divmod(t, 10)
        for i in range(2):
            for e in range(8):
                whole[40 * e + 2 * t + i, 16 * t + 2 * e + i] = 1.0
            for p in range(4):
                half[h, 24 * p + 2 * s + i, 8 * t + 2 * p + i] = 1.0
    return whole, half


FULL, HALF = selections()
WHOLE_ORDER, HALF_ORDER = orderings()


def dot(a, b, ca=1, cb=0):
    return lax.dot_general(a, b, (((ca,), (cb,)), ((), ())), preferred_element_type=F32)


def iota(shape, dim):
    return lax.broadcasted_iota(jnp.int32, shape, dim)


def swap_halves(x):
    return pltpu.roll(x, 64, x.ndim - 1)


def split2(x):
    high = x.astype(BF)
    return high, (x - high.astype(F32)).astype(BF)


def split3(x):
    high = x.astype(BF)
    rest = x - high.astype(F32)
    mid = rest.astype(BF)
    return high, mid, (rest - mid.astype(F32)).astype(BF)


def pack_kernel(x_ref, whole_ref, half_ref, o_ref):
    def columns(start, count):
        parts = [x_ref[:, 40 * k + start : 40 * k + start + count, :] for k in range(2)]
        parts = [part.astype(F32).reshape(20 * count, 128).astype(BF) for part in parts]
        return jnp.concatenate(parts, axis=1)

    for slot in range(2):
        moved = halves(dot(whole_ref[...], columns(16 * slot, 16)))
        for k in range(2):
            o_ref[k, :, 40 * slot : 40 * slot + 40, :] = moved[k].reshape(8, 40, 128).astype(BF)
    values = columns(32, 8)
    first = halves(dot(half_ref[0], values))
    second = halves(dot(half_ref[1], values))
    low = iota((96, 128), 1) < 64
    for k in range(2):
        real = jnp.where(low, first[k], swap_halves(second[k])).astype(BF)
        imaginary = jnp.where(low, swap_halves(first[k]), second[k]).astype(BF)
        for p in range(4):
            o_ref[k, 2 * p, 80:104, :] = real[24 * p : 24 * p + 24]
            o_ref[k, 2 * p + 1, 80:104, :] = imaginary[24 * p : 24 * p + 24]


def unpack_kernel(y_ref, whole_ref, half_ref, x_ref):
    for slot in range(2):
        parts = [y_ref[k, :, 40 * slot : 40 * slot + 40, :].astype(F32) for k in range(2)]
        parts = [part.reshape(320, 128).astype(BF) for part in parts]
        moved = halves(dot(whole_ref[...], jnp.concatenate(parts, axis=1)))
        for k in range(2):
            start = 40 * k + 16 * slot
            x_ref[:, start : start + 16, :] = moved[k].reshape(20, 16, 128).astype(BF)
    low = iota((96, 128), 1) < 64
    firsts, seconds = [], []
    for k in range(2):
        real, imaginary = [
            jnp.concatenate([y_ref[k, 2 * p + r, 80:104, :].astype(F32) for p in range(4)], axis=0)
            for r in range(2)
        ]
        firsts.append(jnp.where(low, real, swap_halves(imaginary)).astype(BF))
        seconds.append(jnp.where(low, swap_halves(real), imaginary).astype(BF))
    moved = halves(
        dot(half_ref[0], jnp.concatenate(firsts, axis=1))
        + dot(half_ref[1], jnp.concatenate(seconds, axis=1))
    )
    for k in range(2):
        x_ref[:, 40 * k + 32 : 40 * k + 40, :] = moved[k].reshape(20, 8, 128).astype(BF)


NATIVE = pl.BlockSpec((20, 80, 128), lambda o: (0, o, 0))
PACKED = pl.BlockSpec((2, 8, 104, 128), lambda o: (o, 0, 0, 0))


def constant(shape):
    return pl.BlockSpec(shape, lambda o: (0,) * len(shape))


def pack(x):
    return pl.pallas_call(
        pack_kernel,
        grid=(8,),
        out_shape=jax.ShapeDtypeStruct((16, 8, 104, 128), BF),
        in_specs=[NATIVE, constant((320, 320)), constant((2, 96, 160))],
        out_specs=PACKED,
        name="pack",
    )(x, jnp.asarray(WHOLE_ORDER, BF), jnp.asarray(HALF_ORDER, BF))


def unpack(y):
    return pl.pallas_call(
        unpack_kernel,
        grid=(8,),
        out_shape=jax.ShapeDtypeStruct((20, 640, 128), BF),
        in_specs=[PACKED, constant((320, 320)), constant((2, 160, 96))],
        out_specs=NATIVE,
        name="unpack",
    )(y, jnp.asarray(WHOLE_ORDER.T, BF), jnp.asarray(HALF_ORDER.transpose(0, 2, 1), BF))


def target_kernel(place_ref, t_ref, band_ref, *o_refs):
    bands = jnp.broadcast_to(band_ref[:, 0:1].astype(F32), (40, 128))
    low = iota((40, 128), 1) < 64
    for k in range(8):
        e = jnp.bitwise_xor(place_ref[1], k)

        def lanes(start):
            return t_ref[:, pl.ds(pl.multiple_of(start, 128), 128)]

        middle = lanes(2048 + 128 * (e // 2)).astype(F32)
        o_refs[k][:, 0:128] = lanes(128 * e)
        o_refs[k][:, 128:256] = lanes(1024 + 128 * e)
        odd = jnp.broadcast_to(e % 2, (40, 128)) == 1
        part = jnp.where(odd, swap_halves(middle), middle)
        o_refs[k][:, 256:384] = jnp.where(low, part, bands).astype(BF)


def target_blocks(place, target, bands):
    return pl.pallas_call(
        target_kernel,
        out_shape=[jax.ShapeDtypeStruct((40, WIDE), BF)] * 8,
        in_specs=[SMEM, VMEM, VMEM],
        out_specs=[VMEM] * 8,
        name="target_blocks",
    )(place, target, bands)


def own_orders(place_ref):
    ens = place_ref[1]
    return ens, 8 + ens, 16 + ens // 2


def fetches(place_ref, analysis_ref, own_ref, sem):
    return [
        pltpu.make_async_copy(analysis_ref.at[m], own_ref.at[k], sem.at[k])
        for k, m in enumerate(own_orders(place_ref))
    ]


def halves(x):
    return [x[:, 128 * k : 128 * k + 128] for k in range(2)]


STARTS = (0, 40, 80)
COUNTS = (40, 40, 24)


def two_rows_of(rows_ref, g, slot):
    start, count = STARTS[slot], COUNTS[slot]
    parts = [
        rows_ref[:, 2 * g + k, start : start + count, :]
        .astype(F32)
        .reshape(16 * count, 128)
        .astype(BF)
        for k in range(2)
    ]
    return jnp.concatenate(parts, axis=1)


def band_column(target_ref, start, count):
    return target_ref[pl.ds(start, count), 256:384].astype(F32)[:, 64:65]


def spectra_kernel(place_ref, analysis_ref, rows_ref, full_ref, half_ref, *refs):
    target_refs = refs[:8]
    stacked_ref, target_ref, grams_ref = refs[8:11]
    own_ref, to_full_ref, to_half_ref, terms_ref, order_ref, sem = refs[11:]
    copies = fetches(place_ref, analysis_ref, own_ref, sem)
    for copy in copies:
        copy.start()
    for k in range(8):
        order_ref[jnp.bitwise_xor(place_ref[1], k)] = target_refs[k][...].astype(F32)
    target_ref[...] = order_ref[...].reshape(L, WIDE).astype(BF)
    for copy in copies:
        copy.wait()
    base = place_ref[0] * 20
    orders = [base + m for m in own_orders(place_ref)]
    for n in range(4):
        if n < 2:
            spread = dot(own_ref[n], full_ref[...], 0, 0)
        else:
            spread = dot(own_ref[2], half_ref[n - 2], 0, 0)
        member = iota(spread.shape, 1) % 2
        for i in range(2):
            part = jnp.where(member == i, spread, 0.0).astype(BF)
            if n < 2:
                to_full_ref[n, i] = part
            else:
                to_half_ref[n - 2, i] = part
    degree = iota((L, 128), 0)
    low = iota((L, 128), 1) < 64
    keeps = [degree >= orders[0], degree >= orders[1], (degree >= orders[2]) & low]

    def transform(g, carry):
        for slot in range(3):
            values = two_rows_of(rows_ref, g, slot)
            for i in range(2):
                if slot < 2:
                    parts = halves(dot(to_full_ref[slot, i], values))
                else:
                    parts = halves(dot(to_half_ref[0, i], values))
                    other = halves(dot(to_half_ref[1, i], values))
                    parts = [parts[k] + swap_halves(other[k]) for k in range(2)]
                for k in range(2):
                    stacked_ref[4 * g + 2 * k + i, :, 128 * slot : 128 * slot + 128] = jnp.where(
                        keeps[slot], parts[k], 0.0
                    ).astype(BF)
        return carry

    lax.fori_loop(0, 4, transform, 0)
    for slot in range(3):
        lanes = slice(128 * slot, 128 * slot + 128)
        observed = jnp.where(keeps[slot], target_ref[:, lanes].astype(F32), 0.0)
        stacked_ref[MEMBERS, :, lanes] = observed.astype(BF)

    size = MEMBERS * GROUP
    same = (iota((size, size), 0) & 15) == (iota((size, size), 1) & 15)
    gather = ((iota((size, 128), 0) >> 4) == iota((size, 128), 1)).astype(F32).astype(BF)
    at_observed = iota((size, 128), 1) == MEMBERS

    def gram(g, carry):
        start = pl.multiple_of(g * GROUP, GROUP)
        block = stacked_ref[0:MEMBERS, pl.ds(start, GROUP), :].reshape(size, WIDE)
        own = stacked_ref[MEMBERS, pl.ds(start, GROUP), :].astype(F32)
        products = jnp.where(same, dot(block, block, 1, 1), 0.0)
        high, mid, low_part = split3(products)
        sums = dot(high, gather) + dot(mid, gather) + dot(low_part, gather)
        beside = jnp.concatenate([own] * MEMBERS, axis=0) * block.astype(F32)
        sums = jnp.where(at_observed, jnp.sum(beside, axis=1, keepdims=True), sums)
        last = jnp.sum(own * own, axis=1, keepdims=True)
        pieces = [sums[GROUP * i : GROUP * i + GROUP] for i in range(MEMBERS)]
        pieces.append(jnp.where(at_observed[:GROUP], last, 0.0))
        for n in range(3):
            total = pieces[7 * n]
            for i in range(7 * n + 1, min(7 * n + 7, JJ)):
                total = total + pltpu.roll(pieces[i], JJ * (i % 7), 1)
            terms_ref[n, pl.ds(start, GROUP), :] = total
        return carry

    lax.fori_loop(0, NGROUPS, gram, 0, unroll=4)

    column = jnp.broadcast_to(band_column(target_ref, 0, L), (L, 128))
    one_hot = (column == iota((L, 128), 1).astype(F32)).astype(F32).astype(BF)
    for n in range(3):
        total = sum(dot(one_hot, part, 0, 0) for part in split3(terms_ref[n]))
        grams_ref[NBANDS * n : NBANDS * n + NBANDS] = total[:NBANDS]


def spectra(place, analysis, rows, targets, full, half):
    return pl.pallas_call(
        spectra_kernel,
        out_shape=[
            jax.ShapeDtypeStruct((JJ, L, WIDE), BF),
            jax.ShapeDtypeStruct((L, WIDE), BF),
            jax.ShapeDtypeStruct((3 * NBANDS, 128), F32),
        ],
        in_specs=[SMEM, ANY] + [VMEM] * 11,
        out_specs=[VMEM] * 3,
        scratch_shapes=[
            pltpu.VMEM((3, NLAT, L), BF),
            pltpu.VMEM((2, 2, L, 640), BF),
            pltpu.VMEM((2, 2, L, WIDE), BF),
            pltpu.VMEM((3, L, 128), F32),
            pltpu.VMEM((8, 40, WIDE), F32),
            pltpu.SemaphoreType.DMA((3,)),
        ],
        compiler_params=pltpu.CompilerParams(vmem_limit_bytes=VMEM_LIMIT),
        cost_estimate=pl.CostEstimate(
            flops=10_000_000_000, bytes_accessed=12_000_000, transcendentals=0
        ),
        name="spectra",
    )(place, analysis, rows, full, half, *targets)


def gradient_kernel(
    place_ref, analysis_ref, stacked_ref, target_ref, grams_ref, counts_ref,
    symmetric_ref, cotangent_ref, full_ref, half_ref,
    back_ref, grad_ref, loss_ref,
    own_ref, from_full_ref, from_half_ref, sem,
):
    copies = fetches(place_ref, analysis_ref, own_ref, sem)
    for copy in copies:
        copy.start()
    grams = jnp.sum(grams_ref[...], axis=0)
    lane = iota((NBANDS, 128), 1)
    inside = lane < MEMBERS
    rows = []
    own_power = jnp.zeros((NBANDS, 128), F32)
    for i in range(JJ):
        shift = JJ * (i % 7)
        block = grams[NBANDS * (i // 7) : NBANDS * (i // 7) + NBANDS]
        block = pltpu.roll(block, 128 - shift, 1) if shift else block
        rows.append(jnp.where(lane < JJ, block, 0.0))
        own_power = own_power + jnp.where(lane == i, rows[i], 0.0)
    cotangent = cotangent_ref[...]
    scaled = cotangent * (16.0 * MEMBERS * NLAT)
    mixing = []
    score = jnp.zeros((NBANDS, 128), F32)
    beside = jnp.zeros((NBANDS, 128), F32)
    for i in range(MEMBERS):
        squared = rows[i][:, i : i + 1] + own_power - 2.0 * rows[i]
        distance = jnp.sqrt(jnp.maximum(squared, 0.0) + EPSILON)
        observed = distance[:, MEMBERS : MEMBERS + 1]
        pairs = jnp.where(inside, counts_ref[i : i + 1, :] * distance, 0.0)
        score = score + observed / MEMBERS - jnp.sum(pairs, axis=1, keepdims=True) / (
            2.0 * MEMBERS * PARTNERS
        )
        observed_weight = scaled[:, :1] / (MEMBERS * observed)
        pair_weight = scaled * symmetric_ref[i : i + 1, :] / (2.0 * MEMBERS * PARTNERS * distance)
        pair_weight = jnp.where(inside, pair_weight, 0.0)
        own = observed_weight - jnp.sum(pair_weight, axis=1, keepdims=True)
        mixing.append(pair_weight + jnp.where(lane == i, own, 0.0))
        beside = beside + jnp.where(lane == i, -observed_weight, 0.0)
    loss_ref[...] = score * cotangent

    size = MEMBERS * GROUP
    widen = (iota((128, size), 0) == (iota((128, size), 1) >> 4)).astype(F32).astype(BF)
    mix_high, mix_low = split2(jnp.concatenate(mixing, axis=0))
    mix_high = dot(mix_high, widen).astype(BF)
    mix_low = dot(mix_low, widen).astype(BF)
    beside = jnp.concatenate([beside, jnp.zeros((128 - NBANDS, 128), F32)], axis=0)
    beside_high, beside_low = split2(beside)
    same_member = (iota((size, size), 0) >> 4) == (iota((size, size), 1) >> 4)
    band_of_column = (iota((size, size), 1) & 15).astype(F32)
    same_degree = (iota((size, size), 0) & 15) == (iota((size, size), 1) & 15)
    band_of_lane = iota((GROUP, 128), 1).astype(F32)

    def mix(g, carry):
        start = pl.multiple_of(g * GROUP, GROUP)
        bands = band_column(target_ref, start, GROUP)
        column = jnp.concatenate([jnp.broadcast_to(bands, (GROUP, size))] * MEMBERS, axis=0)
        pick = (same_member & (column == band_of_column)).astype(F32).astype(BF)
        high = jnp.where(same_degree, dot(pick, mix_high), 0.0).astype(BF)
        low = jnp.where(same_degree, dot(pick, mix_low), 0.0).astype(BF)
        one_hot = (jnp.broadcast_to(bands, (GROUP, 128)) == band_of_lane).astype(F32).astype(BF)
        weights = dot(one_hot, beside_high) + dot(one_hot, beside_low)
        weights = jnp.concatenate(
            [jnp.broadcast_to(weights[:, i : i + 1], (GROUP, 128)) for i in range(MEMBERS)], axis=0
        )
        block = stacked_ref[0:MEMBERS, pl.ds(start, GROUP), :].reshape(size, WIDE)
        own = stacked_ref[MEMBERS, pl.ds(start, GROUP), :].astype(F32)
        grad = dot(high, block) + dot(low, block)
        for slot in range(3):
            lanes = slice(128 * slot, 128 * slot + 128)
            part = grad[:, lanes] + weights * jnp.concatenate([own[:, lanes]] * MEMBERS, axis=0)
            grad_ref[:, pl.ds(start, GROUP), lanes] = part.astype(BF).reshape(MEMBERS, GROUP, 128)
        return carry

    lax.fori_loop(0, NGROUPS, mix, 0, unroll=2)
    for copy in copies:
        copy.wait()
    for n in range(4):
        choose = full_ref[...] if n < 2 else half_ref[n - 2]
        spread = dot(choose, own_ref[min(n, 2)], 0, 0)
        member = iota(spread.shape, 0) % 2
        for i in range(2):
            part = jnp.where(member == i, spread, 0.0).astype(BF)
            if n < 2:
                from_full_ref[n, i] = part
            else:
                from_half_ref[n - 2, i] = part

    def inverse(g, carry):
        for slot in range(3):
            grads = [jnp.concatenate(grads_of(grad_ref, g, i, slot), axis=1) for i in range(2)]
            from_ref = from_full_ref.at[slot] if slot < 2 else from_half_ref.at[0]
            parts = halves(dot(from_ref[0], grads[0]) + dot(from_ref[1], grads[1]))
            if slot == 2:
                from_ref = from_half_ref.at[1]
                other = halves(dot(from_ref[0], grads[0]) + dot(from_ref[1], grads[1]))
                parts = [parts[k] + swap_halves(other[k]) for k in range(2)]
            start, count = STARTS[slot], COUNTS[slot]
            for k in range(2):
                part = parts[k].reshape(16, count, 128).astype(BF)
                back_ref[:, 2 * g + k, start : start + count, :] = part
        return carry

    lax.fori_loop(0, 4, inverse, 0)


def grads_of(grad_ref, g, i, slot):
    lanes = slice(128 * slot, 128 * slot + 128)
    return [grad_ref[4 * g + 2 * k + i, :, lanes] for k in range(2)]


def gradient(place, analysis, stacked, target, grams, counts, symmetric, cotangent, full, half):
    return pl.pallas_call(
        gradient_kernel,
        out_shape=[
            jax.ShapeDtypeStruct((16, 8, 104, 128), BF),
            jax.ShapeDtypeStruct((MEMBERS, L, WIDE), BF),
            jax.ShapeDtypeStruct((NBANDS, 128), F32),
        ],
        in_specs=[SMEM, ANY] + [VMEM] * 8,
        out_specs=[VMEM] * 3,
        scratch_shapes=[
            pltpu.VMEM((3, NLAT, L), BF),
            pltpu.VMEM((2, 2, 640, L), BF),
            pltpu.VMEM((2, 2, WIDE, L), BF),
            pltpu.SemaphoreType.DMA((3,)),
        ],
        compiler_params=pltpu.CompilerParams(vmem_limit_bytes=VMEM_LIMIT),
        cost_estimate=pl.CostEstimate(
            flops=10_000_000_000, bytes_accessed=12_000_000, transcendentals=0
        ),
        name="gradient",
    )(place, analysis, stacked, target, grams, counts, symmetric, cotangent, full, half)


def weight_kernel(
    place_ref, rows_ref, grad_ref, full_ref, half_ref, weight_ref, full_sum_ref, half_sum_ref
):
    full_sum_ref[...] = jnp.zeros_like(full_sum_ref)
    half_sum_ref[...] = jnp.zeros_like(half_sum_ref)

    def step(g, carry):
        for slot in range(3):
            values = two_rows_of(rows_ref, g, slot)
            member = iota((values.shape[0], L), 0) % 2
            sides = [[grads_of(grad_ref, g, i, slot) for i in range(2)]]
            if slot == 2:
                sides.append(
                    [[swap_halves(x.astype(F32)).astype(BF) for x in pair] for pair in sides[0]]
                )
            for h, side in enumerate(sides):
                grads = [jnp.concatenate(side[i], axis=1) for i in range(2)]
                terms = jnp.where(
                    member == 0, dot(values, grads[0], 1, 1), dot(values, grads[1], 1, 1)
                )
                if slot < 2:
                    full_sum_ref[slot] += terms
                else:
                    half_sum_ref[h] += terms
        return carry

    lax.fori_loop(0, 4, step, 0)
    for slot in range(3):
        if slot < 2:
            parts = split2(full_sum_ref[slot])
            weight = dot(full_ref[...], parts[0]) + dot(full_ref[...], parts[1])
        else:
            weight = jnp.zeros((NLAT, L), F32)
            for h in range(2):
                parts = split2(half_sum_ref[h])
                weight = weight + dot(half_ref[h], parts[0]) + dot(half_ref[h], parts[1])
        weight = weight * WEIGHT_RATIO
        for c in range(16):
            other = jnp.bitwise_xor(place_ref[2], c // 8)
            step_to = jnp.bitwise_xor(place_ref[1], c % 8)
            weight_ref[other, step_to, slot] = weight[20 * c : 20 * c + 20].astype(BF)


def weights(place, rows, grads, full, half):
    return pl.pallas_call(
        weight_kernel,
        out_shape=jax.ShapeDtypeStruct((2, 8, 3, 20, L), BF),
        in_specs=[SMEM] + [VMEM] * 4,
        out_specs=VMEM,
        scratch_shapes=[
            pltpu.VMEM((2, 640, L), F32),
            pltpu.VMEM((2, WIDE, L), F32),
        ],
        compiler_params=pltpu.CompilerParams(vmem_limit_bytes=VMEM_LIMIT),
        cost_estimate=pl.CostEstimate(
            flops=5_000_000_000, bytes_accessed=8_000_000, transcendentals=0
        ),
        name="weights",
    )(place, rows, grads, full, half)


def finish_kernel(place_ref, *refs):
    *r_refs, o_ref, order_ref = refs
    for k in range(8):
        order_ref[jnp.bitwise_xor(place_ref[1], k)] = r_refs[k][...]
    for e in range(8):
        o_ref[:, e, :] = order_ref[e, 0].astype(F32)
        o_ref[:, 8 + e, :] = order_ref[e, 1].astype(F32)
    for p in range(4):
        o_ref[:, 16 + p, :] = order_ref[2 * p, 2].astype(F32) + order_ref[2 * p + 1, 2].astype(F32)


def finish(place, received):
    return pl.pallas_call(
        finish_kernel,
        out_shape=jax.ShapeDtypeStruct((20, 20, L), F32),
        in_specs=[SMEM] + [VMEM] * 8,
        out_specs=VMEM,
        scratch_shapes=[pltpu.VMEM((8, 3, 20, L), BF)],
        name="finish",
    )(place, *received)


def exchange(x, axes):
    return lax.all_to_all(x, axes, split_axis=0, concat_axis=0, tiled=True)


def swap(blocks):
    return [blocks[0]] + [
        lax.ppermute(blocks[k], ENS, [(e, e ^ k) for e in range(8)]) for k in range(1, 8)
    ]


def travel(x):
    moved = exchange(x.reshape(128, 52, 2, 128), EVERY)
    return moved.reshape(16, 8, 104, 128)


def body(fourier, analysis, target, band_ids, partners, band_cotangent):
    place = jnp.stack([lax.axis_index(ORDER), lax.axis_index(ENS), lax.axis_index("dp")])
    place = place.astype(jnp.int32)
    full = jnp.asarray(FULL, BF)
    half = jnp.asarray(HALF, BF)
    by_order = jnp.transpose(analysis, (1, 0, 2))
    native = jnp.transpose(fourier[0].reshape(2, 20, 320, 128), (1, 2, 0, 3)).reshape(20, 640, 128)
    packed = pack(native)
    target_in, packed = lax.optimization_barrier((target[0], packed))
    rows = travel(packed)
    targets = swap(target_blocks(place, target_in, band_ids))
    stacked, observed, grams = spectra(place, by_order, rows, targets, full, half)
    grams = exchange(jnp.broadcast_to(grams, (16, *grams.shape)), ORDER).sum(axis=0)
    grams = exchange(jnp.broadcast_to(grams, (8, *grams.shape)), ENS)
    member_ids = jnp.arange(128, dtype=jnp.int32)
    counts = jnp.sum((partners[:, :, None] == member_ids[None, None, :]).astype(F32), axis=1)
    square = counts[:, :MEMBERS]
    symmetric = jnp.pad(square + square.T, ((0, 0), (0, 128 - MEMBERS)))
    cotangent = lax.dynamic_slice_in_dim(band_cotangent, lax.axis_index("dp"), 1, 0)[0]
    cotangent = jnp.broadcast_to(cotangent[:, None], (NBANDS, 128))
    back, grads, loss = gradient(
        place, by_order, stacked, observed, grams, counts, symmetric, cotangent, full, half
    )
    returned = travel(back)
    weight = weights(place, rows, grads, full, half)
    beside = lax.ppermute(weight[1], "dp", [(0, 1), (1, 0)])
    weight = (weight[0].astype(F32) + beside.astype(F32)).astype(BF)
    grad_analysis = finish(place, swap([weight[k] for k in range(8)]))
    loss_bands = lax.psum(loss[:, 0], "dp")
    native_grad = unpack(returned).reshape(20, 320, 2, 128)
    grad_fourier = jnp.transpose(native_grad, (2, 0, 1, 3)).reshape(1, 2, 20, 40960)
    return (grad_fourier, grad_analysis, loss_bands)


def solution(mesh):
    torus = Mesh(
        mesh.devices.reshape(mesh.shape["dp"], 4, 4, 2, 4),
        ("dp", "order_0", "order_1", "ens_0", "ens_1"),
    )
    in_specs = (
        P("dp", ENS, ORDER, None),
        P(None, ORDER, None),
        P("dp", ENS, ORDER),
        P(ENS, ORDER),
        P(),
        P(),
    )
    out_specs = (P("dp", ENS, ORDER, None), P(DP_ENS, ORDER, None), P())
    return jax.shard_map(body, mesh=torus, in_specs=in_specs, out_specs=out_specs, check_vma=False)
```

```python
import functools

import jax
import jax.numpy as jnp
import numpy as np
from jax import lax
from jax.experimental import pallas as pl
from jax.experimental.pallas import tpu as pltpu
from jax.sharding import Mesh
from jax.sharding import PartitionSpec as P

MEMBERS = 16
NLAT = 320
L = 320
NBANDS = 16
PARTNERS = 4
JJ = MEMBERS + 1
ORDER = ("order_0", "order_1")
ENS = ("ens_0", "ens_1")
DP_ENS = ("dp", "ens_0", "ens_1")
EVERY = ORDER + ENS
EPSILON = 1e-06
WEIGHT_RATIO = 1.0 / 64.0
BF = jnp.bfloat16
F32 = jnp.float32
GROUP = 16
NGROUPS = L // GROUP
WIDE = 384
MIB = 1024 * 1024
VMEM = pl.BlockSpec(memory_space=pltpu.VMEM)
SMEM = pl.BlockSpec(memory_space=pltpu.SMEM)
HBM = pl.BlockSpec(memory_space=pltpu.HBM)


def selections():
    full = np.zeros((NLAT, 640), np.float32)
    half = np.zeros((2, NLAT, WIDE), np.float32)
    for t in range(NLAT):
        full[t, 2 * t : 2 * t + 2] = 1.0
        o, rest = divmod(t, 20)
        h, s = divmod(rest, 10)
        half[h, t, 24 * o + 2 * s : 24 * o + 2 * s + 2] = 1.0
    return full, half


def orderings():
    whole = np.zeros((320, 320), np.float32)
    half = np.zeros((2, 96, 160), np.float32)
    for t in range(20):
        h, s = divmod(t, 10)
        for i in range(2):
            for e in range(8):
                whole[40 * e + 2 * t + i, 16 * t + 2 * e + i] = 1.0
            for p in range(4):
                half[h, 24 * p + 2 * s + i, 8 * t + 2 * p + i] = 1.0
    return whole, half


FULL, HALF = selections()
WHOLE_ORDER, HALF_ORDER = orderings()


def dot(a, b, ca=1, cb=0):
    return lax.dot_general(a, b, (((ca,), (cb,)), ((), ())), preferred_element_type=F32)


def iota(shape, dim):
    return lax.broadcasted_iota(jnp.int32, shape, dim)


def swap_halves(x):
    return pltpu.roll(x, 64, x.ndim - 1)


def split2(x):
    high = x.astype(BF)
    return high, (x - high.astype(F32)).astype(BF)


def split3(x):
    high = x.astype(BF)
    rest = x - high.astype(F32)
    mid = rest.astype(BF)
    return high, mid, (rest - mid.astype(F32)).astype(BF)


def pack_kernel(x_ref, whole_ref, half_ref, o_ref):
    def columns(start, count):
        parts = [x_ref[:, 40 * k + start : 40 * k + start + count, :] for k in range(2)]
        parts = [part.astype(F32).reshape(20 * count, 128).astype(BF) for part in parts]
        return jnp.concatenate(parts, axis=1)

    for slot in range(2):
        moved = halves(dot(whole_ref[...], columns(16 * slot, 16)))
        for k in range(2):
            o_ref[k, :, 40 * slot : 40 * slot + 40, :] = moved[k].reshape(8, 40, 128).astype(BF)
    values = columns(32, 8)
    first = halves(dot(half_ref[0], values))
    second = halves(dot(half_ref[1], values))
    low = iota((96, 128), 1) < 64
    for k in range(2):
        real = jnp.where(low, first[k], swap_halves(second[k])).astype(BF)
        imaginary = jnp.where(low, swap_halves(first[k]), second[k]).astype(BF)
        for p in range(4):
            o_ref[k, 2 * p, 80:104, :] = real[24 * p : 24 * p + 24]
            o_ref[k, 2 * p + 1, 80:104, :] = imaginary[24 * p : 24 * p + 24]


def unpack_kernel(y_ref, whole_ref, half_ref, x_ref):
    for slot in range(2):
        parts = [y_ref[k, :, 40 * slot : 40 * slot + 40, :].astype(F32) for k in range(2)]
        parts = [part.reshape(320, 128).astype(BF) for part in parts]
        moved = halves(dot(whole_ref[...], jnp.concatenate(parts, axis=1)))
        for k in range(2):
            start = 40 * k + 16 * slot
            x_ref[:, start : start + 16, :] = moved[k].reshape(20, 16, 128).astype(BF)
    low = iota((96, 128), 1) < 64
    firsts, seconds = [], []
    for k in range(2):
        real, imaginary = [
            jnp.concatenate([y_ref[k, 2 * p + r, 80:104, :].astype(F32) for p in range(4)], axis=0)
            for r in range(2)
        ]
        firsts.append(jnp.where(low, real, swap_halves(imaginary)).astype(BF))
        seconds.append(jnp.where(low, swap_halves(real), imaginary).astype(BF))
    moved = halves(
        dot(half_ref[0], jnp.concatenate(firsts, axis=1))
        + dot(half_ref[1], jnp.concatenate(seconds, axis=1))
    )
    for k in range(2):
        x_ref[:, 40 * k + 32 : 40 * k + 40, :] = moved[k].reshape(20, 8, 128).astype(BF)


NATIVE = pl.BlockSpec((20, 80, 128), lambda o: (0, o, 0))
PACKED = pl.BlockSpec((2, 8, 104, 128), lambda o: (o, 0, 0, 0))


def constant(shape):
    return pl.BlockSpec(shape, lambda o: (0,) * len(shape))


def pack(x):
    return pl.pallas_call(
        pack_kernel,
        grid=(8,),
        out_shape=jax.ShapeDtypeStruct((16, 8, 104, 128), BF),
        in_specs=[NATIVE, constant((320, 320)), constant((2, 96, 160))],
        out_specs=PACKED,
        name="pack",
    )(x, jnp.asarray(WHOLE_ORDER, BF), jnp.asarray(HALF_ORDER, BF))


def unpack(y):
    return pl.pallas_call(
        unpack_kernel,
        grid=(8,),
        out_shape=jax.ShapeDtypeStruct((20, 640, 128), BF),
        in_specs=[PACKED, constant((320, 320)), constant((2, 160, 96))],
        out_specs=NATIVE,
        name="unpack",
    )(y, jnp.asarray(WHOLE_ORDER.T, BF), jnp.asarray(HALF_ORDER.transpose(0, 2, 1), BF))


def target_kernel(place_ref, t_ref, band_ref, *refs):
    *o_refs, held_ref, sem = refs
    bands = jnp.broadcast_to(band_ref[:, 0:1].astype(F32), (40, 128))
    low = iota((40, 128), 1) < 64
    for k in range(8):
        e = jnp.bitwise_xor(place_ref[1], k)

        def lanes(start):
            return t_ref[:, pl.ds(pl.multiple_of(start, 128), 128)]

        middle = lanes(2048 + 128 * (e // 2)).astype(F32)
        held_ref[k, :, 0:128] = lanes(128 * e)
        held_ref[k, :, 128:256] = lanes(1024 + 128 * e)
        odd = jnp.broadcast_to(e % 2, (40, 128)) == 1
        part = jnp.where(odd, swap_halves(middle), middle)
        held_ref[k, :, 256:384] = jnp.where(low, part, bands).astype(BF)
    copies = [pltpu.make_async_copy(held_ref.at[k], o_refs[k], sem.at[k]) for k in range(8)]
    for copy in copies:
        copy.start()
    for copy in copies:
        copy.wait()


def target_blocks(place, target, bands):
    return pl.pallas_call(
        target_kernel,
        out_shape=[jax.ShapeDtypeStruct((40, WIDE), BF)] * 8,
        in_specs=[SMEM, VMEM, VMEM],
        out_specs=[HBM] * 8,
        scratch_shapes=[pltpu.VMEM((8, 40, WIDE), BF), pltpu.SemaphoreType.DMA((8,))],
        compiler_params=pltpu.CompilerParams(vmem_limit_bytes=63 * MIB),
        name="target_blocks",
    )(place, target, bands)


def own_orders(place_ref):
    ens = place_ref[1]
    return ens, 8 + ens, 16 + ens // 2


def fetches(place_ref, analysis_ref, own_ref, sem):
    return [
        pltpu.make_async_copy(analysis_ref.at[m], own_ref.at[k], sem.at[k])
        for k, m in enumerate(own_orders(place_ref))
    ]


def halves(x):
    return [x[:, 128 * k : 128 * k + 128] for k in range(2)]


STARTS = (0, 40, 80)
COUNTS = (40, 40, 24)


def two_rows_of(rows_ref, g, slot):
    start, count = STARTS[slot], COUNTS[slot]
    parts = [
        rows_ref[:, 2 * g + k, start : start + count, :]
        .astype(F32)
        .reshape(16 * count, 128)
        .astype(BF)
        for k in range(2)
    ]
    return jnp.concatenate(parts, axis=1)


def band_column(target_ref, start, count):
    return target_ref[pl.ds(start, count), 256:384].astype(F32)[:, 64:65]


def prepare_kernel(
    place_ref, analysis_ref, full_ref, half_ref, other_row_ref, other_column_ref,
    to_full_ref, to_half_ref, from_full_ref, from_half_ref, select_ref, to_mixing_ref, own_ref, sem,
):
    copies = fetches(place_ref, analysis_ref, own_ref, sem)
    for copy in copies:
        copy.start()
    def is_at(a, b):
        n = (a >= 7).astype(jnp.int32) + (a >= 14).astype(jnp.int32)
        return (iota((WIDE, 128), 0) == 128 * n + JJ * (a - 7 * n) + b).astype(F32)

    lane = iota((WIDE, 128), 1)
    who = lane & 15
    other = jnp.broadcast_to(other_row_ref[0:1, :], (WIDE, 128))
    select = is_at(who, who) + is_at(other, other) - 2.0 * is_at(who, other)
    select_ref[...] = jnp.where(lane < 80, select, 0.0).astype(BF)
    row, j = iota((128, 128), 0), iota((128, 128), 1)
    who, other = row & 15, other_column_ref[...]
    pair = (row >= 16) & (row < 80)
    for i in range(MEMBERS):
        own = (j == i).astype(F32)
        value = jnp.where(pair & (who == i), (other == j).astype(F32) - own, 0.0)
        value = value + jnp.where(pair & (other == i), (who == j).astype(F32) - own, 0.0)
        value = value + jnp.where((row < 16) & (who == i), own, 0.0)
        to_mixing_ref[:, 128 * i : 128 * i + 128] = value.astype(BF)
    for copy in copies:
        copy.wait()
    for n in range(4):
        choose = full_ref[...] if n < 2 else half_ref[n - 2]
        own = own_ref[min(n, 2)]
        to_ref = to_full_ref.at[n] if n < 2 else to_half_ref.at[n - 2]
        from_ref = from_full_ref.at[n] if n < 2 else from_half_ref.at[n - 2]
        spread = dot(own, choose, 0, 0)
        member = iota(spread.shape, 1) % 2
        for i in range(2):
            to_ref[i] = jnp.where(member == i, spread, 0.0).astype(BF)
        spread = dot(choose, own, 0, 0)
        member = iota(spread.shape, 0) % 2
        for i in range(2):
            from_ref[i] = jnp.where(member == i, spread, 0.0).astype(BF)


def prepare(place, analysis, full, half, partners):
    other = jnp.concatenate(
        [jnp.full((16,), MEMBERS, jnp.int32), partners.T.reshape(64), jnp.zeros((48,), jnp.int32)]
    )
    return pl.pallas_call(
        prepare_kernel,
        out_shape=[
            jax.ShapeDtypeStruct((2, 2, L, 640), BF),
            jax.ShapeDtypeStruct((2, 2, L, WIDE), BF),
            jax.ShapeDtypeStruct((2, 2, 640, L), BF),
            jax.ShapeDtypeStruct((2, 2, WIDE, L), BF),
            jax.ShapeDtypeStruct((WIDE, 128), BF),
            jax.ShapeDtypeStruct((128, MEMBERS * 128), BF),
        ],
        in_specs=[SMEM, HBM, VMEM, VMEM, VMEM, VMEM],
        out_specs=[VMEM] * 6,
        scratch_shapes=[pltpu.VMEM((3, NLAT, L), BF), pltpu.SemaphoreType.DMA((3,))],
        compiler_params=pltpu.CompilerParams(vmem_limit_bytes=63 * MIB),
        name="prepare",
    )(
        place, analysis, full, half,
        jnp.broadcast_to(other[None], (8, 128)), jnp.broadcast_to(other[:, None], (128, 128)),
    )


def compact(x):
    top, rest = x[:8], x[8:]
    lane = iota((8, 128), 1)
    first = jnp.where(lane < 80, top, pltpu.roll(rest, 80, 1))
    left = pltpu.roll(rest, 80, 1)
    lane = iota((1, 128), 1)
    tails = []
    for n in range(2):
        tail = jnp.zeros((1, 128), F32)
        for r in range(4):
            row = pltpu.roll(left[4 * n + r : 4 * n + r + 1], 32 * r, 1)
            tail = jnp.where((lane >= 32 * r) & (lane < 32 * r + 32), row, tail)
        tails.append(tail)
    return jnp.concatenate([first] + tails, axis=0)


def expand(x):
    first = x[:8]
    lane = iota((8, 128), 1)
    top = jnp.where(lane < 80, first, 0.0)
    rows = []
    for n in range(2):
        for r in range(4):
            rows.append(pltpu.roll(x[8 + n : 9 + n], (48 - 32 * r) % 128, 1))
    rest = jnp.where(lane < 48, pltpu.roll(first, 48, 1), jnp.concatenate(rows, axis=0))
    return jnp.concatenate([top, jnp.where(lane < 80, rest, 0.0)], axis=0)


def spectra_kernel(place_ref, rows_hbm, to_full_hbm, to_half_hbm, select_hbm, *refs):
    target_refs = refs[:8]
    stacked_hbm, target_hbm, sums_hbm = refs[8:11]
    to_full_ref, to_half_ref, select_ref, stacked_ref, target_ref, sums_ref = refs[11:17]
    rows_ref, terms_ref, order_ref, in_sem, rows_sem, target_sem, out_sem = refs[17:]

    def load_rows(g):
        where = pl.ds(2 * g, 2)
        return pltpu.make_async_copy(rows_hbm.at[:, where], rows_ref.at[:, where], rows_sem.at[g])

    load_rows(0).start()
    loads = [pltpu.make_async_copy(to_full_hbm, to_full_ref, in_sem.at[0])]
    loads.append(pltpu.make_async_copy(to_half_hbm, to_half_ref, in_sem.at[1]))
    loads.append(pltpu.make_async_copy(select_hbm, select_ref, in_sem.at[2]))
    for k in range(8):
        there = order_ref.at[jnp.bitwise_xor(place_ref[1], k)]
        loads.append(pltpu.make_async_copy(target_refs[k], there, target_sem.at[k]))
    for copy in loads[:2]:
        copy.start()
    for g in range(1, 4):
        load_rows(g).start()
    for copy in loads[2:]:
        copy.start()
    for copy in loads[:2]:
        copy.wait()
    base = place_ref[0] * 20
    orders = [base + m for m in own_orders(place_ref)]
    degree = iota((L, 128), 0)
    low = iota((L, 128), 1) < 64
    keeps = [degree >= orders[0], degree >= orders[1], (degree >= orders[2]) & low]

    def transform(g, carry):
        load_rows(g).wait()
        for slot in range(3):
            values = two_rows_of(rows_ref, g, slot)
            for i in range(2):
                if slot < 2:
                    parts = halves(dot(to_full_ref[slot, i], values))
                else:
                    parts = halves(dot(to_half_ref[0, i], values))
                    other = halves(dot(to_half_ref[1, i], values))
                    parts = [parts[k] + swap_halves(other[k]) for k in range(2)]
                for k in range(2):
                    stacked_ref[4 * g + 2 * k + i, :, 128 * slot : 128 * slot + 128] = jnp.where(
                        keeps[slot], parts[k], 0.0
                    ).astype(BF)
        store(g).start()
        return carry

    def store(g):
        where = pl.ds(4 * g, 4)
        return pltpu.make_async_copy(stacked_ref.at[where], stacked_hbm.at[where], out_sem.at[g])

    lax.fori_loop(0, 4, transform, 0)
    for copy in loads[2:]:
        copy.wait()
    target_ref[...] = order_ref[...].astype(F32).reshape(L, WIDE).astype(BF)
    stores = [pltpu.make_async_copy(target_ref, target_hbm, out_sem.at[4])]
    for slot in range(3):
        lanes = slice(128 * slot, 128 * slot + 128)
        observed = jnp.where(keeps[slot], target_ref[:, lanes].astype(F32), 0.0)
        stacked_ref[MEMBERS, :, lanes] = observed.astype(BF)
    last = stacked_hbm.at[MEMBERS]
    stores.append(pltpu.make_async_copy(stacked_ref.at[MEMBERS], last, out_sem.at[5]))
    for copy in stores:
        copy.start()

    size = MEMBERS * GROUP
    same = (iota((size, size), 0) & 15) == (iota((size, size), 1) & 15)
    gather = ((iota((size, 128), 0) >> 4) == iota((size, 128), 1)).astype(F32).astype(BF)
    at_observed = iota((size, 128), 1) == MEMBERS

    def gram(g, carry):
        start = pl.multiple_of(g * GROUP, GROUP)
        block = stacked_ref[0:MEMBERS, pl.ds(start, GROUP), :].reshape(size, WIDE)
        own = stacked_ref[MEMBERS, pl.ds(start, GROUP), :].astype(F32)
        products = jnp.where(same, dot(block, block, 1, 1), 0.0)
        high, mid, low_part = split3(products)
        sums = dot(high, gather) + dot(mid, gather) + dot(low_part, gather)
        beside = jnp.concatenate([own] * MEMBERS, axis=0) * block.astype(F32)
        sums = jnp.where(at_observed, jnp.sum(beside, axis=1, keepdims=True), sums)
        last = jnp.sum(own * own, axis=1, keepdims=True)
        pieces = [sums[GROUP * i : GROUP * i + GROUP] for i in range(MEMBERS)]
        pieces.append(jnp.where(at_observed[:GROUP], last, 0.0))
        for n in range(3):
            total = pieces[7 * n]
            for i in range(7 * n + 1, min(7 * n + 7, JJ)):
                total = total + pltpu.roll(pieces[i], JJ * (i % 7), 1)
            terms_ref[n, pl.ds(start, GROUP), :] = total
        return carry

    lax.fori_loop(0, NGROUPS, gram, 0, unroll=4)

    column = jnp.broadcast_to(band_column(target_ref, 0, L), (L, 128))
    one_hot = (column == iota((L, 128), 1).astype(F32)).astype(F32).astype(BF)
    squares = jnp.zeros((NBANDS, 128), F32)
    for n in range(3):
        total = sum(dot(one_hot, part, 0, 0) for part in split3(terms_ref[n]))[:NBANDS]
        for part in split3(total):
            squares = squares + dot(part, select_ref[128 * n : 128 * n + 128, :])
    sums = compact(squares)
    sums = jnp.concatenate([sums] * 4, axis=0)
    sums_ref[...] = jnp.broadcast_to(sums[None], (32, 40, 128))
    stores.append(pltpu.make_async_copy(sums_ref, sums_hbm, out_sem.at[6]))
    stores[2].start()
    for copy in stores:
        copy.wait()
    for g in range(4):
        store(g).wait()


def spectra(place, rows, to_full, to_half, select, targets):
    return pl.pallas_call(
        spectra_kernel,
        out_shape=[
            jax.ShapeDtypeStruct((JJ, L, WIDE), BF),
            jax.ShapeDtypeStruct((L, WIDE), BF),
            jax.ShapeDtypeStruct((32, 40, 128), F32),
        ],
        in_specs=[SMEM] + [HBM] * 12,
        out_specs=[HBM] * 3,
        scratch_shapes=[
            pltpu.VMEM((2, 2, L, 640), BF),
            pltpu.VMEM((2, 2, L, WIDE), BF),
            pltpu.VMEM((WIDE, 128), BF),
            pltpu.VMEM((JJ, L, WIDE), BF),
            pltpu.VMEM((L, WIDE), BF),
            pltpu.VMEM((32, 40, 128), F32),
            pltpu.VMEM((16, 8, 104, 128), BF),
            pltpu.VMEM((3, L, 128), F32),
            pltpu.VMEM((8, 40, WIDE), BF),
            pltpu.SemaphoreType.DMA((3,)),
            pltpu.SemaphoreType.DMA((4,)),
            pltpu.SemaphoreType.DMA((8,)),
            pltpu.SemaphoreType.DMA((7,)),
        ],
        compiler_params=pltpu.CompilerParams(vmem_limit_bytes=60 * MIB),
        cost_estimate=pl.CostEstimate(
            flops=10_000_000_000, bytes_accessed=12_000_000, transcendentals=0
        ),
        name="spectra",
    )(place, rows, to_full, to_half, select, *targets)


def gradient_kernel(
    stacked_hbm, target_hbm, sums_ref, cotangent_ref, share_ref, to_mixing_hbm,
    from_full_hbm, from_half_hbm,
    back_ref, grad_hbm, loss_ref,
    stacked_ref, target_ref, to_mixing_ref, from_full_ref, from_half_ref, grad_ref,
    held_ref, in_sem, sem,
):
    loads = [
        pltpu.make_async_copy(there, here, in_sem.at[n])
        for n, (there, here) in enumerate(
            (
                (to_mixing_hbm, to_mixing_ref),
                (target_hbm, target_ref),
                (stacked_hbm, stacked_ref),
                (from_full_hbm, from_full_ref),
                (from_half_hbm, from_half_ref),
            )
        )
    ]
    for copy in loads:
        copy.start()
    sums = jnp.sum(sums_ref[...], axis=0)
    sums = sum(sums[10 * n : 10 * n + 10] for n in range(4))
    lane = iota((NBANDS, 128), 1)
    distance = jnp.sqrt(jnp.maximum(expand(sums), 0.0) + EPSILON)
    cotangent = cotangent_ref[...]
    share = share_ref[0:1, :]
    score = jnp.sum(distance * share, axis=1, keepdims=True)
    loss_ref[...] = score * cotangent
    weight = cotangent * (16.0 * MEMBERS * NLAT) * jnp.abs(share) / distance
    beside = jnp.where(lane < MEMBERS, -weight, 0.0)
    loads[0].wait()
    mixing = sum(dot(part, to_mixing_ref[...]) for part in split3(weight))
    mixing = [mixing[:, 128 * i : 128 * i + 128] for i in range(MEMBERS)]

    size = MEMBERS * GROUP
    widen = (iota((128, size), 0) == (iota((128, size), 1) >> 4)).astype(F32).astype(BF)
    mix_high, mix_low = split2(jnp.concatenate(mixing, axis=0))
    mix_high = dot(mix_high, widen).astype(BF)
    mix_low = dot(mix_low, widen).astype(BF)
    beside = jnp.concatenate([beside, jnp.zeros((128 - NBANDS, 128), F32)], axis=0)
    beside_high, beside_low = split2(beside)
    same_member = (iota((size, size), 0) >> 4) == (iota((size, size), 1) >> 4)
    band_of_column = (iota((size, size), 1) & 15).astype(F32)
    same_degree = (iota((size, size), 0) & 15) == (iota((size, size), 1) & 15)
    band_of_lane = iota((GROUP, 128), 1).astype(F32)

    def mix(g, carry):
        start = pl.multiple_of(g * GROUP, GROUP)
        bands = band_column(target_ref, start, GROUP)
        column = jnp.concatenate([jnp.broadcast_to(bands, (GROUP, size))] * MEMBERS, axis=0)
        pick = (same_member & (column == band_of_column)).astype(F32).astype(BF)
        high = jnp.where(same_degree, dot(pick, mix_high), 0.0).astype(BF)
        low = jnp.where(same_degree, dot(pick, mix_low), 0.0).astype(BF)
        one_hot = (jnp.broadcast_to(bands, (GROUP, 128)) == band_of_lane).astype(F32).astype(BF)
        weights = dot(one_hot, beside_high) + dot(one_hot, beside_low)
        weights = jnp.concatenate(
            [jnp.broadcast_to(weights[:, i : i + 1], (GROUP, 128)) for i in range(MEMBERS)], axis=0
        )
        block = stacked_ref[0:MEMBERS, pl.ds(start, GROUP), :].reshape(size, WIDE)
        own = stacked_ref[MEMBERS, pl.ds(start, GROUP), :].astype(F32)
        grad = dot(high, block) + dot(low, block)
        for slot in range(3):
            lanes = slice(128 * slot, 128 * slot + 128)
            part = grad[:, lanes] + weights * jnp.concatenate([own[:, lanes]] * MEMBERS, axis=0)
            grad_ref[:, pl.ds(start, GROUP), lanes] = part.astype(BF).reshape(MEMBERS, GROUP, 128)
        return carry

    loads[1].wait()
    loads[2].wait()
    lax.fori_loop(0, NGROUPS, mix, 0, unroll=2)
    kept = pltpu.make_async_copy(grad_ref, grad_hbm, sem.at[4])
    kept.start()
    loads[3].wait()
    loads[4].wait()
    def inverse(g, carry):
        for slot in range(3):
            grads = [jnp.concatenate(grads_of(grad_ref, g, i, slot), axis=1) for i in range(2)]
            from_ref = from_full_ref.at[slot] if slot < 2 else from_half_ref.at[0]
            parts = halves(dot(from_ref[0], grads[0]) + dot(from_ref[1], grads[1]))
            if slot == 2:
                from_ref = from_half_ref.at[1]
                other = halves(dot(from_ref[0], grads[0]) + dot(from_ref[1], grads[1]))
                parts = [parts[k] + swap_halves(other[k]) for k in range(2)]
            start, count = STARTS[slot], COUNTS[slot]
            for k in range(2):
                part = parts[k].reshape(16, count, 128).astype(BF)
                held_ref[:, 2 * g + k, start : start + count, :] = part
        send(g).start()
        return carry

    def send(g):
        where = pl.ds(2 * g, 2)
        return pltpu.make_async_copy(held_ref.at[:, where], back_ref.at[:, where], sem.at[g])

    lax.fori_loop(0, 4, inverse, 0)
    for g in range(4):
        send(g).wait()
    kept.wait()


def grads_of(grad_ref, g, i, slot):
    lanes = slice(128 * slot, 128 * slot + 128)
    return [grad_ref[4 * g + 2 * k + i, :, lanes] for k in range(2)]


def gradient(stacked, target, sums, cotangent, share, to_mixing, from_full, from_half):
    return pl.pallas_call(
        gradient_kernel,
        out_shape=[
            jax.ShapeDtypeStruct((16, 8, 104, 128), BF),
            jax.ShapeDtypeStruct((MEMBERS, L, WIDE), BF),
            jax.ShapeDtypeStruct((NBANDS, 128), F32),
        ],
        in_specs=[HBM, HBM, VMEM, VMEM, VMEM, HBM, HBM, HBM],
        out_specs=[HBM, HBM, VMEM],
        scratch_shapes=[
            pltpu.VMEM((JJ, L, WIDE), BF),
            pltpu.VMEM((L, WIDE), BF),
            pltpu.VMEM((128, MEMBERS * 128), BF),
            pltpu.VMEM((2, 2, 640, L), BF),
            pltpu.VMEM((2, 2, WIDE, L), BF),
            pltpu.VMEM((MEMBERS, L, WIDE), BF),
            pltpu.VMEM((16, 8, 104, 128), BF),
            pltpu.SemaphoreType.DMA((5,)),
            pltpu.SemaphoreType.DMA((5,)),
        ],
        compiler_params=pltpu.CompilerParams(vmem_limit_bytes=63 * MIB),
        cost_estimate=pl.CostEstimate(
            flops=10_000_000_000, bytes_accessed=12_000_000, transcendentals=0
        ),
        name="gradient",
    )(stacked, target, sums, cotangent, share, to_mixing, from_full, from_half)


def weight_kernel(
    place_ref, rows_ref, grad_ref, full_ref, half_ref, weight_ref, full_sum_ref, half_sum_ref
):
    full_sum_ref[...] = jnp.zeros_like(full_sum_ref)
    half_sum_ref[...] = jnp.zeros_like(half_sum_ref)

    def step(g, carry):
        for slot in range(3):
            values = two_rows_of(rows_ref, g, slot)
            member = iota((values.shape[0], L), 0) % 2
            sides = [[grads_of(grad_ref, g, i, slot) for i in range(2)]]
            if slot == 2:
                sides.append(
                    [[swap_halves(x.astype(F32)).astype(BF) for x in pair] for pair in sides[0]]
                )
            for h, side in enumerate(sides):
                grads = [jnp.concatenate(side[i], axis=1) for i in range(2)]
                terms = jnp.where(
                    member == 0, dot(values, grads[0], 1, 1), dot(values, grads[1], 1, 1)
                )
                if slot < 2:
                    full_sum_ref[slot] += terms
                else:
                    half_sum_ref[h] += terms
        return carry

    lax.fori_loop(0, 4, step, 0)
    for slot in range(3):
        if slot < 2:
            parts = split2(full_sum_ref[slot])
            weight = dot(full_ref[...], parts[0]) + dot(full_ref[...], parts[1])
        else:
            weight = jnp.zeros((NLAT, L), F32)
            for h in range(2):
                parts = split2(half_sum_ref[h])
                weight = weight + dot(half_ref[h], parts[0]) + dot(half_ref[h], parts[1])
        weight = weight * WEIGHT_RATIO
        for c in range(16):
            other = jnp.bitwise_xor(place_ref[2], c // 8)
            step_to = jnp.bitwise_xor(place_ref[1], c % 8)
            weight_ref[other, step_to, slot] = weight[20 * c : 20 * c + 20].astype(BF)


def weights(place, rows, grads, full, half):
    return pl.pallas_call(
        weight_kernel,
        out_shape=jax.ShapeDtypeStruct((2, 8, 3, 20, L), BF),
        in_specs=[SMEM] + [VMEM] * 4,
        out_specs=VMEM,
        scratch_shapes=[
            pltpu.VMEM((2, 640, L), F32),
            pltpu.VMEM((2, WIDE, L), F32),
        ],
        compiler_params=pltpu.CompilerParams(vmem_limit_bytes=63 * MIB),
        cost_estimate=pl.CostEstimate(
            flops=5_000_000_000, bytes_accessed=8_000_000, transcendentals=0
        ),
        name="weights",
    )(place, rows, grads, full, half)


def finish_kernel(place_ref, *refs):
    *r_refs, o_ref, order_ref = refs
    for k in range(8):
        order_ref[jnp.bitwise_xor(place_ref[1], k)] = r_refs[k][...]
    for e in range(8):
        o_ref[:, e, :] = order_ref[e, 0].astype(F32)
        o_ref[:, 8 + e, :] = order_ref[e, 1].astype(F32)
    for p in range(4):
        o_ref[:, 16 + p, :] = order_ref[2 * p, 2].astype(F32) + order_ref[2 * p + 1, 2].astype(F32)


def finish(place, received):
    return pl.pallas_call(
        finish_kernel,
        out_shape=jax.ShapeDtypeStruct((20, 20, L), F32),
        in_specs=[SMEM] + [VMEM] * 8,
        out_specs=VMEM,
        scratch_shapes=[pltpu.VMEM((8, 3, 20, L), BF)],
        name="finish",
    )(place, *received)


def exchange(x, axes):
    return lax.all_to_all(x, axes, split_axis=0, concat_axis=0, tiled=True)


def swap(blocks):
    return [blocks[0]] + [
        lax.ppermute(blocks[k], ENS, [(e, e ^ k) for e in range(8)]) for k in range(1, 8)
    ]


def travel(x):
    moved = exchange(x.reshape(128, 52, 2, 128), EVERY)
    return moved.reshape(16, 8, 104, 128)


def body(fourier, analysis, target, band_ids, partners, band_cotangent):
    place = jnp.stack([lax.axis_index(ORDER), lax.axis_index(ENS), lax.axis_index("dp")])
    place = place.astype(jnp.int32)
    full = jnp.asarray(FULL, BF)
    half = jnp.asarray(HALF, BF)
    by_order = jnp.transpose(analysis, (1, 0, 2))
    native = jnp.transpose(fourier[0].reshape(2, 20, 320, 128), (1, 2, 0, 3)).reshape(20, 640, 128)
    packed = pack(native)
    target_in, partners, full, place, packed = lax.optimization_barrier(
        (target[0], partners, full, place, packed)
    )
    rows = travel(packed)
    targets = swap(target_blocks(place, target_in, band_ids))
    to_full, to_half, from_full, from_half, select, to_mixing = prepare(
        place, by_order, full, half, partners
    )
    cotangent = lax.dynamic_slice_in_dim(band_cotangent, lax.axis_index("dp"), 1, 0)[0]
    cotangent = jnp.broadcast_to(cotangent[:, None], (NBANDS, 128))
    share = np.zeros((8, 128), np.float32)
    share[:, :16] = 1.0 / MEMBERS
    share[:, 16:80] = -1.0 / (2.0 * MEMBERS * PARTNERS)
    stacked, observed, sums = spectra(place, rows, to_full, to_half, select, targets)
    sums = exchange(sums.reshape(128, 5, 2, 128), EVERY).reshape(32, 40, 128)
    back, grads, loss = gradient(
        stacked, observed, sums, cotangent, jnp.asarray(share), to_mixing, from_full, from_half
    )
    returned = travel(back)
    loss = loss[:, 0]
    loss_bands = loss + lax.ppermute(loss, "dp", [(0, 1), (1, 0)])
    weight = weights(place, rows, grads, full, half)
    beside = lax.ppermute(weight[1], "dp", [(0, 1), (1, 0)])
    weight = (weight[0].astype(F32) + beside.astype(F32)).astype(BF)
    grad_analysis = finish(place, swap([weight[k] for k in range(8)]))
    native_grad = unpack(returned).reshape(20, 320, 2, 128)
    grad_fourier = jnp.transpose(native_grad, (2, 0, 1, 3)).reshape(1, 2, 20, 40960)
    return (grad_fourier, grad_analysis, loss_bands)


def solution(mesh):
    torus = Mesh(
        mesh.devices.reshape(mesh.shape["dp"], 4, 4, 2, 4),
        ("dp", "order_0", "order_1", "ens_0", "ens_1"),
    )
    in_specs = (
        P("dp", ENS, ORDER, None),
        P(None, ORDER, None),
        P("dp", ENS, ORDER),
        P(ENS, ORDER),
        P(),
        P(),
    )
    out_specs = (P("dp", ENS, ORDER, None), P(DP_ENS, ORDER, None), P())
    return jax.shard_map(body, mesh=torus, in_specs=in_specs, out_specs=out_specs, check_vma=False)
```

```python
import functools

import jax
import jax.numpy as jnp
import numpy as np
from jax import lax
from jax.experimental import pallas as pl
from jax.experimental.pallas import tpu as pltpu
from jax.sharding import Mesh
from jax.sharding import PartitionSpec as P

MEMBERS = 16
NLAT = 320
L = 320
NBANDS = 16
PARTNERS = 4
JJ = MEMBERS + 1
ORDER = ("order_0", "order_1")
ENS = ("ens_0", "ens_1")
DP_ENS = ("dp", "ens_0", "ens_1")
EVERY = ORDER + ENS
EPSILON = 1e-06
WEIGHT_RATIO = 1.0 / 64.0
BF = jnp.bfloat16
F32 = jnp.float32
GROUP = 16
NGROUPS = L // GROUP
WIDE = 384
MIB = 1024 * 1024
VMEM = pl.BlockSpec(memory_space=pltpu.VMEM)
SMEM = pl.BlockSpec(memory_space=pltpu.SMEM)
HBM = pl.BlockSpec(memory_space=pltpu.HBM)


def selections():
    full = np.zeros((NLAT, 640), np.float32)
    half = np.zeros((2, NLAT, WIDE), np.float32)
    for t in range(NLAT):
        full[t, 2 * t : 2 * t + 2] = 1.0
        o, rest = divmod(t, 20)
        h, s = divmod(rest, 10)
        half[h, t, 24 * o + 2 * s : 24 * o + 2 * s + 2] = 1.0
    return full, half


def orderings():
    whole = np.zeros((320, 320), np.float32)
    half = np.zeros((2, 96, 160), np.float32)
    for t in range(20):
        h, s = divmod(t, 10)
        for i in range(2):
            for e in range(8):
                whole[40 * e + 2 * t + i, 16 * t + 2 * e + i] = 1.0
            for p in range(4):
                half[h, 24 * p + 2 * s + i, 8 * t + 2 * p + i] = 1.0
    return whole, half


FULL, HALF = selections()
WHOLE_ORDER, HALF_ORDER = orderings()


def dot(a, b, ca=1, cb=0):
    return lax.dot_general(a, b, (((ca,), (cb,)), ((), ())), preferred_element_type=F32)


def iota(shape, dim):
    return lax.broadcasted_iota(jnp.int32, shape, dim)


def swap_halves(x):
    return pltpu.roll(x, 64, x.ndim - 1)


def split2(x):
    high = x.astype(BF)
    return high, (x - high.astype(F32)).astype(BF)


def split3(x):
    high = x.astype(BF)
    rest = x - high.astype(F32)
    mid = rest.astype(BF)
    return high, mid, (rest - mid.astype(F32)).astype(BF)


def pack_kernel(x_ref, whole_ref, half_ref, o_ref):
    def columns(start, count):
        parts = [x_ref[:, 40 * k + start : 40 * k + start + count, :] for k in range(2)]
        parts = [part.astype(F32).reshape(20 * count, 128).astype(BF) for part in parts]
        return jnp.concatenate(parts, axis=1)

    for slot in range(2):
        moved = halves(dot(whole_ref[...], columns(16 * slot, 16)))
        for k in range(2):
            o_ref[k, :, 40 * slot : 40 * slot + 40, :] = moved[k].reshape(8, 40, 128).astype(BF)
    values = columns(32, 8)
    first = halves(dot(half_ref[0], values))
    second = halves(dot(half_ref[1], values))
    low = iota((96, 128), 1) < 64
    for k in range(2):
        real = jnp.where(low, first[k], swap_halves(second[k])).astype(BF)
        imaginary = jnp.where(low, swap_halves(first[k]), second[k]).astype(BF)
        for p in range(4):
            o_ref[k, 2 * p, 80:104, :] = real[24 * p : 24 * p + 24]
            o_ref[k, 2 * p + 1, 80:104, :] = imaginary[24 * p : 24 * p + 24]


def unpack_kernel(y_ref, whole_ref, half_ref, x_ref):
    for slot in range(2):
        parts = [y_ref[k, :, 40 * slot : 40 * slot + 40, :].astype(F32) for k in range(2)]
        parts = [part.reshape(320, 128).astype(BF) for part in parts]
        moved = halves(dot(whole_ref[...], jnp.concatenate(parts, axis=1)))
        for k in range(2):
            start = 40 * k + 16 * slot
            x_ref[:, start : start + 16, :] = moved[k].reshape(20, 16, 128).astype(BF)
    low = iota((96, 128), 1) < 64
    firsts, seconds = [], []
    for k in range(2):
        real, imaginary = [
            jnp.concatenate([y_ref[k, 2 * p + r, 80:104, :].astype(F32) for p in range(4)], axis=0)
            for r in range(2)
        ]
        firsts.append(jnp.where(low, real, swap_halves(imaginary)).astype(BF))
        seconds.append(jnp.where(low, swap_halves(real), imaginary).astype(BF))
    moved = halves(
        dot(half_ref[0], jnp.concatenate(firsts, axis=1))
        + dot(half_ref[1], jnp.concatenate(seconds, axis=1))
    )
    for k in range(2):
        x_ref[:, 40 * k + 32 : 40 * k + 40, :] = moved[k].reshape(20, 8, 128).astype(BF)


NATIVE = pl.BlockSpec((20, 80, 128), lambda o: (0, o, 0))
PACKED = pl.BlockSpec((2, 8, 104, 128), lambda o: (o, 0, 0, 0))


def constant(shape):
    return pl.BlockSpec(shape, lambda o: (0,) * len(shape))


def pack(x):
    return pl.pallas_call(
        pack_kernel,
        grid=(8,),
        out_shape=jax.ShapeDtypeStruct((16, 8, 104, 128), BF),
        in_specs=[NATIVE, constant((320, 320)), constant((2, 96, 160))],
        out_specs=PACKED,
        name="pack",
    )(x, jnp.asarray(WHOLE_ORDER, BF), jnp.asarray(HALF_ORDER, BF))


def unpack(y):
    return pl.pallas_call(
        unpack_kernel,
        grid=(8,),
        out_shape=jax.ShapeDtypeStruct((20, 640, 128), BF),
        in_specs=[PACKED, constant((320, 320)), constant((2, 160, 96))],
        out_specs=NATIVE,
        name="unpack",
    )(y, jnp.asarray(WHOLE_ORDER.T, BF), jnp.asarray(HALF_ORDER.transpose(0, 2, 1), BF))


def target_kernel(place_ref, t_ref, band_ref, *refs):
    *o_refs, held_ref, sem = refs
    bands = jnp.broadcast_to(band_ref[:, 0:1].astype(F32), (40, 128))
    low = iota((40, 128), 1) < 64
    for k in range(8):
        e = jnp.bitwise_xor(place_ref[1], k)

        def lanes(start):
            return t_ref[:, pl.ds(pl.multiple_of(start, 128), 128)]

        middle = lanes(2048 + 128 * (e // 2)).astype(F32)
        held_ref[k, :, 0:128] = lanes(128 * e)
        held_ref[k, :, 128:256] = lanes(1024 + 128 * e)
        odd = jnp.broadcast_to(e % 2, (40, 128)) == 1
        part = jnp.where(odd, swap_halves(middle), middle)
        held_ref[k, :, 256:384] = jnp.where(low, part, bands).astype(BF)
    copies = [pltpu.make_async_copy(held_ref.at[k], o_refs[k], sem.at[k]) for k in range(8)]
    for copy in copies:
        copy.start()
    for copy in copies:
        copy.wait()


def target_blocks(place, target, bands):
    return pl.pallas_call(
        target_kernel,
        out_shape=[jax.ShapeDtypeStruct((40, WIDE), BF)] * 8,
        in_specs=[SMEM, VMEM, VMEM],
        out_specs=[HBM] * 8,
        scratch_shapes=[pltpu.VMEM((8, 40, WIDE), BF), pltpu.SemaphoreType.DMA((8,))],
        compiler_params=pltpu.CompilerParams(vmem_limit_bytes=63 * MIB),
        name="target_blocks",
    )(place, target, bands)


def own_orders(place_ref):
    ens = place_ref[1]
    return ens, 8 + ens, 16 + ens // 2


def fetches(place_ref, analysis_ref, own_ref, sem):
    return [
        pltpu.make_async_copy(analysis_ref.at[m], own_ref.at[k], sem.at[k])
        for k, m in enumerate(own_orders(place_ref))
    ]


def halves(x):
    return [x[:, 128 * k : 128 * k + 128] for k in range(2)]


STARTS = (0, 40, 80)
COUNTS = (40, 40, 24)


def two_rows_of(rows_ref, g, slot):
    start, count = STARTS[slot], COUNTS[slot]
    parts = [
        rows_ref[:, 2 * g + k, start : start + count, :]
        .astype(F32)
        .reshape(16 * count, 128)
        .astype(BF)
        for k in range(2)
    ]
    return jnp.concatenate(parts, axis=1)


def band_column(target_ref, start, count):
    return target_ref[pl.ds(start, count), 256:384].astype(F32)[:, 64:65]


def prepare_kernel(
    place_ref, analysis_ref, full_ref, half_ref, other_column_ref,
    to_full_ref, to_half_ref, from_full_ref, from_half_ref, to_mixing_ref, own_ref, sem,
):
    copies = fetches(place_ref, analysis_ref, own_ref, sem)
    for copy in copies:
        copy.start()
    row, j = iota((128, 128), 0), iota((128, 128), 1)
    who, other = row & 15, other_column_ref[...]
    pair = (row >= 16) & (row < 80)
    for i in range(MEMBERS):
        own = (j == i).astype(F32)
        value = jnp.where(pair & (who == i), (other == j).astype(F32) - own, 0.0)
        value = value + jnp.where(pair & (other == i), (who == j).astype(F32) - own, 0.0)
        value = value + jnp.where((row < 16) & (who == i), own, 0.0)
        to_mixing_ref[:, 128 * i : 128 * i + 128] = value.astype(BF)
    for copy in copies:
        copy.wait()
    for n in range(4):
        choose = full_ref[...] if n < 2 else half_ref[n - 2]
        own = own_ref[min(n, 2)]
        to_ref = to_full_ref.at[n] if n < 2 else to_half_ref.at[n - 2]
        from_ref = from_full_ref.at[n] if n < 2 else from_half_ref.at[n - 2]
        spread = dot(own, choose, 0, 0)
        member = iota(spread.shape, 1) % 2
        for i in range(2):
            to_ref[i] = jnp.where(member == i, spread, 0.0).astype(BF)
        spread = dot(choose, own, 0, 0)
        member = iota(spread.shape, 0) % 2
        for i in range(2):
            from_ref[i] = jnp.where(member == i, spread, 0.0).astype(BF)


def prepare(place, analysis, full, half, other):
    return pl.pallas_call(
        prepare_kernel,
        out_shape=[
            jax.ShapeDtypeStruct((2, 2, L, 640), BF),
            jax.ShapeDtypeStruct((2, 2, L, WIDE), BF),
            jax.ShapeDtypeStruct((2, 2, 640, L), BF),
            jax.ShapeDtypeStruct((2, 2, WIDE, L), BF),
            jax.ShapeDtypeStruct((128, MEMBERS * 128), BF),
        ],
        in_specs=[SMEM, HBM, VMEM, VMEM, VMEM],
        out_specs=[VMEM] * 5,
        scratch_shapes=[pltpu.VMEM((3, NLAT, L), BF), pltpu.SemaphoreType.DMA((3,))],
        compiler_params=pltpu.CompilerParams(vmem_limit_bytes=63 * MIB),
        name="prepare",
    )(place, analysis, full, half, other)


def block_mask(size, kind, lanes=None):
    shape = (size, lanes or size)
    row, lane = iota(shape, 0), iota(shape, 1)
    same = (row >> 4) == (lane >> 4) if kind == "block" else (row & 15) == (lane & 15)
    return same.astype(F32).astype(BF)


def pick_bands(bands, mask):
    shape = (GROUP, 128)
    one_hot = jnp.broadcast_to(bands, shape) == (iota(shape, 1) & 15).astype(F32)
    tile = jnp.concatenate([one_hot.astype(F32).astype(BF)] * MEMBERS, axis=0)
    return jnp.concatenate([tile, tile], axis=1) * mask


def fold(x):
    x = x[:, :128] + x[:, 128:]
    for shift in (64, 32, 16):
        x = x + pltpu.roll(x, shift, 1)
    return x


def compact(x):
    top, rest = x[:8], x[8:]
    lane = iota((8, 128), 1)
    first = jnp.where(lane < 80, top, pltpu.roll(rest, 80, 1))
    left = pltpu.roll(rest, 80, 1)
    lane = iota((1, 128), 1)
    tails = []
    for n in range(2):
        tail = jnp.zeros((1, 128), F32)
        for r in range(4):
            row = pltpu.roll(left[4 * n + r : 4 * n + r + 1], 32 * r, 1)
            tail = jnp.where((lane >= 32 * r) & (lane < 32 * r + 32), row, tail)
        tails.append(tail)
    return jnp.concatenate([first] + tails, axis=0)


def expand(x):
    first = x[:8]
    lane = iota((8, 128), 1)
    top = jnp.where(lane < 80, first, 0.0)
    rows = []
    for n in range(2):
        for r in range(4):
            rows.append(pltpu.roll(x[8 + n : 9 + n], (48 - 32 * r) % 128, 1))
    rest = jnp.where(lane < 48, pltpu.roll(first, 48, 1), jnp.concatenate(rows, axis=0))
    return jnp.concatenate([top, jnp.where(lane < 80, rest, 0.0)], axis=0)


def spectra_kernel(place_ref, rows_hbm, to_full_hbm, to_half_hbm, other_ref, *refs):
    target_refs = refs[:8]
    stacked_hbm, target_hbm, sums_hbm = refs[8:11]
    to_full_ref, to_half_ref, stacked_ref, target_ref, sums_ref = refs[11:16]
    rows_ref, mask_ref, order_ref, in_sem, rows_sem, target_sem, out_sem = refs[16:]

    def load_rows(g):
        where = pl.ds(2 * g, 2)
        return pltpu.make_async_copy(rows_hbm.at[:, where], rows_ref.at[:, where], rows_sem.at[g])

    load_rows(0).start()
    loads = [pltpu.make_async_copy(to_full_hbm, to_full_ref, in_sem.at[0])]
    loads.append(pltpu.make_async_copy(to_half_hbm, to_half_ref, in_sem.at[1]))
    for k in range(8):
        there = order_ref.at[jnp.bitwise_xor(place_ref[1], k)]
        loads.append(pltpu.make_async_copy(target_refs[k], there, target_sem.at[k]))
    for copy in loads[:2]:
        copy.start()
    for g in range(1, 4):
        load_rows(g).start()
    for copy in loads[2:]:
        copy.start()
    mask_ref[...] = block_mask(256, "block")
    for copy in loads[:2]:
        copy.wait()
    base = place_ref[0] * 20
    orders = [base + m for m in own_orders(place_ref)]
    degree = iota((L, 128), 0)
    low = iota((L, 128), 1) < 64
    keeps = [degree >= orders[0], degree >= orders[1], (degree >= orders[2]) & low]

    def transform(g, carry):
        load_rows(g).wait()
        for slot in range(3):
            values = two_rows_of(rows_ref, g, slot)
            for i in range(2):
                if slot < 2:
                    parts = halves(dot(to_full_ref[slot, i], values))
                else:
                    parts = halves(dot(to_half_ref[0, i], values))
                    other = halves(dot(to_half_ref[1, i], values))
                    parts = [parts[k] + swap_halves(other[k]) for k in range(2)]
                for k in range(2):
                    stacked_ref[4 * g + 2 * k + i, :, 128 * slot : 128 * slot + 128] = jnp.where(
                        keeps[slot], parts[k], 0.0
                    ).astype(BF)
        store(g).start()
        return carry

    def store(g):
        where = pl.ds(4 * g, 4)
        return pltpu.make_async_copy(stacked_ref.at[where], stacked_hbm.at[where], out_sem.at[g])

    lax.fori_loop(0, 4, transform, 0)
    for copy in loads[2:]:
        copy.wait()
    target_ref[...] = order_ref[...].astype(F32).reshape(L, WIDE).astype(BF)
    stores = [pltpu.make_async_copy(target_ref, target_hbm, out_sem.at[4])]
    for slot in range(3):
        lanes = slice(128 * slot, 128 * slot + 128)
        observed = jnp.where(keeps[slot], target_ref[:, lanes].astype(F32), 0.0)
        stacked_ref[MEMBERS, :, lanes] = observed.astype(BF)
    last = stacked_hbm.at[MEMBERS]
    stores.append(pltpu.make_async_copy(stacked_ref.at[MEMBERS], last, out_sem.at[5]))
    for copy in stores:
        copy.start()

    size = MEMBERS * GROUP
    same = (iota((JJ * GROUP, size), 0) & 15) == (iota((JJ * GROUP, size), 1) & 15)
    empty = jnp.zeros((32 - JJ, size), F32)

    def gram(g, carry):
        totals, last = carry
        start = pl.multiple_of(g * GROUP, GROUP)
        block = stacked_ref[:, pl.ds(start, GROUP), :].reshape(JJ * GROUP, WIDE)
        products = jnp.where(same, dot(block, block[:size], 1, 1), 0.0)
        products = jnp.sum(products.reshape(JJ, GROUP, size), axis=1)
        parts = split3(jnp.concatenate([products, empty], axis=0))
        bands = band_column(target_ref, start, GROUP)
        moved = dot(jnp.concatenate(parts, axis=0), pick_bands(bands, mask_ref[...]))
        totals = totals + (moved[:32] + moved[32:64] + moved[64:])
        own = block[size:].astype(F32)
        power = jnp.sum(own * own, axis=1, keepdims=True)
        lane = (iota((GROUP, 128), 1) & 15).astype(F32)
        power = jnp.where(jnp.broadcast_to(bands, (GROUP, 128)) == lane, power, 0.0)
        return totals, last + jnp.sum(power, axis=0, keepdims=True)

    start = (jnp.zeros((32, size), F32), jnp.zeros((1, 128), F32))
    totals, last = lax.fori_loop(0, NGROUPS, gram, start, unroll=2)

    grams = totals[:MEMBERS]
    member = iota((MEMBERS, size), 1) >> 4
    diagonal = jnp.where(iota((MEMBERS, size), 0) == member, grams, 0.0)
    powers = jnp.sum(diagonal, axis=0, keepdims=True)
    own_power = fold(diagonal)
    squares = jnp.concatenate([own_power, own_power], axis=1) + powers - 2.0 * grams
    beside = powers + jnp.concatenate([last, last], axis=1) - 2.0 * totals[MEMBERS : MEMBERS + 1]
    beside = jnp.broadcast_to(beside, (MEMBERS, size))
    chosen = fold(jnp.where(iota((MEMBERS, size), 0) == member, beside, 0.0))
    kind = iota((MEMBERS, 128), 1) >> 4
    wanted = jnp.where(kind == 0, chosen, 0.0)
    for p in range(PARTNERS):
        other = other_ref[GROUP * (p + 1) : GROUP * (p + 2), :]
        other = jnp.concatenate([other, other], axis=1)
        chosen = fold(jnp.where(member == other, squares, 0.0))
        wanted = wanted + jnp.where(kind == p + 1, chosen, 0.0)
    wanted = jnp.concatenate([wanted, jnp.zeros((112, 128), F32)], axis=0).T
    squares = wanted[:NBANDS]
    for c in range(1, PARTNERS + 1):
        squares = squares + pltpu.roll(wanted[16 * c : 16 * c + 16], 16 * c, 1)
    sums = compact(squares)
    sums = jnp.concatenate([sums] * 4, axis=0)
    sums_ref[...] = jnp.broadcast_to(sums[None], (32, 40, 128))
    stores.append(pltpu.make_async_copy(sums_ref, sums_hbm, out_sem.at[6]))
    stores[2].start()
    for copy in stores:
        copy.wait()
    for g in range(4):
        store(g).wait()


def spectra(place, rows, to_full, to_half, other, targets):
    return pl.pallas_call(
        spectra_kernel,
        out_shape=[
            jax.ShapeDtypeStruct((JJ, L, WIDE), BF),
            jax.ShapeDtypeStruct((L, WIDE), BF),
            jax.ShapeDtypeStruct((32, 40, 128), F32),
        ],
        in_specs=[SMEM] + [HBM] * 3 + [VMEM] + [HBM] * 8,
        out_specs=[HBM] * 3,
        scratch_shapes=[
            pltpu.VMEM((2, 2, L, 640), BF),
            pltpu.VMEM((2, 2, L, WIDE), BF),
            pltpu.VMEM((JJ, L, WIDE), BF),
            pltpu.VMEM((L, WIDE), BF),
            pltpu.VMEM((32, 40, 128), F32),
            pltpu.VMEM((16, 8, 104, 128), BF),
            pltpu.VMEM((256, 256), BF),
            pltpu.VMEM((8, 40, WIDE), BF),
            pltpu.SemaphoreType.DMA((2,)),
            pltpu.SemaphoreType.DMA((4,)),
            pltpu.SemaphoreType.DMA((8,)),
            pltpu.SemaphoreType.DMA((7,)),
        ],
        compiler_params=pltpu.CompilerParams(vmem_limit_bytes=60 * MIB),
        cost_estimate=pl.CostEstimate(
            flops=10_000_000_000, bytes_accessed=12_000_000, transcendentals=0
        ),
        name="spectra",
    )(place, rows, to_full, to_half, other, *targets)


def gradient_kernel(
    stacked_hbm, target_hbm, sums_ref, cotangent_ref, share_ref, to_mixing_hbm,
    from_full_hbm, from_half_hbm,
    back_ref, grad_hbm, loss_ref,
    stacked_ref, target_ref, to_mixing_ref, from_full_ref, from_half_ref, grad_ref,
    held_ref, member_ref, degree_ref, in_sem, stacked_sem, sem,
):
    loads = [
        pltpu.make_async_copy(there, here, in_sem.at[n])
        for n, (there, here) in enumerate(
            (
                (to_mixing_hbm, to_mixing_ref),
                (target_hbm, target_ref),
                (from_full_hbm, from_full_ref),
                (from_half_hbm, from_half_ref),
            )
        )
    ]
    piece = L // 4

    def load_piece(n):
        where = pl.ds(piece * n, piece)
        return pltpu.make_async_copy(
            stacked_hbm.at[:, where], stacked_ref.at[:, where], stacked_sem.at[n]
        )

    def keep_piece(n):
        where = pl.ds(piece * n, piece)
        return pltpu.make_async_copy(grad_ref.at[:, where], grad_hbm.at[:, where], sem.at[4 + n])

    for copy in loads[:2]:
        copy.start()
    for n in range(4):
        load_piece(n).start()
    for copy in loads[2:]:
        copy.start()
    member_ref[...] = block_mask(256, "block")
    degree_ref[...] = block_mask(256, "inside")
    sums = jnp.sum(sums_ref[...], axis=0)
    sums = sum(sums[10 * n : 10 * n + 10] for n in range(4))
    lane = iota((NBANDS, 128), 1)
    distance = jnp.sqrt(jnp.maximum(expand(sums), 0.0) + EPSILON)
    cotangent = cotangent_ref[...]
    share = share_ref[0:1, :]
    score = jnp.sum(distance * share, axis=1, keepdims=True)
    loss_ref[...] = score * cotangent
    weight = cotangent * (16.0 * MEMBERS * NLAT) * jnp.abs(share) / distance
    beside = jnp.where(lane < MEMBERS, -weight, 0.0)
    loads[0].wait()
    mixing = sum(dot(part, to_mixing_ref[...]) for part in split3(weight))
    mixing = [mixing[:, 128 * i : 128 * i + 128] for i in range(MEMBERS)]

    size = MEMBERS * GROUP
    widen = (iota((128, size), 0) == (iota((128, size), 1) >> 4)).astype(F32).astype(BF)
    mix_high, mix_low = split2(jnp.concatenate(mixing, axis=0))
    mix_high = dot(mix_high, widen).astype(BF)
    mix_low = dot(mix_low, widen).astype(BF)
    beside = jnp.concatenate([beside, jnp.zeros((128 - NBANDS, 128), F32)], axis=0)
    beside_high, beside_low = split2(beside)
    band_of_lane = iota((GROUP, 128), 1).astype(F32)

    def mix(g, carry):
        start = pl.multiple_of(g * GROUP, GROUP)
        bands = band_column(target_ref, start, GROUP)
        pick = pick_bands(bands, member_ref[...])
        degree = degree_ref[...]
        high = dot(pick, mix_high).astype(BF) * degree
        low = dot(pick, mix_low).astype(BF) * degree
        one_hot = (jnp.broadcast_to(bands, (GROUP, 128)) == band_of_lane).astype(F32).astype(BF)
        weights = dot(one_hot, beside_high) + dot(one_hot, beside_low)
        weights = jnp.concatenate(
            [jnp.broadcast_to(weights[:, i : i + 1], (GROUP, 128)) for i in range(MEMBERS)], axis=0
        )
        block = stacked_ref[0:MEMBERS, pl.ds(start, GROUP), :].reshape(size, WIDE)
        own = stacked_ref[MEMBERS, pl.ds(start, GROUP), :].astype(F32)
        grad = dot(high, block) + dot(low, block)
        for slot in range(3):
            lanes = slice(128 * slot, 128 * slot + 128)
            part = grad[:, lanes] + weights * jnp.concatenate([own[:, lanes]] * MEMBERS, axis=0)
            grad_ref[:, pl.ds(start, GROUP), lanes] = part.astype(BF).reshape(MEMBERS, GROUP, 128)
        return carry

    loads[1].wait()
    for n in range(4):
        load_piece(n).wait()
        lax.fori_loop(5 * n, 5 * n + 5, mix, 0, unroll=5)
        keep_piece(n).start()
    for copy in loads[2:]:
        copy.wait()
    def inverse(g, carry):
        for slot in range(3):
            grads = [jnp.concatenate(grads_of(grad_ref, g, i, slot), axis=1) for i in range(2)]
            from_ref = from_full_ref.at[slot] if slot < 2 else from_half_ref.at[0]
            parts = halves(dot(from_ref[0], grads[0]) + dot(from_ref[1], grads[1]))
            if slot == 2:
                from_ref = from_half_ref.at[1]
                other = halves(dot(from_ref[0], grads[0]) + dot(from_ref[1], grads[1]))
                parts = [parts[k] + swap_halves(other[k]) for k in range(2)]
            start, count = STARTS[slot], COUNTS[slot]
            for k in range(2):
                part = parts[k].reshape(16, count, 128).astype(BF)
                held_ref[:, 2 * g + k, start : start + count, :] = part
        send(g).start()
        return carry

    def send(g):
        where = pl.ds(2 * g, 2)
        return pltpu.make_async_copy(held_ref.at[:, where], back_ref.at[:, where], sem.at[g])

    lax.fori_loop(0, 4, inverse, 0)
    for g in range(4):
        send(g).wait()
        keep_piece(g).wait()


def grads_of(grad_ref, g, i, slot):
    lanes = slice(128 * slot, 128 * slot + 128)
    return [grad_ref[4 * g + 2 * k + i, :, lanes] for k in range(2)]


def gradient(stacked, target, sums, cotangent, share, to_mixing, from_full, from_half):
    return pl.pallas_call(
        gradient_kernel,
        out_shape=[
            jax.ShapeDtypeStruct((16, 8, 104, 128), BF),
            jax.ShapeDtypeStruct((MEMBERS, L, WIDE), BF),
            jax.ShapeDtypeStruct((NBANDS, 128), F32),
        ],
        in_specs=[HBM, HBM, VMEM, VMEM, VMEM, HBM, HBM, HBM],
        out_specs=[HBM, HBM, VMEM],
        scratch_shapes=[
            pltpu.VMEM((JJ, L, WIDE), BF),
            pltpu.VMEM((L, WIDE), BF),
            pltpu.VMEM((128, MEMBERS * 128), BF),
            pltpu.VMEM((2, 2, 640, L), BF),
            pltpu.VMEM((2, 2, WIDE, L), BF),
            pltpu.VMEM((MEMBERS, L, WIDE), BF),
            pltpu.VMEM((16, 8, 104, 128), BF),
            pltpu.VMEM((256, 256), BF),
            pltpu.VMEM((256, 256), BF),
            pltpu.SemaphoreType.DMA((4,)),
            pltpu.SemaphoreType.DMA((4,)),
            pltpu.SemaphoreType.DMA((8,)),
        ],
        compiler_params=pltpu.CompilerParams(vmem_limit_bytes=63 * MIB),
        cost_estimate=pl.CostEstimate(
            flops=10_000_000_000, bytes_accessed=12_000_000, transcendentals=0
        ),
        name="gradient",
    )(stacked, target, sums, cotangent, share, to_mixing, from_full, from_half)


def weight_kernel(
    place_ref, rows_ref, grad_ref, full_ref, half_ref, weight_ref, full_sum_ref, half_sum_ref
):
    full_sum_ref[...] = jnp.zeros_like(full_sum_ref)
    half_sum_ref[...] = jnp.zeros_like(half_sum_ref)

    def step(g, carry):
        for slot in range(3):
            values = two_rows_of(rows_ref, g, slot)
            member = iota((values.shape[0], L), 0) % 2
            sides = [[grads_of(grad_ref, g, i, slot) for i in range(2)]]
            if slot == 2:
                sides.append(
                    [[swap_halves(x.astype(F32)).astype(BF) for x in pair] for pair in sides[0]]
                )
            for h, side in enumerate(sides):
                grads = [jnp.concatenate(side[i], axis=1) for i in range(2)]
                terms = jnp.where(
                    member == 0, dot(values, grads[0], 1, 1), dot(values, grads[1], 1, 1)
                )
                if slot < 2:
                    full_sum_ref[slot] += terms
                else:
                    half_sum_ref[h] += terms
        return carry

    lax.fori_loop(0, 4, step, 0)
    for slot in range(3):
        if slot < 2:
            parts = split2(full_sum_ref[slot])
            weight = dot(full_ref[...], parts[0]) + dot(full_ref[...], parts[1])
        else:
            weight = jnp.zeros((NLAT, L), F32)
            for h in range(2):
                parts = split2(half_sum_ref[h])
                weight = weight + dot(half_ref[h], parts[0]) + dot(half_ref[h], parts[1])
        weight = weight * WEIGHT_RATIO
        for c in range(16):
            other = jnp.bitwise_xor(place_ref[2], c // 8)
            step_to = jnp.bitwise_xor(place_ref[1], c % 8)
            weight_ref[other, step_to, slot] = weight[20 * c : 20 * c + 20].astype(BF)


def weights(place, rows, grads, full, half):
    return pl.pallas_call(
        weight_kernel,
        out_shape=jax.ShapeDtypeStruct((2, 8, 3, 20, L), BF),
        in_specs=[SMEM] + [VMEM] * 4,
        out_specs=VMEM,
        scratch_shapes=[
            pltpu.VMEM((2, 640, L), F32),
            pltpu.VMEM((2, WIDE, L), F32),
        ],
        compiler_params=pltpu.CompilerParams(vmem_limit_bytes=63 * MIB),
        cost_estimate=pl.CostEstimate(
            flops=5_000_000_000, bytes_accessed=8_000_000, transcendentals=0
        ),
        name="weights",
    )(place, rows, grads, full, half)


def finish_kernel(place_ref, *refs):
    *r_refs, o_ref, order_ref = refs
    for k in range(8):
        order_ref[jnp.bitwise_xor(place_ref[1], k)] = r_refs[k][...]
    for e in range(8):
        o_ref[:, e, :] = order_ref[e, 0].astype(F32)
        o_ref[:, 8 + e, :] = order_ref[e, 1].astype(F32)
    for p in range(4):
        o_ref[:, 16 + p, :] = order_ref[2 * p, 2].astype(F32) + order_ref[2 * p + 1, 2].astype(F32)


def finish(place, received):
    return pl.pallas_call(
        finish_kernel,
        out_shape=jax.ShapeDtypeStruct((20, 20, L), F32),
        in_specs=[SMEM] + [VMEM] * 8,
        out_specs=VMEM,
        scratch_shapes=[pltpu.VMEM((8, 3, 20, L), BF)],
        name="finish",
    )(place, *received)


def exchange(x, axes):
    return lax.all_to_all(x, axes, split_axis=0, concat_axis=0, tiled=True)


def swap(blocks):
    return [blocks[0]] + [
        lax.ppermute(blocks[k], ENS, [(e, e ^ k) for e in range(8)]) for k in range(1, 8)
    ]


def travel(x):
    moved = exchange(x.reshape(128, 52, 2, 128), EVERY)
    return moved.reshape(16, 8, 104, 128)


def body(fourier, analysis, target, band_ids, partners, band_cotangent):
    place = jnp.stack([lax.axis_index(ORDER), lax.axis_index(ENS), lax.axis_index("dp")])
    place = place.astype(jnp.int32)
    full = jnp.asarray(FULL, BF)
    half = jnp.asarray(HALF, BF)
    by_order = jnp.transpose(analysis, (1, 0, 2))
    native = jnp.transpose(fourier[0].reshape(2, 20, 320, 128), (1, 2, 0, 3)).reshape(20, 640, 128)
    packed = pack(native)
    target_in, partners, full, cotangent, packed = lax.optimization_barrier(
        (target[0], partners, full, band_cotangent, packed)
    )
    rows = travel(packed)
    targets = swap(target_blocks(place, target_in, band_ids))
    other = jnp.concatenate(
        [jnp.full((16,), MEMBERS, jnp.int32), partners.T.reshape(64), jnp.zeros((48,), jnp.int32)]
    )
    other = jnp.broadcast_to(other[:, None], (128, 128))
    to_full, to_half, from_full, from_half, to_mixing = prepare(
        place, by_order, full, half, other
    )
    cotangent = lax.dynamic_slice_in_dim(cotangent, lax.axis_index("dp"), 1, 0)[0]
    cotangent = jnp.broadcast_to(cotangent[:, None], (NBANDS, 128))
    cotangent, rows = lax.optimization_barrier((cotangent, rows))
    share = np.zeros((8, 128), np.float32)
    share[:, :16] = 1.0 / MEMBERS
    share[:, 16:80] = -1.0 / (2.0 * MEMBERS * PARTNERS)
    stacked, observed, sums = spectra(place, rows, to_full, to_half, other, targets)
    sums = exchange(sums.reshape(128, 5, 2, 128), EVERY).reshape(32, 40, 128)
    back, grads, loss = gradient(
        stacked, observed, sums, cotangent, jnp.asarray(share), to_mixing, from_full, from_half
    )
    returned = travel(back)
    loss = loss[:, 0]
    loss_bands = loss + lax.ppermute(loss, "dp", [(0, 1), (1, 0)])
    weight = weights(place, rows, grads, full, half)
    beside = lax.ppermute(weight[1], "dp", [(0, 1), (1, 0)])
    weight = (weight[0].astype(F32) + beside.astype(F32)).astype(BF)
    native_grad, place = lax.optimization_barrier((unpack(returned), place))
    grad_analysis = finish(place, swap([weight[k] for k in range(8)]))
    native_grad = native_grad.reshape(20, 320, 2, 128)
    grad_fourier = jnp.transpose(native_grad, (2, 0, 1, 3)).reshape(1, 2, 20, 40960)
    return (grad_fourier, grad_analysis, loss_bands)


def solution(mesh):
    torus = Mesh(
        mesh.devices.reshape(mesh.shape["dp"], 4, 4, 2, 4),
        ("dp", "order_0", "order_1", "ens_0", "ens_1"),
    )
    in_specs = (
        P("dp", ENS, ORDER, None),
        P(None, ORDER, None),
        P("dp", ENS, ORDER),
        P(ENS, ORDER),
        P(),
        P(),
    )
    out_specs = (P("dp", ENS, ORDER, None), P(DP_ENS, ORDER, None), P())
    return jax.shard_map(body, mesh=torus, in_specs=in_specs, out_specs=out_specs, check_vma=False)
```

```python
import functools

import jax
import jax.numpy as jnp
import numpy as np
from jax import lax
from jax.experimental import pallas as pl
from jax.experimental.pallas import tpu as pltpu
from jax.sharding import Mesh
from jax.sharding import PartitionSpec as P

MEMBERS = 16
NLAT = 320
L = 320
NBANDS = 16
PARTNERS = 4
JJ = MEMBERS + 1
ORDER = ("order_0", "order_1")
ENS = ("ens_0", "ens_1")
DP_ENS = ("dp", "ens_0", "ens_1")
EVERY = ORDER + ENS
EPSILON = 1e-06
WEIGHT_RATIO = 1.0 / 64.0
BF = jnp.bfloat16
F32 = jnp.float32
GROUP = 16
NGROUPS = L // GROUP
WIDE = 384
MIB = 1024 * 1024
VMEM = pl.BlockSpec(memory_space=pltpu.VMEM)
SMEM = pl.BlockSpec(memory_space=pltpu.SMEM)
HBM = pl.BlockSpec(memory_space=pltpu.HBM)


def selections():
    full = np.zeros((NLAT, 640), np.float32)
    half = np.zeros((2, NLAT, WIDE), np.float32)
    for t in range(NLAT):
        full[t, 2 * t : 2 * t + 2] = 1.0
        o, rest = divmod(t, 20)
        h, s = divmod(rest, 10)
        half[h, t, 24 * o + 2 * s : 24 * o + 2 * s + 2] = 1.0
    return full, half


def orderings():
    whole = np.zeros((64, 64), np.float32)
    half = np.zeros((2, 96, 160), np.float32)
    for i in range(2):
        for t in range(4):
            for e in range(8):
                whole[8 * e + 2 * t + i, 16 * t + 2 * e + i] = 1.0
        for t in range(20):
            h, s = divmod(t, 10)
            for p in range(4):
                half[h, 24 * p + 2 * s + i, 8 * t + 2 * p + i] = 1.0
    return whole, half


FULL, HALF = selections()
WHOLE_ORDER, HALF_ORDER = orderings()


def dot(a, b, ca=1, cb=0):
    return lax.dot_general(a, b, (((ca,), (cb,)), ((), ())), preferred_element_type=F32)


def iota(shape, dim):
    return lax.broadcasted_iota(jnp.int32, shape, dim)


def swap_halves(x):
    return pltpu.roll(x, 64, x.ndim - 1)


def split2(x):
    high = x.astype(BF)
    return high, (x - high.astype(F32)).astype(BF)


def split3(x):
    high = x.astype(BF)
    rest = x - high.astype(F32)
    mid = rest.astype(BF)
    return high, mid, (rest - mid.astype(F32)).astype(BF)


STEP = 4


def pack_step(x_ref, whole_ref, half_ref, o_ref):
    def block(rows, columns):
        return x_ref[rows, columns, :].astype(F32).reshape(-1, 128).astype(BF)

    for k in range(STEP):
        for slot in range(2):
            start = 40 * k + 16 * slot
            parts = [block(slice(4 * c, 4 * c + 4), slice(start, start + 16)) for c in range(5)]
            moved = dot(whole_ref[...], jnp.concatenate(parts, axis=1))
            moved = [moved[:, 128 * c : 128 * c + 128].reshape(8, 8, 128) for c in range(5)]
            moved = jnp.concatenate(moved, axis=1).astype(BF)
            o_ref[k, :, 40 * slot : 40 * slot + 40, :] = moved
    parts = [block(slice(0, 20), slice(40 * k + 32, 40 * k + 40)) for k in range(STEP)]
    values = jnp.concatenate(parts, axis=1)
    firsts = dot(half_ref[0], values)
    seconds = dot(half_ref[1], values)
    low = iota((96, 128), 1) < 64
    for k in range(STEP):
        first = firsts[:, 128 * k : 128 * k + 128]
        second = seconds[:, 128 * k : 128 * k + 128]
        real = jnp.where(low, first, swap_halves(second)).astype(BF)
        imaginary = jnp.where(low, swap_halves(first), second).astype(BF)
        for p in range(4):
            o_ref[k, 2 * p, 80:104, :] = real[24 * p : 24 * p + 24]
            o_ref[k, 2 * p + 1, 80:104, :] = imaginary[24 * p : 24 * p + 24]


def unpack_step(y_ref, whole_ref, half_ref, x_ref):
    for k in range(STEP):
        for slot in range(2):
            rows = y_ref[k, :, 40 * slot : 40 * slot + 40, :].astype(F32)
            parts = [rows[:, 8 * c : 8 * c + 8].reshape(64, 128).astype(BF) for c in range(5)]
            moved = dot(whole_ref[...], jnp.concatenate(parts, axis=1))
            moved = [moved[:, 128 * c : 128 * c + 128].reshape(4, 16, 128) for c in range(5)]
            start = 40 * k + 16 * slot
            x_ref[:, start : start + 16, :] = jnp.concatenate(moved, axis=0).astype(BF)
    low = iota((96, 128), 1) < 64
    firsts, seconds = [], []
    for k in range(STEP):
        real, imaginary = [
            jnp.concatenate([y_ref[k, 2 * p + r, 80:104, :].astype(F32) for p in range(4)], axis=0)
            for r in range(2)
        ]
        firsts.append(jnp.where(low, real, swap_halves(imaginary)).astype(BF))
        seconds.append(jnp.where(low, swap_halves(real), imaginary).astype(BF))
    moved = dot(half_ref[0], jnp.concatenate(firsts, axis=1))
    moved = moved + dot(half_ref[1], jnp.concatenate(seconds, axis=1))
    for k in range(STEP):
        part = moved[:, 128 * k : 128 * k + 128].reshape(20, 8, 128).astype(BF)
        x_ref[:, 40 * k + 32 : 40 * k + 40, :] = part


def in_steps(step, place_in, place_out, in_hbm, whole_ref, half_ref, out_hbm, *refs, between=None):
    in_ref, out_ref, in_sem, out_sem = refs

    def load(g):
        return pltpu.make_async_copy(place_in(in_hbm, g), in_ref.at[g], in_sem.at[g])

    def store(g):
        return pltpu.make_async_copy(out_ref.at[g], place_out(out_hbm, g), out_sem.at[g])

    for g in range(16 // STEP):
        load(g).start()

    def one(g, carry):
        load(g).wait()
        step(in_ref.at[g], whole_ref, half_ref, out_ref.at[g])
        store(g).start()
        return carry

    lax.fori_loop(0, 8 // STEP, one, 0)
    if between is not None:
        between()
    lax.fori_loop(8 // STEP, 16 // STEP, one, 0)
    for g in range(16 // STEP):
        store(g).wait()


def unpack_kernel(place_ref, in_hbm, whole_ref, half_ref, *refs):
    r_refs, (out_hbm, weight_hbm), rest = refs[:8], refs[8:10], refs[10:]
    *step_refs, order_ref, weight_ref, r_sem, weight_sem = rest
    loads = [
        pltpu.make_async_copy(
            r_refs[k], order_ref.at[jnp.bitwise_xor(place_ref[1], k)], r_sem.at[k]
        )
        for k in range(8)
    ]
    out = pltpu.make_async_copy(weight_ref, weight_hbm, weight_sem)

    def finish():
        for copy in loads:
            copy.wait()
        for e in range(8):
            weight_ref[:, e, :] = order_ref[e, 0].astype(F32)
            weight_ref[:, 8 + e, :] = order_ref[e, 1].astype(F32)
        for p in range(4):
            both = order_ref[2 * p, 2].astype(F32) + order_ref[2 * p + 1, 2].astype(F32)
            weight_ref[:, 16 + p, :] = both
        out.start()

    for copy in loads:
        copy.start()
    in_steps(
        unpack_step, packed_at, native_at, in_hbm, whole_ref, half_ref, out_hbm, *step_refs,
        between=finish,
    )
    out.wait()


def native_at(ref, g):
    return ref.at[:, pl.ds(40 * STEP * g, 40 * STEP)]


def packed_at(ref, g):
    return ref.at[pl.ds(STEP * g, STEP)]


NATIVE = pltpu.VMEM((16 // STEP, 20, 40 * STEP, 128), BF)
PACKED = pltpu.VMEM((16 // STEP, STEP, 8, 104, 128), BF)
SEMS = [pltpu.SemaphoreType.DMA((16 // STEP,))] * 2


def pack(x):
    return pl.pallas_call(
        functools.partial(in_steps, pack_step, native_at, packed_at),
        out_shape=jax.ShapeDtypeStruct((16, 8, 104, 128), BF),
        in_specs=[HBM, VMEM, VMEM],
        out_specs=HBM,
        scratch_shapes=[NATIVE, PACKED] + SEMS,
        compiler_params=pltpu.CompilerParams(vmem_limit_bytes=63 * MIB),
        name="pack",
    )(x, jnp.asarray(WHOLE_ORDER, BF), jnp.asarray(HALF_ORDER, BF))


def unpack(place, y, received):
    return pl.pallas_call(
        unpack_kernel,
        out_shape=[
            jax.ShapeDtypeStruct((20, 640, 128), BF),
            jax.ShapeDtypeStruct((20, 20, L), F32),
        ],
        in_specs=[SMEM, HBM, VMEM, VMEM] + [HBM] * 8,
        out_specs=[HBM, HBM],
        scratch_shapes=[PACKED, NATIVE]
        + SEMS
        + [
            pltpu.VMEM((8, 3, 20, L), BF),
            pltpu.VMEM((20, 20, L), F32),
            pltpu.SemaphoreType.DMA((8,)),
            pltpu.SemaphoreType.DMA(()),
        ],
        compiler_params=pltpu.CompilerParams(vmem_limit_bytes=63 * MIB),
        name="unpack",
    )(
        place, y, jnp.asarray(WHOLE_ORDER.T, BF), jnp.asarray(HALF_ORDER.transpose(0, 2, 1), BF),
        *received,
    )


def target_kernel(place_ref, t_ref, band_ref, *refs):
    *o_refs, held_ref, sem = refs
    bands = jnp.broadcast_to(band_ref[:, 0:1].astype(F32), (40, 128))
    low = iota((40, 128), 1) < 64
    for k in range(8):
        e = jnp.bitwise_xor(place_ref[1], k)

        def lanes(start):
            return t_ref[:, pl.ds(pl.multiple_of(start, 128), 128)]

        middle = lanes(2048 + 128 * (e // 2)).astype(F32)
        held_ref[k, :, 0:128] = lanes(128 * e)
        held_ref[k, :, 128:256] = lanes(1024 + 128 * e)
        odd = jnp.broadcast_to(e % 2, (40, 128)) == 1
        part = jnp.where(odd, swap_halves(middle), middle)
        held_ref[k, :, 256:384] = jnp.where(low, part, bands).astype(BF)
    copies = [pltpu.make_async_copy(held_ref.at[k], o_refs[k], sem.at[k]) for k in range(8)]
    for copy in copies:
        copy.start()
    for copy in copies:
        copy.wait()


def target_blocks(place, target, bands):
    return pl.pallas_call(
        target_kernel,
        out_shape=[jax.ShapeDtypeStruct((40, WIDE), BF)] * 8,
        in_specs=[SMEM, VMEM, VMEM],
        out_specs=[HBM] * 8,
        scratch_shapes=[pltpu.VMEM((8, 40, WIDE), BF), pltpu.SemaphoreType.DMA((8,))],
        compiler_params=pltpu.CompilerParams(vmem_limit_bytes=63 * MIB),
        name="target_blocks",
    )(place, target, bands)


def own_orders(place_ref):
    ens = place_ref[1]
    return ens, 8 + ens, 16 + ens // 2


def fetches(place_ref, analysis_ref, own_ref, sem):
    return [
        pltpu.make_async_copy(analysis_ref.at[m], own_ref.at[k], sem.at[k])
        for k, m in enumerate(own_orders(place_ref))
    ]


def halves(x):
    return [x[:, 128 * k : 128 * k + 128] for k in range(2)]


STARTS = (0, 40, 80)
COUNTS = (40, 40, 24)


def two_rows_of(rows_ref, g, slot):
    start, count = STARTS[slot], COUNTS[slot]
    parts = [
        rows_ref[:, 2 * g + k, start : start + count, :]
        .astype(F32)
        .reshape(16 * count, 128)
        .astype(BF)
        for k in range(2)
    ]
    return jnp.concatenate(parts, axis=1)


def band_column(target_ref, start, count):
    return target_ref[pl.ds(start, count), 256:384].astype(F32)[:, 64:65]


def prepare_kernel(
    place_ref, analysis_ref, full_ref, half_ref, other_column_ref,
    to_full_ref, to_half_ref, from_full_ref, from_half_ref, to_mixing_ref, own_ref, sem,
):
    copies = fetches(place_ref, analysis_ref, own_ref, sem)
    for copy in copies:
        copy.start()
    row, j = iota((128, 128), 0), iota((128, 128), 1)
    who, other = row & 15, other_column_ref[...]
    pair = (row >= 16) & (row < 80)
    for i in range(MEMBERS):
        own = (j == i).astype(F32)
        value = jnp.where(pair & (who == i), (other == j).astype(F32) - own, 0.0)
        value = value + jnp.where(pair & (other == i), (who == j).astype(F32) - own, 0.0)
        value = value + jnp.where((row < 16) & (who == i), own, 0.0)
        to_mixing_ref[:, 128 * i : 128 * i + 128] = value.astype(BF)
    for copy in copies:
        copy.wait()
    for n in range(4):
        choose = full_ref[...] if n < 2 else half_ref[n - 2]
        own = own_ref[min(n, 2)]
        to_ref = to_full_ref.at[n] if n < 2 else to_half_ref.at[n - 2]
        from_ref = from_full_ref.at[n] if n < 2 else from_half_ref.at[n - 2]
        spread = dot(own, choose, 0, 0)
        member = iota(spread.shape, 1) % 2
        for i in range(2):
            to_ref[i] = jnp.where(member == i, spread, 0.0).astype(BF)
        spread = dot(choose, own, 0, 0)
        member = iota(spread.shape, 0) % 2
        for i in range(2):
            from_ref[i] = jnp.where(member == i, spread, 0.0).astype(BF)


def prepare(place, analysis, full, half, other):
    return pl.pallas_call(
        prepare_kernel,
        out_shape=[
            jax.ShapeDtypeStruct((2, 2, L, 640), BF),
            jax.ShapeDtypeStruct((2, 2, L, WIDE), BF),
            jax.ShapeDtypeStruct((2, 2, 640, L), BF),
            jax.ShapeDtypeStruct((2, 2, WIDE, L), BF),
            jax.ShapeDtypeStruct((128, MEMBERS * 128), BF),
        ],
        in_specs=[SMEM, HBM, VMEM, VMEM, VMEM],
        out_specs=[VMEM] * 5,
        scratch_shapes=[pltpu.VMEM((3, NLAT, L), BF), pltpu.SemaphoreType.DMA((3,))],
        compiler_params=pltpu.CompilerParams(vmem_limit_bytes=63 * MIB),
        name="prepare",
    )(place, analysis, full, half, other)


def block_mask(size, kind, lanes=None):
    shape = (size, lanes or size)
    row, lane = iota(shape, 0), iota(shape, 1)
    same = (row >> 4) == (lane >> 4) if kind == "block" else (row & 15) == (lane & 15)
    return same.astype(F32).astype(BF)


def pick_bands(bands, mask):
    shape = (GROUP, 128)
    one_hot = jnp.broadcast_to(bands, shape) == (iota(shape, 1) & 15).astype(F32)
    tile = jnp.concatenate([one_hot.astype(F32).astype(BF)] * MEMBERS, axis=0)
    return jnp.concatenate([tile, tile], axis=1) * mask


def fold(x):
    x = x[:, :128] + x[:, 128:]
    for shift in (64, 32, 16):
        x = x + pltpu.roll(x, shift, 1)
    return x


def compact(x):
    top, rest = x[:8], x[8:]
    lane = iota((8, 128), 1)
    first = jnp.where(lane < 80, top, pltpu.roll(rest, 80, 1))
    left = pltpu.roll(rest, 80, 1)
    lane = iota((1, 128), 1)
    tails = []
    for n in range(2):
        tail = jnp.zeros((1, 128), F32)
        for r in range(4):
            row = pltpu.roll(left[4 * n + r : 4 * n + r + 1], 32 * r, 1)
            tail = jnp.where((lane >= 32 * r) & (lane < 32 * r + 32), row, tail)
        tails.append(tail)
    return jnp.concatenate([first] + tails, axis=0)


def expand(x):
    first = x[:8]
    lane = iota((8, 128), 1)
    top = jnp.where(lane < 80, first, 0.0)
    rows = []
    for n in range(2):
        for r in range(4):
            rows.append(pltpu.roll(x[8 + n : 9 + n], (48 - 32 * r) % 128, 1))
    rest = jnp.where(lane < 48, pltpu.roll(first, 48, 1), jnp.concatenate(rows, axis=0))
    return jnp.concatenate([top, jnp.where(lane < 80, rest, 0.0)], axis=0)


def spectra_kernel(place_ref, rows_hbm, to_full_hbm, to_half_hbm, other_ref, *refs):
    target_refs = refs[:8]
    stacked_hbm, target_hbm, sums_hbm = refs[8:11]
    to_full_ref, to_half_ref, stacked_ref, target_ref, sums_ref = refs[11:16]
    rows_ref, mask_ref, order_ref, in_sem, rows_sem, target_sem, out_sem = refs[16:]

    def load_rows(g):
        where = pl.ds(2 * g, 2)
        return pltpu.make_async_copy(rows_hbm.at[:, where], rows_ref.at[:, where], rows_sem.at[g])

    load_rows(0).start()
    loads = [
        pltpu.make_async_copy(to_full_hbm.at[n], to_full_ref.at[n], in_sem.at[n]) for n in range(2)
    ]
    loads.append(pltpu.make_async_copy(to_half_hbm, to_half_ref, in_sem.at[2]))
    for k in range(8):
        there = order_ref.at[jnp.bitwise_xor(place_ref[1], k)]
        loads.append(pltpu.make_async_copy(target_refs[k], there, target_sem.at[k]))
    for copy in loads[:3]:
        copy.start()
    for g in range(1, 4):
        load_rows(g).start()
    for copy in loads[3:]:
        copy.start()
    mask_ref[...] = block_mask(256, "block")
    base = place_ref[0] * 20
    orders = [base + m for m in own_orders(place_ref)]
    degree = iota((L, 128), 0)
    low = iota((L, 128), 1) < 64
    keeps = [degree >= orders[0], degree >= orders[1], (degree >= orders[2]) & low]

    def transform(g, carry, operators=None):
        load_rows(g).wait()
        for slot in range(3):
            if operators:
                operators[slot].wait()
            values = two_rows_of(rows_ref, g, slot)
            for i in range(2):
                if slot < 2:
                    parts = halves(dot(to_full_ref[slot, i], values))
                else:
                    parts = halves(dot(to_half_ref[0, i], values))
                    other = halves(dot(to_half_ref[1, i], values))
                    parts = [parts[k] + swap_halves(other[k]) for k in range(2)]
                for k in range(2):
                    stacked_ref[4 * g + 2 * k + i, :, 128 * slot : 128 * slot + 128] = jnp.where(
                        keeps[slot], parts[k], 0.0
                    ).astype(BF)
        store(g).start()
        return carry

    def store(g):
        where = pl.ds(4 * g, 4)
        return pltpu.make_async_copy(stacked_ref.at[where], stacked_hbm.at[where], out_sem.at[g])

    transform(0, 0, loads[:3])
    lax.fori_loop(1, 4, transform, 0)
    for copy in loads[3:]:
        copy.wait()
    target_ref[...] = order_ref[...].astype(F32).reshape(L, WIDE).astype(BF)
    stores = [pltpu.make_async_copy(target_ref, target_hbm, out_sem.at[4])]
    for slot in range(3):
        lanes = slice(128 * slot, 128 * slot + 128)
        observed = jnp.where(keeps[slot], target_ref[:, lanes].astype(F32), 0.0)
        stacked_ref[MEMBERS, :, lanes] = observed.astype(BF)
    last = stacked_hbm.at[MEMBERS]
    stores.append(pltpu.make_async_copy(stacked_ref.at[MEMBERS], last, out_sem.at[5]))
    for copy in stores:
        copy.start()

    size = MEMBERS * GROUP
    same = (iota((JJ * GROUP, size), 0) & 15) == (iota((JJ * GROUP, size), 1) & 15)
    empty = jnp.zeros((32 - JJ, size), F32)

    def gram(g, carry):
        totals, last = carry
        start = pl.multiple_of(g * GROUP, GROUP)
        block = stacked_ref[:, pl.ds(start, GROUP), :].reshape(JJ * GROUP, WIDE)
        products = jnp.where(same, dot(block, block[:size], 1, 1), 0.0)
        products = jnp.sum(products.reshape(JJ, GROUP, size), axis=1)
        parts = split3(jnp.concatenate([products, empty], axis=0))
        bands = band_column(target_ref, start, GROUP)
        moved = dot(jnp.concatenate(parts, axis=0), pick_bands(bands, mask_ref[...]))
        totals = totals + (moved[:32] + moved[32:64] + moved[64:])
        own = block[size:].astype(F32)
        power = jnp.sum(own * own, axis=1, keepdims=True)
        lane = (iota((GROUP, 128), 1) & 15).astype(F32)
        power = jnp.where(jnp.broadcast_to(bands, (GROUP, 128)) == lane, power, 0.0)
        return totals, last + jnp.sum(power, axis=0, keepdims=True)

    start = (jnp.zeros((32, size), F32), jnp.zeros((1, 128), F32))
    totals, last = lax.fori_loop(0, NGROUPS, gram, start, unroll=2)

    grams = totals[:MEMBERS]
    member = iota((MEMBERS, size), 1) >> 4
    diagonal = jnp.where(iota((MEMBERS, size), 0) == member, grams, 0.0)
    powers = jnp.sum(diagonal, axis=0, keepdims=True)
    own_power = fold(diagonal)
    squares = jnp.concatenate([own_power, own_power], axis=1) + powers - 2.0 * grams
    beside = powers + jnp.concatenate([last, last], axis=1) - 2.0 * totals[MEMBERS : MEMBERS + 1]
    beside = jnp.broadcast_to(beside, (MEMBERS, size))
    chosen = fold(jnp.where(iota((MEMBERS, size), 0) == member, beside, 0.0))
    kind = iota((MEMBERS, 128), 1) >> 4
    wanted = jnp.where(kind == 0, chosen, 0.0)
    for p in range(PARTNERS):
        other = other_ref[GROUP * (p + 1) : GROUP * (p + 2), :]
        other = jnp.concatenate([other, other], axis=1)
        chosen = fold(jnp.where(member == other, squares, 0.0))
        wanted = wanted + jnp.where(kind == p + 1, chosen, 0.0)
    wanted = jnp.concatenate([wanted, jnp.zeros((112, 128), F32)], axis=0).T
    squares = wanted[:NBANDS]
    for c in range(1, PARTNERS + 1):
        squares = squares + pltpu.roll(wanted[16 * c : 16 * c + 16], 16 * c, 1)
    sums = compact(squares)
    sums = jnp.concatenate([sums] * 4, axis=0)
    sums_ref[...] = jnp.broadcast_to(sums[None], (32, 40, 128))
    stores.append(pltpu.make_async_copy(sums_ref, sums_hbm, out_sem.at[6]))
    stores[2].start()
    for copy in stores:
        copy.wait()
    for g in range(4):
        store(g).wait()


def spectra(place, rows, to_full, to_half, other, targets):
    return pl.pallas_call(
        spectra_kernel,
        out_shape=[
            jax.ShapeDtypeStruct((JJ, L, WIDE), BF),
            jax.ShapeDtypeStruct((L, WIDE), BF),
            jax.ShapeDtypeStruct((32, 40, 128), F32),
        ],
        in_specs=[SMEM] + [HBM] * 3 + [VMEM] + [HBM] * 8,
        out_specs=[HBM] * 3,
        scratch_shapes=[
            pltpu.VMEM((2, 2, L, 640), BF),
            pltpu.VMEM((2, 2, L, WIDE), BF),
            pltpu.VMEM((JJ, L, WIDE), BF),
            pltpu.VMEM((L, WIDE), BF),
            pltpu.VMEM((32, 40, 128), F32),
            pltpu.VMEM((16, 8, 104, 128), BF),
            pltpu.VMEM((256, 256), BF),
            pltpu.VMEM((8, 40, WIDE), BF),
            pltpu.SemaphoreType.DMA((3,)),
            pltpu.SemaphoreType.DMA((4,)),
            pltpu.SemaphoreType.DMA((8,)),
            pltpu.SemaphoreType.DMA((7,)),
        ],
        compiler_params=pltpu.CompilerParams(vmem_limit_bytes=60 * MIB),
        cost_estimate=pl.CostEstimate(
            flops=10_000_000_000, bytes_accessed=12_000_000, transcendentals=0
        ),
        name="spectra",
    )(place, rows, to_full, to_half, other, *targets)


def gradient_kernel(
    stacked_hbm, target_hbm, sums_ref, cotangent_ref, share_ref, to_mixing_hbm,
    from_full_hbm, from_half_hbm,
    back_ref, grad_hbm, loss_ref,
    stacked_ref, target_ref, to_mixing_ref, from_full_ref, from_half_ref, grad_ref,
    held_ref, member_ref, degree_ref, in_sem, stacked_sem, sem,
):
    loads = [
        pltpu.make_async_copy(there, here, in_sem.at[n])
        for n, (there, here) in enumerate(
            (
                (to_mixing_hbm, to_mixing_ref),
                (target_hbm, target_ref),
                (from_full_hbm, from_full_ref),
                (from_half_hbm, from_half_ref),
            )
        )
    ]
    piece = L // 4

    def load_piece(n):
        where = pl.ds(piece * n, piece)
        return pltpu.make_async_copy(
            stacked_hbm.at[:, where], stacked_ref.at[:, where], stacked_sem.at[n]
        )

    def keep_piece(n):
        where = pl.ds(piece * n, piece)
        return pltpu.make_async_copy(grad_ref.at[:, where], grad_hbm.at[:, where], sem.at[4 + n])

    for copy in loads[:2]:
        copy.start()
    for n in range(4):
        load_piece(n).start()
    for copy in loads[2:]:
        copy.start()
    member_ref[...] = block_mask(256, "block")
    degree_ref[...] = block_mask(256, "inside")
    sums = jnp.sum(sums_ref[...], axis=0)
    sums = sum(sums[10 * n : 10 * n + 10] for n in range(4))
    lane = iota((NBANDS, 128), 1)
    distance = jnp.sqrt(jnp.maximum(expand(sums), 0.0) + EPSILON)
    cotangent = cotangent_ref[...]
    share = share_ref[0:1, :]
    score = jnp.sum(distance * share, axis=1, keepdims=True)
    loss_ref[...] = score * cotangent
    weight = cotangent * (16.0 * MEMBERS * NLAT) * jnp.abs(share) / distance
    beside = jnp.where(lane < MEMBERS, -weight, 0.0)
    loads[0].wait()
    mixing = dot(jnp.concatenate(split3(weight), axis=0), to_mixing_ref[...])
    mixing = mixing[:16] + mixing[16:32] + mixing[32:]
    mixing = [mixing[:, 128 * i : 128 * i + 128] for i in range(MEMBERS)]

    size = MEMBERS * GROUP
    widen = (iota((128, size), 0) == (iota((128, size), 1) >> 4)).astype(F32).astype(BF)
    mix_high, mix_low = split2(jnp.concatenate(mixing, axis=0))
    mix_high = dot(mix_high, widen).astype(BF)
    mix_low = dot(mix_low, widen).astype(BF)
    beside_both = jnp.concatenate(
        [part.astype(F32) for part in split2(beside)] + [jnp.zeros((96, 128), F32)], axis=0
    ).astype(BF)
    band_of_lane = (iota((GROUP, 128), 1) & 15).astype(F32)

    def mix(g, carry):
        start = pl.multiple_of(g * GROUP, GROUP)
        bands = band_column(target_ref, start, GROUP)
        pick = pick_bands(bands, member_ref[...])
        degree = degree_ref[...]
        high = dot(pick, mix_high).astype(BF) * degree
        low = dot(pick, mix_low).astype(BF) * degree
        one_hot = (jnp.broadcast_to(bands, (GROUP, 128)) == band_of_lane).astype(F32).astype(BF)
        weights = dot(one_hot, beside_both)
        weights = jnp.concatenate(
            [jnp.broadcast_to(weights[:, i : i + 1], (GROUP, 128)) for i in range(MEMBERS)], axis=0
        )
        block = stacked_ref[0:MEMBERS, pl.ds(start, GROUP), :].reshape(size, WIDE)
        own = stacked_ref[MEMBERS, pl.ds(start, GROUP), :].astype(F32)
        grad = dot(high, block) + dot(low, block)
        for slot in range(3):
            lanes = slice(128 * slot, 128 * slot + 128)
            part = grad[:, lanes] + weights * jnp.concatenate([own[:, lanes]] * MEMBERS, axis=0)
            grad_ref[:, pl.ds(start, GROUP), lanes] = part.astype(BF).reshape(MEMBERS, GROUP, 128)
        return carry

    loads[1].wait()
    for n in range(4):
        load_piece(n).wait()
        lax.fori_loop(5 * n, 5 * n + 5, mix, 0, unroll=5)
        keep_piece(n).start()
    for copy in loads[2:]:
        copy.wait()
    def inverse(g, carry):
        for slot in range(3):
            grads = [jnp.concatenate(grads_of(grad_ref, g, i, slot), axis=1) for i in range(2)]
            from_ref = from_full_ref.at[slot] if slot < 2 else from_half_ref.at[0]
            parts = halves(dot(from_ref[0], grads[0]) + dot(from_ref[1], grads[1]))
            if slot == 2:
                from_ref = from_half_ref.at[1]
                other = halves(dot(from_ref[0], grads[0]) + dot(from_ref[1], grads[1]))
                parts = [parts[k] + swap_halves(other[k]) for k in range(2)]
            start, count = STARTS[slot], COUNTS[slot]
            for k in range(2):
                part = parts[k].reshape(16, count, 128).astype(BF)
                held_ref[:, 2 * g + k, start : start + count, :] = part
        send(g).start()
        return carry

    def send(g):
        where = pl.ds(2 * g, 2)
        return pltpu.make_async_copy(held_ref.at[:, where], back_ref.at[:, where], sem.at[g])

    lax.fori_loop(0, 4, inverse, 0)
    for g in range(4):
        send(g).wait()
        keep_piece(g).wait()


def grads_of(grad_ref, g, i, slot):
    lanes = slice(128 * slot, 128 * slot + 128)
    return [grad_ref[4 * g + 2 * k + i, :, lanes] for k in range(2)]


def gradient(stacked, target, sums, cotangent, share, to_mixing, from_full, from_half):
    return pl.pallas_call(
        gradient_kernel,
        out_shape=[
            jax.ShapeDtypeStruct((16, 8, 104, 128), BF),
            jax.ShapeDtypeStruct((MEMBERS, L, WIDE), BF),
            jax.ShapeDtypeStruct((NBANDS, 128), F32),
        ],
        in_specs=[HBM, HBM, VMEM, VMEM, VMEM, HBM, HBM, HBM],
        out_specs=[HBM, HBM, VMEM],
        scratch_shapes=[
            pltpu.VMEM((JJ, L, WIDE), BF),
            pltpu.VMEM((L, WIDE), BF),
            pltpu.VMEM((128, MEMBERS * 128), BF),
            pltpu.VMEM((2, 2, 640, L), BF),
            pltpu.VMEM((2, 2, WIDE, L), BF),
            pltpu.VMEM((MEMBERS, L, WIDE), BF),
            pltpu.VMEM((16, 8, 104, 128), BF),
            pltpu.VMEM((256, 256), BF),
            pltpu.VMEM((256, 256), BF),
            pltpu.SemaphoreType.DMA((4,)),
            pltpu.SemaphoreType.DMA((4,)),
            pltpu.SemaphoreType.DMA((8,)),
        ],
        compiler_params=pltpu.CompilerParams(vmem_limit_bytes=63 * MIB),
        cost_estimate=pl.CostEstimate(
            flops=10_000_000_000, bytes_accessed=12_000_000, transcendentals=0
        ),
        name="gradient",
    )(stacked, target, sums, cotangent, share, to_mixing, from_full, from_half)


def weight_kernel(
    place_ref, rows_ref, grad_ref, full_ref, half_ref, weight_ref, full_sum_ref, half_sum_ref
):
    full_sum_ref[...] = jnp.zeros_like(full_sum_ref)
    half_sum_ref[...] = jnp.zeros_like(half_sum_ref)

    def step(g, carry):
        for slot in range(3):
            values = two_rows_of(rows_ref, g, slot)
            member = iota((values.shape[0], L), 0) % 2
            sides = [[grads_of(grad_ref, g, i, slot) for i in range(2)]]
            if slot == 2:
                sides.append(
                    [[swap_halves(x.astype(F32)).astype(BF) for x in pair] for pair in sides[0]]
                )
            for h, side in enumerate(sides):
                grads = [jnp.concatenate(side[i], axis=1) for i in range(2)]
                terms = jnp.where(
                    member == 0, dot(values, grads[0], 1, 1), dot(values, grads[1], 1, 1)
                )
                if slot < 2:
                    full_sum_ref[slot] += terms
                else:
                    half_sum_ref[h] += terms
        return carry

    lax.fori_loop(0, 4, step, 0)
    for slot in range(3):
        if slot < 2:
            parts = split2(full_sum_ref[slot])
            weight = dot(full_ref[...], parts[0]) + dot(full_ref[...], parts[1])
        else:
            weight = jnp.zeros((NLAT, L), F32)
            for h in range(2):
                parts = split2(half_sum_ref[h])
                weight = weight + dot(half_ref[h], parts[0]) + dot(half_ref[h], parts[1])
        weight = weight * WEIGHT_RATIO
        for c in range(16):
            other = jnp.bitwise_xor(place_ref[2], c // 8)
            step_to = jnp.bitwise_xor(place_ref[1], c % 8)
            weight_ref[other, step_to, slot] = weight[20 * c : 20 * c + 20].astype(BF)


def weights(place, rows, grads, full, half):
    return pl.pallas_call(
        weight_kernel,
        out_shape=jax.ShapeDtypeStruct((2, 8, 3, 20, L), BF),
        in_specs=[SMEM] + [VMEM] * 4,
        out_specs=VMEM,
        scratch_shapes=[
            pltpu.VMEM((2, 640, L), F32),
            pltpu.VMEM((2, WIDE, L), F32),
        ],
        compiler_params=pltpu.CompilerParams(vmem_limit_bytes=63 * MIB),
        cost_estimate=pl.CostEstimate(
            flops=5_000_000_000, bytes_accessed=8_000_000, transcendentals=0
        ),
        name="weights",
    )(place, rows, grads, full, half)


def exchange(x, axes):
    return lax.all_to_all(x, axes, split_axis=0, concat_axis=0, tiled=True)


def swap(blocks):
    return [blocks[0]] + [
        lax.ppermute(blocks[k], ENS, [(e, e ^ k) for e in range(8)]) for k in range(1, 8)
    ]


def travel(x):
    moved = exchange(x.reshape(128, 52, 2, 128), EVERY)
    return moved.reshape(16, 8, 104, 128)


def body(fourier, analysis, target, band_ids, partners, band_cotangent):
    place = jnp.stack([lax.axis_index(ORDER), lax.axis_index(ENS), lax.axis_index("dp")])
    place = place.astype(jnp.int32)
    full = jnp.asarray(FULL, BF)
    half = jnp.asarray(HALF, BF)
    by_order = jnp.transpose(analysis, (1, 0, 2))
    native = jnp.transpose(fourier[0].reshape(2, 20, 320, 128), (1, 2, 0, 3)).reshape(20, 640, 128)
    packed = pack(native)
    target_in, partners, full, cotangent, packed = lax.optimization_barrier(
        (target[0], partners, full, band_cotangent, packed)
    )
    rows = travel(packed)
    targets = swap(target_blocks(place, target_in, band_ids))
    other = jnp.concatenate(
        [jnp.full((16,), MEMBERS, jnp.int32), partners.T.reshape(64), jnp.zeros((48,), jnp.int32)]
    )
    other = jnp.broadcast_to(other[:, None], (128, 128))
    to_full, to_half, from_full, from_half, to_mixing = prepare(
        place, by_order, full, half, other
    )
    cotangent = lax.dynamic_slice_in_dim(cotangent, lax.axis_index("dp"), 1, 0)[0]
    cotangent = jnp.broadcast_to(cotangent[:, None], (NBANDS, 128))
    cotangent, rows = lax.optimization_barrier((cotangent, rows))
    share = np.zeros((8, 128), np.float32)
    share[:, :16] = 1.0 / MEMBERS
    share[:, 16:80] = -1.0 / (2.0 * MEMBERS * PARTNERS)
    stacked, observed, sums = spectra(place, rows, to_full, to_half, other, targets)
    sums = exchange(sums.reshape(128, 5, 2, 128), EVERY).reshape(32, 40, 128)
    back, grads, loss = gradient(
        stacked, observed, sums, cotangent, jnp.asarray(share), to_mixing, from_full, from_half
    )
    returned = travel(back)
    loss = loss[:, 0]
    loss_bands = loss + lax.ppermute(loss, "dp", [(0, 1), (1, 0)])
    weight = weights(place, rows, grads, full, half)
    beside = lax.ppermute(weight[1], "dp", [(0, 1), (1, 0)])
    weight = (weight[0].astype(F32) + beside.astype(F32)).astype(BF)
    native_grad, grad_analysis = unpack(place, returned, swap([weight[k] for k in range(8)]))
    native_grad = native_grad.reshape(20, 320, 2, 128)
    grad_fourier = jnp.transpose(native_grad, (2, 0, 1, 3)).reshape(1, 2, 20, 40960)
    return (grad_fourier, grad_analysis, loss_bands)


def solution(mesh):
    torus = Mesh(
        mesh.devices.reshape(mesh.shape["dp"], 4, 4, 2, 4),
        ("dp", "order_0", "order_1", "ens_0", "ens_1"),
    )
    in_specs = (
        P("dp", ENS, ORDER, None),
        P(None, ORDER, None),
        P("dp", ENS, ORDER),
        P(ENS, ORDER),
        P(),
        P(),
    )
    out_specs = (P("dp", ENS, ORDER, None), P(DP_ENS, ORDER, None), P())
    return jax.shard_map(body, mesh=torus, in_specs=in_specs, out_specs=out_specs, check_vma=False)
```

```python
import functools

import jax
import jax.numpy as jnp
import numpy as np
from jax import lax
from jax.experimental import pallas as pl
from jax.experimental.pallas import tpu as pltpu
from jax.sharding import Mesh
from jax.sharding import PartitionSpec as P

MEMBERS = 16
NLAT = 320
L = 320
NBANDS = 16
PARTNERS = 4
JJ = MEMBERS + 1
ORDER = ("order_0", "order_1")
ENS = ("ens_0", "ens_1")
DP_ENS = ("dp", "ens_0", "ens_1")
EVERY = ORDER + ENS
EPSILON = 1e-06
WEIGHT_RATIO = 1.0 / 64.0
BF = jnp.bfloat16
F32 = jnp.float32
GROUP = 16
NGROUPS = L // GROUP
WIDE = 384
MIB = 1024 * 1024
VMEM = pl.BlockSpec(memory_space=pltpu.VMEM)
SMEM = pl.BlockSpec(memory_space=pltpu.SMEM)
HBM = pl.BlockSpec(memory_space=pltpu.HBM)


def selections():
    full = np.zeros((NLAT, 640), np.float32)
    half = np.zeros((2, NLAT, WIDE), np.float32)
    for t in range(NLAT):
        full[t, 2 * t : 2 * t + 2] = 1.0
        o, rest = divmod(t, 20)
        h, s = divmod(rest, 10)
        half[h, t, 24 * o + 2 * s : 24 * o + 2 * s + 2] = 1.0
    return full, half


def orderings():
    whole = np.zeros((64, 64), np.float32)
    half = np.zeros((2, 96, 160), np.float32)
    for i in range(2):
        for t in range(4):
            for e in range(8):
                whole[8 * e + 2 * t + i, 16 * t + 2 * e + i] = 1.0
        for t in range(20):
            h, s = divmod(t, 10)
            for p in range(4):
                half[h, 24 * p + 2 * s + i, 8 * t + 2 * p + i] = 1.0
    return whole, half


FULL, HALF = selections()
WHOLE_ORDER, HALF_ORDER = orderings()


def dot(a, b, ca=1, cb=0):
    return lax.dot_general(a, b, (((ca,), (cb,)), ((), ())), preferred_element_type=F32)


def iota(shape, dim):
    return lax.broadcasted_iota(jnp.int32, shape, dim)


def swap_halves(x):
    return pltpu.roll(x, 64, x.ndim - 1)


def split2(x):
    high = x.astype(BF)
    return high, (x - high.astype(F32)).astype(BF)


def split3(x):
    high = x.astype(BF)
    rest = x - high.astype(F32)
    mid = rest.astype(BF)
    return high, mid, (rest - mid.astype(F32)).astype(BF)


STEP = 4


def pack_step(x_ref, whole_ref, half_ref, o_ref):
    def block(rows, columns):
        return x_ref[rows, columns, :].astype(F32).reshape(-1, 128).astype(BF)

    for k in range(STEP):
        for slot in range(2):
            start = 40 * k + 16 * slot
            parts = [block(slice(4 * c, 4 * c + 4), slice(start, start + 16)) for c in range(5)]
            moved = dot(whole_ref[...], jnp.concatenate(parts, axis=1))
            moved = [moved[:, 128 * c : 128 * c + 128].reshape(8, 8, 128) for c in range(5)]
            moved = jnp.concatenate(moved, axis=1).astype(BF)
            o_ref[k, :, 40 * slot : 40 * slot + 40, :] = moved
    parts = [block(slice(0, 20), slice(40 * k + 32, 40 * k + 40)) for k in range(STEP)]
    values = jnp.concatenate(parts, axis=1)
    firsts = dot(half_ref[0], values)
    seconds = dot(half_ref[1], values)
    low = iota((96, 128), 1) < 64
    for k in range(STEP):
        first = firsts[:, 128 * k : 128 * k + 128]
        second = seconds[:, 128 * k : 128 * k + 128]
        real = jnp.where(low, first, swap_halves(second)).astype(BF)
        imaginary = jnp.where(low, swap_halves(first), second).astype(BF)
        for p in range(4):
            o_ref[k, 2 * p, 80:104, :] = real[24 * p : 24 * p + 24]
            o_ref[k, 2 * p + 1, 80:104, :] = imaginary[24 * p : 24 * p + 24]


def unpack_step(y_ref, whole_ref, half_ref, x_ref):
    for k in range(STEP):
        for slot in range(2):
            rows = y_ref[k, :, 40 * slot : 40 * slot + 40, :].astype(F32)
            parts = [rows[:, 8 * c : 8 * c + 8].reshape(64, 128).astype(BF) for c in range(5)]
            moved = dot(whole_ref[...], jnp.concatenate(parts, axis=1))
            moved = [moved[:, 128 * c : 128 * c + 128].reshape(4, 16, 128) for c in range(5)]
            start = 40 * k + 16 * slot
            x_ref[:, start : start + 16, :] = jnp.concatenate(moved, axis=0).astype(BF)
    low = iota((96, 128), 1) < 64
    firsts, seconds = [], []
    for k in range(STEP):
        real, imaginary = [
            jnp.concatenate([y_ref[k, 2 * p + r, 80:104, :].astype(F32) for p in range(4)], axis=0)
            for r in range(2)
        ]
        firsts.append(jnp.where(low, real, swap_halves(imaginary)).astype(BF))
        seconds.append(jnp.where(low, swap_halves(real), imaginary).astype(BF))
    moved = dot(half_ref[0], jnp.concatenate(firsts, axis=1))
    moved = moved + dot(half_ref[1], jnp.concatenate(seconds, axis=1))
    for k in range(STEP):
        part = moved[:, 128 * k : 128 * k + 128].reshape(20, 8, 128).astype(BF)
        x_ref[:, 40 * k + 32 : 40 * k + 40, :] = part


def in_steps(step, place_in, place_out, in_hbm, whole_ref, half_ref, out_hbm, *refs, between=None):
    in_ref, out_ref, in_sem, out_sem = refs

    def load(g):
        return pltpu.make_async_copy(place_in(in_hbm, g), in_ref.at[g], in_sem.at[g])

    def store(g):
        return pltpu.make_async_copy(out_ref.at[g], place_out(out_hbm, g), out_sem.at[g])

    for g in range(16 // STEP):
        load(g).start()

    def one(g, carry):
        load(g).wait()
        step(in_ref.at[g], whole_ref, half_ref, out_ref.at[g])
        store(g).start()
        return carry

    lax.fori_loop(0, 8 // STEP, one, 0)
    if between is not None:
        between()
    lax.fori_loop(8 // STEP, 16 // STEP, one, 0)
    for g in range(16 // STEP):
        store(g).wait()


def unpack_kernel(place_ref, in_hbm, whole_ref, half_ref, *refs):
    r_refs, (out_hbm, weight_hbm), rest = refs[:8], refs[8:10], refs[10:]
    *step_refs, order_ref, weight_ref, r_sem, weight_sem = rest
    loads = [
        pltpu.make_async_copy(
            r_refs[k], order_ref.at[jnp.bitwise_xor(place_ref[1], k)], r_sem.at[k]
        )
        for k in range(8)
    ]
    out = pltpu.make_async_copy(weight_ref, weight_hbm, weight_sem)

    def finish():
        for copy in loads:
            copy.wait()
        for e in range(8):
            weight_ref[:, e, :] = order_ref[e, 0].astype(F32)
            weight_ref[:, 8 + e, :] = order_ref[e, 1].astype(F32)
        for p in range(4):
            both = order_ref[2 * p, 2].astype(F32) + order_ref[2 * p + 1, 2].astype(F32)
            weight_ref[:, 16 + p, :] = both
        out.start()

    for copy in loads:
        copy.start()
    in_steps(
        unpack_step, packed_at, native_at, in_hbm, whole_ref, half_ref, out_hbm, *step_refs,
        between=finish,
    )
    out.wait()


def native_at(ref, g):
    return ref.at[:, pl.ds(40 * STEP * g, 40 * STEP)]


def packed_at(ref, g):
    return ref.at[pl.ds(STEP * g, STEP)]


NATIVE = pltpu.VMEM((16 // STEP, 20, 40 * STEP, 128), BF)
PACKED = pltpu.VMEM((16 // STEP, STEP, 8, 104, 128), BF)
SEMS = [pltpu.SemaphoreType.DMA((16 // STEP,))] * 2


def pack(x):
    return pl.pallas_call(
        functools.partial(in_steps, pack_step, native_at, packed_at),
        out_shape=jax.ShapeDtypeStruct((16, 8, 104, 128), BF),
        in_specs=[HBM, VMEM, VMEM],
        out_specs=HBM,
        scratch_shapes=[NATIVE, PACKED] + SEMS,
        compiler_params=pltpu.CompilerParams(vmem_limit_bytes=63 * MIB),
        name="pack",
    )(x, jnp.asarray(WHOLE_ORDER, BF), jnp.asarray(HALF_ORDER, BF))


def unpack(place, y, received):
    return pl.pallas_call(
        unpack_kernel,
        out_shape=[
            jax.ShapeDtypeStruct((20, 640, 128), BF),
            jax.ShapeDtypeStruct((20, 20, L), F32),
        ],
        in_specs=[SMEM, HBM, VMEM, VMEM] + [HBM] * 8,
        out_specs=[HBM, HBM],
        scratch_shapes=[PACKED, NATIVE]
        + SEMS
        + [
            pltpu.VMEM((8, 3, 20, L), BF),
            pltpu.VMEM((20, 20, L), F32),
            pltpu.SemaphoreType.DMA((8,)),
            pltpu.SemaphoreType.DMA(()),
        ],
        compiler_params=pltpu.CompilerParams(vmem_limit_bytes=63 * MIB),
        name="unpack",
    )(
        place, y, jnp.asarray(WHOLE_ORDER.T, BF), jnp.asarray(HALF_ORDER.transpose(0, 2, 1), BF),
        *received,
    )


def target_kernel(place_ref, t_ref, band_ref, *refs):
    *o_refs, held_ref, sem = refs
    bands = jnp.broadcast_to(band_ref[:, 0:1].astype(F32), (40, 128))
    low = iota((40, 128), 1) < 64
    for k in range(8):
        e = jnp.bitwise_xor(place_ref[1], k)

        def lanes(start):
            return t_ref[:, pl.ds(pl.multiple_of(start, 128), 128)]

        middle = lanes(2048 + 128 * (e // 2)).astype(F32)
        held_ref[k, :, 0:128] = lanes(128 * e)
        held_ref[k, :, 128:256] = lanes(1024 + 128 * e)
        odd = jnp.broadcast_to(e % 2, (40, 128)) == 1
        part = jnp.where(odd, swap_halves(middle), middle)
        held_ref[k, :, 256:384] = jnp.where(low, part, bands).astype(BF)
    copies = [pltpu.make_async_copy(held_ref.at[k], o_refs[k], sem.at[k]) for k in range(8)]
    for copy in copies:
        copy.start()
    for copy in copies:
        copy.wait()


def target_blocks(place, target, bands):
    return pl.pallas_call(
        target_kernel,
        out_shape=[jax.ShapeDtypeStruct((40, WIDE), BF)] * 8,
        in_specs=[SMEM, VMEM, VMEM],
        out_specs=[HBM] * 8,
        scratch_shapes=[pltpu.VMEM((8, 40, WIDE), BF), pltpu.SemaphoreType.DMA((8,))],
        compiler_params=pltpu.CompilerParams(vmem_limit_bytes=63 * MIB),
        name="target_blocks",
    )(place, target, bands)


def own_orders(place_ref):
    ens = place_ref[1]
    return ens, 8 + ens, 16 + ens // 2


def fetches(place_ref, analysis_ref, own_ref, sem):
    return [
        pltpu.make_async_copy(analysis_ref.at[m], own_ref.at[k], sem.at[k])
        for k, m in enumerate(own_orders(place_ref))
    ]


def halves(x):
    return [x[:, 128 * k : 128 * k + 128] for k in range(2)]


STARTS = (0, 40, 80)
COUNTS = (40, 40, 24)


def two_rows_of(rows_ref, g, slot):
    start, count = STARTS[slot], COUNTS[slot]
    parts = [
        rows_ref[:, 2 * g + k, start : start + count, :]
        .astype(F32)
        .reshape(16 * count, 128)
        .astype(BF)
        for k in range(2)
    ]
    return jnp.concatenate(parts, axis=1)


def band_column(target_ref, start, count):
    return target_ref[pl.ds(start, count), 256:384].astype(F32)[:, 64:65]


def prepare_kernel(
    place_ref, analysis_ref, full_ref, half_ref, other_column_ref,
    to_full_ref, to_half_ref, from_full_ref, from_half_ref, to_mixing_ref, own_ref, sem,
):
    copies = fetches(place_ref, analysis_ref, own_ref, sem)
    for copy in copies:
        copy.start()
    row, j = iota((128, 128), 0), iota((128, 128), 1)
    who, other = row & 15, other_column_ref[...]
    pair = (row >= 16) & (row < 80)
    for i in range(MEMBERS):
        own = (j == i).astype(F32)
        value = jnp.where(pair & (who == i), (other == j).astype(F32) - own, 0.0)
        value = value + jnp.where(pair & (other == i), (who == j).astype(F32) - own, 0.0)
        value = value + jnp.where((row < 16) & (who == i), own, 0.0)
        to_mixing_ref[:, 128 * i : 128 * i + 128] = value.astype(BF)
    for copy in copies:
        copy.wait()
    for n in range(4):
        choose = full_ref[...] if n < 2 else half_ref[n - 2]
        own = own_ref[min(n, 2)]
        to_ref = to_full_ref.at[n] if n < 2 else to_half_ref.at[n - 2]
        from_ref = from_full_ref.at[n] if n < 2 else from_half_ref.at[n - 2]
        from_ref[...] = jnp.zeros_like(from_ref)
        spread = dot(own, choose, 0, 0)
        member = iota(spread.shape, 1) % 2
        for i in range(2):
            to_ref[i] = jnp.where(member == i, spread, 0.0).astype(BF)
        spread = dot(choose, own, 0, 0)
        member = iota(spread.shape, 0) % 2
        for i in range(2):
            from_ref[:, WIDE * i : WIDE * i + L] = jnp.where(member == i, spread, 0.0).astype(BF)


def prepare(place, analysis, full, half, other):
    return pl.pallas_call(
        prepare_kernel,
        out_shape=[
            jax.ShapeDtypeStruct((2, 2, L, 640), BF),
            jax.ShapeDtypeStruct((2, 2, L, WIDE), BF),
            jax.ShapeDtypeStruct((2, 640, WIDE + L), BF),
            jax.ShapeDtypeStruct((2, WIDE, WIDE + L), BF),
            jax.ShapeDtypeStruct((128, MEMBERS * 128), BF),
        ],
        in_specs=[SMEM, HBM, VMEM, VMEM, VMEM],
        out_specs=[VMEM] * 5,
        scratch_shapes=[pltpu.VMEM((3, NLAT, L), BF), pltpu.SemaphoreType.DMA((3,))],
        compiler_params=pltpu.CompilerParams(vmem_limit_bytes=63 * MIB),
        name="prepare",
    )(place, analysis, full, half, other)


def block_mask(size, kind, lanes=None):
    shape = (size, lanes or size)
    row, lane = iota(shape, 0), iota(shape, 1)
    same = (row >> 4) == (lane >> 4) if kind == "block" else (row & 15) == (lane & 15)
    return same.astype(F32).astype(BF)


def pick_bands(bands, mask):
    shape = (GROUP, 128)
    one_hot = jnp.broadcast_to(bands, shape) == (iota(shape, 1) & 15).astype(F32)
    tile = jnp.concatenate([one_hot.astype(F32).astype(BF)] * MEMBERS, axis=0)
    return jnp.concatenate([tile, tile], axis=1) * mask


def fold(x):
    x = x[:, :128] + x[:, 128:]
    for shift in (64, 32, 16):
        x = x + pltpu.roll(x, shift, 1)
    return x


def compact(x):
    top, rest = x[:8], x[8:]
    lane = iota((8, 128), 1)
    first = jnp.where(lane < 80, top, pltpu.roll(rest, 80, 1))
    left = pltpu.roll(rest, 80, 1)
    lane = iota((1, 128), 1)
    tails = []
    for n in range(2):
        tail = jnp.zeros((1, 128), F32)
        for r in range(4):
            row = pltpu.roll(left[4 * n + r : 4 * n + r + 1], 32 * r, 1)
            tail = jnp.where((lane >= 32 * r) & (lane < 32 * r + 32), row, tail)
        tails.append(tail)
    return jnp.concatenate([first] + tails, axis=0)


def expand(x):
    first = x[:8]
    lane = iota((8, 128), 1)
    top = jnp.where(lane < 80, first, 0.0)
    rows = []
    for n in range(2):
        for r in range(4):
            rows.append(pltpu.roll(x[8 + n : 9 + n], (48 - 32 * r) % 128, 1))
    rest = jnp.where(lane < 48, pltpu.roll(first, 48, 1), jnp.concatenate(rows, axis=0))
    return jnp.concatenate([top, jnp.where(lane < 80, rest, 0.0)], axis=0)


def spectra_kernel(place_ref, rows_hbm, to_full_hbm, to_half_hbm, other_ref, *refs):
    target_refs = refs[:8]
    stacked_hbm, target_hbm, sums_hbm = refs[8:11]
    to_full_ref, to_half_ref, stacked_ref, target_ref, sums_ref = refs[11:16]
    rows_ref, mask_ref, order_ref, in_sem, rows_sem, target_sem, out_sem = refs[16:]

    def load_rows(g):
        where = pl.ds(2 * g, 2)
        return pltpu.make_async_copy(rows_hbm.at[:, where], rows_ref.at[:, where], rows_sem.at[g])

    load_rows(0).start()
    loads = [
        pltpu.make_async_copy(to_full_hbm.at[n], to_full_ref.at[n], in_sem.at[n]) for n in range(2)
    ]
    loads.append(pltpu.make_async_copy(to_half_hbm, to_half_ref, in_sem.at[2]))
    for k in range(8):
        there = order_ref.at[jnp.bitwise_xor(place_ref[1], k)]
        loads.append(pltpu.make_async_copy(target_refs[k], there, target_sem.at[k]))
    for copy in loads[:3]:
        copy.start()
    for g in range(1, 4):
        load_rows(g).start()
    for copy in loads[3:]:
        copy.start()
    mask_ref[...] = block_mask(256, "block")
    base = place_ref[0] * 20
    orders = [base + m for m in own_orders(place_ref)]
    degree = iota((L, 128), 0)
    low = iota((L, 128), 1) < 64
    keeps = [degree >= orders[0], degree >= orders[1], (degree >= orders[2]) & low]

    def transform(g, carry, operators=None):
        load_rows(g).wait()
        for slot in range(3):
            if operators:
                operators[slot].wait()
            values = two_rows_of(rows_ref, g, slot)
            for i in range(2):
                if slot < 2:
                    parts = halves(dot(to_full_ref[slot, i], values))
                else:
                    parts = halves(dot(to_half_ref[0, i], values))
                    other = halves(dot(to_half_ref[1, i], values))
                    parts = [parts[k] + swap_halves(other[k]) for k in range(2)]
                for k in range(2):
                    stacked_ref[4 * g + 2 * k + i, :, 128 * slot : 128 * slot + 128] = jnp.where(
                        keeps[slot], parts[k], 0.0
                    ).astype(BF)
        store(g).start()
        return carry

    def store(g):
        where = pl.ds(4 * g, 4)
        return pltpu.make_async_copy(stacked_ref.at[where], stacked_hbm.at[where], out_sem.at[g])

    transform(0, 0, loads[:3])
    lax.fori_loop(1, 4, transform, 0)
    for copy in loads[3:]:
        copy.wait()
    target_ref[...] = order_ref[...].astype(F32).reshape(L, WIDE).astype(BF)
    stores = [pltpu.make_async_copy(target_ref, target_hbm, out_sem.at[4])]
    for slot in range(3):
        lanes = slice(128 * slot, 128 * slot + 128)
        observed = jnp.where(keeps[slot], target_ref[:, lanes].astype(F32), 0.0)
        stacked_ref[MEMBERS, :, lanes] = observed.astype(BF)
    last = stacked_hbm.at[MEMBERS]
    stores.append(pltpu.make_async_copy(stacked_ref.at[MEMBERS], last, out_sem.at[5]))
    for copy in stores:
        copy.start()

    size = MEMBERS * GROUP
    same = (iota((JJ * GROUP, size), 0) & 15) == (iota((JJ * GROUP, size), 1) & 15)
    empty = jnp.zeros((32 - JJ, size), F32)

    def gram(g, carry):
        totals, last = carry
        start = pl.multiple_of(g * GROUP, GROUP)
        block = stacked_ref[:, pl.ds(start, GROUP), :].reshape(JJ * GROUP, WIDE)
        products = jnp.where(same, dot(block, block[:size], 1, 1), 0.0)
        products = jnp.sum(products.reshape(JJ, GROUP, size), axis=1)
        parts = split3(jnp.concatenate([products, empty], axis=0))
        bands = band_column(target_ref, start, GROUP)
        moved = dot(jnp.concatenate(parts, axis=0), pick_bands(bands, mask_ref[...]))
        totals = totals + (moved[:32] + moved[32:64] + moved[64:])
        own = block[size:].astype(F32)
        power = jnp.sum(own * own, axis=1, keepdims=True)
        lane = (iota((GROUP, 128), 1) & 15).astype(F32)
        power = jnp.where(jnp.broadcast_to(bands, (GROUP, 128)) == lane, power, 0.0)
        return totals, last + jnp.sum(power, axis=0, keepdims=True)

    start = (jnp.zeros((32, size), F32), jnp.zeros((1, 128), F32))
    totals, last = lax.fori_loop(0, NGROUPS, gram, start, unroll=2)

    grams = totals[:MEMBERS]
    member = iota((MEMBERS, size), 1) >> 4
    diagonal = jnp.where(iota((MEMBERS, size), 0) == member, grams, 0.0)
    powers = jnp.sum(diagonal, axis=0, keepdims=True)
    own_power = fold(diagonal)
    squares = jnp.concatenate([own_power, own_power], axis=1) + powers - 2.0 * grams
    beside = powers + jnp.concatenate([last, last], axis=1) - 2.0 * totals[MEMBERS : MEMBERS + 1]
    beside = jnp.broadcast_to(beside, (MEMBERS, size))
    chosen = fold(jnp.where(iota((MEMBERS, size), 0) == member, beside, 0.0))
    kind = iota((MEMBERS, 128), 1) >> 4
    wanted = jnp.where(kind == 0, chosen, 0.0)
    for p in range(PARTNERS):
        other = other_ref[GROUP * (p + 1) : GROUP * (p + 2), :]
        other = jnp.concatenate([other, other], axis=1)
        chosen = fold(jnp.where(member == other, squares, 0.0))
        wanted = wanted + jnp.where(kind == p + 1, chosen, 0.0)
    wanted = jnp.concatenate([wanted, jnp.zeros((112, 128), F32)], axis=0).T
    squares = wanted[:NBANDS]
    for c in range(1, PARTNERS + 1):
        squares = squares + pltpu.roll(wanted[16 * c : 16 * c + 16], 16 * c, 1)
    sums = compact(squares)
    sums = jnp.concatenate([sums] * 4, axis=0)
    sums_ref[...] = jnp.broadcast_to(sums[None], (32, 40, 128))
    stores.append(pltpu.make_async_copy(sums_ref, sums_hbm, out_sem.at[6]))
    stores[2].start()
    for copy in stores:
        copy.wait()
    for g in range(4):
        store(g).wait()


def spectra(place, rows, to_full, to_half, other, targets):
    return pl.pallas_call(
        spectra_kernel,
        out_shape=[
            jax.ShapeDtypeStruct((JJ, L, WIDE), BF),
            jax.ShapeDtypeStruct((L, WIDE), BF),
            jax.ShapeDtypeStruct((32, 40, 128), F32),
        ],
        in_specs=[SMEM] + [HBM] * 3 + [VMEM] + [HBM] * 8,
        out_specs=[HBM] * 3,
        scratch_shapes=[
            pltpu.VMEM((2, 2, L, 640), BF),
            pltpu.VMEM((2, 2, L, WIDE), BF),
            pltpu.VMEM((JJ, L, WIDE), BF),
            pltpu.VMEM((L, WIDE), BF),
            pltpu.VMEM((32, 40, 128), F32),
            pltpu.VMEM((16, 8, 104, 128), BF),
            pltpu.VMEM((256, 256), BF),
            pltpu.VMEM((8, 40, WIDE), BF),
            pltpu.SemaphoreType.DMA((3,)),
            pltpu.SemaphoreType.DMA((4,)),
            pltpu.SemaphoreType.DMA((8,)),
            pltpu.SemaphoreType.DMA((7,)),
        ],
        compiler_params=pltpu.CompilerParams(vmem_limit_bytes=60 * MIB),
        cost_estimate=pl.CostEstimate(
            flops=10_000_000_000, bytes_accessed=12_000_000, transcendentals=0
        ),
        name="spectra",
    )(place, rows, to_full, to_half, other, *targets)


def gradient_kernel(
    stacked_hbm, target_hbm, sums_ref, cotangent_ref, share_ref, to_mixing_hbm,
    from_full_hbm, from_half_hbm,
    back_ref, grad_hbm, loss_ref,
    stacked_ref, target_ref, to_mixing_ref, from_full_ref, from_half_ref, grad_ref,
    held_ref, member_ref, degree_ref, in_sem, stacked_sem, sem,
):
    loads = [
        pltpu.make_async_copy(there, here, in_sem.at[n])
        for n, (there, here) in enumerate(
            (
                (to_mixing_hbm, to_mixing_ref),
                (target_hbm, target_ref),
                (from_full_hbm, from_full_ref),
                (from_half_hbm, from_half_ref),
            )
        )
    ]
    piece = L // 4

    def load_piece(n):
        where = pl.ds(piece * n, piece)
        return pltpu.make_async_copy(
            stacked_hbm.at[:, where], stacked_ref.at[:, where], stacked_sem.at[n]
        )

    def keep_piece(n):
        where = pl.ds(piece * n, piece)
        return pltpu.make_async_copy(grad_ref.at[:, where], grad_hbm.at[:, where], sem.at[4 + n])

    for copy in loads[:2]:
        copy.start()
    for n in range(4):
        load_piece(n).start()
    for copy in loads[2:]:
        copy.start()
    member_ref[...] = block_mask(256, "block")
    degree_ref[...] = block_mask(256, "inside")
    sums = jnp.sum(sums_ref[...], axis=0)
    sums = sum(sums[10 * n : 10 * n + 10] for n in range(4))
    lane = iota((NBANDS, 128), 1)
    distance = jnp.sqrt(jnp.maximum(expand(sums), 0.0) + EPSILON)
    cotangent = cotangent_ref[...]
    share = share_ref[0:1, :]
    score = jnp.sum(distance * share, axis=1, keepdims=True)
    loss_ref[...] = score * cotangent
    weight = cotangent * (16.0 * MEMBERS * NLAT) * jnp.abs(share) / distance
    beside = jnp.where(lane < MEMBERS, -weight, 0.0)
    loads[0].wait()
    mixing = dot(jnp.concatenate(split3(weight), axis=0), to_mixing_ref[...])
    mixing = mixing[:16] + mixing[16:32] + mixing[32:]
    mixing = [mixing[:, 128 * i : 128 * i + 128] for i in range(MEMBERS)]

    size = MEMBERS * GROUP
    widen = (iota((128, size), 0) == (iota((128, size), 1) >> 4)).astype(F32).astype(BF)
    mix_high, mix_low = split2(jnp.concatenate(mixing, axis=0))
    mix_high = dot(mix_high, widen).astype(BF)
    mix_low = dot(mix_low, widen).astype(BF)
    beside_both = jnp.concatenate(
        [part.astype(F32) for part in split2(beside)] + [jnp.zeros((96, 128), F32)], axis=0
    ).astype(BF)
    band_of_lane = (iota((GROUP, 128), 1) & 15).astype(F32)

    def mix(g, carry):
        start = pl.multiple_of(g * GROUP, GROUP)
        bands = band_column(target_ref, start, GROUP)
        pick = pick_bands(bands, member_ref[...])
        degree = degree_ref[...]
        high = dot(pick, mix_high).astype(BF) * degree
        low = dot(pick, mix_low).astype(BF) * degree
        one_hot = (jnp.broadcast_to(bands, (GROUP, 128)) == band_of_lane).astype(F32).astype(BF)
        weights = dot(one_hot, beside_both)
        weights = jnp.concatenate(
            [jnp.broadcast_to(weights[:, i : i + 1], (GROUP, 128)) for i in range(MEMBERS)], axis=0
        )
        block = stacked_ref[0:MEMBERS, pl.ds(start, GROUP), :].reshape(size, WIDE)
        own = stacked_ref[MEMBERS, pl.ds(start, GROUP), :].astype(F32)
        grad = dot(high, block) + dot(low, block)
        for slot in range(3):
            lanes = slice(128 * slot, 128 * slot + 128)
            part = grad[:, lanes] + weights * jnp.concatenate([own[:, lanes]] * MEMBERS, axis=0)
            grad_ref[:, pl.ds(start, GROUP), lanes] = part.astype(BF).reshape(MEMBERS, GROUP, 128)
        return carry

    loads[1].wait()
    for n in range(4):
        load_piece(n).wait()
        lax.fori_loop(5 * n, 5 * n + 5, mix, 0, unroll=5)
        keep_piece(n).start()
    for copy in loads[2:]:
        copy.wait()
    def inverse(g, carry):
        for slot in range(3):
            grads = [jnp.concatenate(grads_of(grad_ref, g, i, slot), axis=1) for i in range(2)]
            grads = jnp.concatenate([grads[0], jnp.zeros((WIDE - L, 256), BF), grads[1]], axis=0)
            parts = halves(dot(from_full_ref[slot] if slot < 2 else from_half_ref[0], grads))
            if slot == 2:
                other = halves(dot(from_half_ref[1], grads))
                parts = [parts[k] + swap_halves(other[k]) for k in range(2)]
            start, count = STARTS[slot], COUNTS[slot]
            for k in range(2):
                part = parts[k].reshape(16, count, 128).astype(BF)
                held_ref[:, 2 * g + k, start : start + count, :] = part
        send(g).start()
        return carry

    def send(g):
        where = pl.ds(2 * g, 2)
        return pltpu.make_async_copy(held_ref.at[:, where], back_ref.at[:, where], sem.at[g])

    lax.fori_loop(0, 4, inverse, 0)
    for g in range(4):
        send(g).wait()
        keep_piece(g).wait()


def grads_of(grad_ref, g, i, slot):
    lanes = slice(128 * slot, 128 * slot + 128)
    return [grad_ref[4 * g + 2 * k + i, :, lanes] for k in range(2)]


def gradient(stacked, target, sums, cotangent, share, to_mixing, from_full, from_half):
    return pl.pallas_call(
        gradient_kernel,
        out_shape=[
            jax.ShapeDtypeStruct((16, 8, 104, 128), BF),
            jax.ShapeDtypeStruct((MEMBERS, L, WIDE), BF),
            jax.ShapeDtypeStruct((NBANDS, 128), F32),
        ],
        in_specs=[HBM, HBM, VMEM, VMEM, VMEM, HBM, HBM, HBM],
        out_specs=[HBM, HBM, VMEM],
        scratch_shapes=[
            pltpu.VMEM((JJ, L, WIDE), BF),
            pltpu.VMEM((L, WIDE), BF),
            pltpu.VMEM((128, MEMBERS * 128), BF),
            pltpu.VMEM((2, 640, WIDE + L), BF),
            pltpu.VMEM((2, WIDE, WIDE + L), BF),
            pltpu.VMEM((MEMBERS, L, WIDE), BF),
            pltpu.VMEM((16, 8, 104, 128), BF),
            pltpu.VMEM((256, 256), BF),
            pltpu.VMEM((256, 256), BF),
            pltpu.SemaphoreType.DMA((4,)),
            pltpu.SemaphoreType.DMA((4,)),
            pltpu.SemaphoreType.DMA((8,)),
        ],
        compiler_params=pltpu.CompilerParams(vmem_limit_bytes=63 * MIB),
        cost_estimate=pl.CostEstimate(
            flops=10_000_000_000, bytes_accessed=12_000_000, transcendentals=0
        ),
        name="gradient",
    )(stacked, target, sums, cotangent, share, to_mixing, from_full, from_half)


def weight_kernel(
    place_ref, rows_ref, grad_ref, full_ref, half_ref, weight_ref, full_sum_ref, half_sum_ref
):
    full_sum_ref[...] = jnp.zeros_like(full_sum_ref)
    half_sum_ref[...] = jnp.zeros_like(half_sum_ref)

    def step(g, carry):
        for slot in range(3):
            values = two_rows_of(rows_ref, g, slot)
            member = iota((values.shape[0], L), 0) % 2
            sides = [[grads_of(grad_ref, g, i, slot) for i in range(2)]]
            if slot == 2:
                sides.append(
                    [[swap_halves(x.astype(F32)).astype(BF) for x in pair] for pair in sides[0]]
                )
            for h, side in enumerate(sides):
                grads = [jnp.concatenate(side[i], axis=1) for i in range(2)]
                terms = jnp.where(
                    member == 0, dot(values, grads[0], 1, 1), dot(values, grads[1], 1, 1)
                )
                if slot < 2:
                    full_sum_ref[slot] += terms
                else:
                    half_sum_ref[h] += terms
        return carry

    lax.fori_loop(0, 4, step, 0)
    for slot in range(3):
        if slot < 2:
            parts = split2(full_sum_ref[slot])
            weight = dot(full_ref[...], parts[0]) + dot(full_ref[...], parts[1])
        else:
            weight = jnp.zeros((NLAT, L), F32)
            for h in range(2):
                parts = split2(half_sum_ref[h])
                weight = weight + dot(half_ref[h], parts[0]) + dot(half_ref[h], parts[1])
        weight = weight * WEIGHT_RATIO
        for c in range(16):
            other = jnp.bitwise_xor(place_ref[2], c // 8)
            step_to = jnp.bitwise_xor(place_ref[1], c % 8)
            weight_ref[other, step_to, slot] = weight[20 * c : 20 * c + 20].astype(BF)


def weights(place, rows, grads, full, half):
    return pl.pallas_call(
        weight_kernel,
        out_shape=jax.ShapeDtypeStruct((2, 8, 3, 20, L), BF),
        in_specs=[SMEM] + [VMEM] * 4,
        out_specs=VMEM,
        scratch_shapes=[
            pltpu.VMEM((2, 640, L), F32),
            pltpu.VMEM((2, WIDE, L), F32),
        ],
        compiler_params=pltpu.CompilerParams(vmem_limit_bytes=63 * MIB),
        cost_estimate=pl.CostEstimate(
            flops=5_000_000_000, bytes_accessed=8_000_000, transcendentals=0
        ),
        name="weights",
    )(place, rows, grads, full, half)


def exchange(x, axes):
    return lax.all_to_all(x, axes, split_axis=0, concat_axis=0, tiled=True)


def swap(blocks, kinds):
    return [lax.ppermute(blocks[k], ENS, [(e, e ^ k) for e in range(8)]) for k in kinds]


def travel(x):
    moved = exchange(x.reshape(128, 52, 2, 128), EVERY)
    return moved.reshape(16, 8, 104, 128)


def body(fourier, analysis, target, band_ids, partners, band_cotangent):
    place = jnp.stack([lax.axis_index(ORDER), lax.axis_index(ENS), lax.axis_index("dp")])
    place = place.astype(jnp.int32)
    full = jnp.asarray(FULL, BF)
    half = jnp.asarray(HALF, BF)
    by_order = jnp.transpose(analysis, (1, 0, 2))
    native = jnp.transpose(fourier[0].reshape(2, 20, 320, 128), (1, 2, 0, 3)).reshape(20, 640, 128)
    packed = pack(native)
    target_in, partners, full, cotangent, packed = lax.optimization_barrier(
        (target[0], partners, full, band_cotangent, packed)
    )
    rows = travel(packed)
    blocks = target_blocks(place, target_in, band_ids)
    targets = [blocks[0]] + swap(blocks, range(1, 8))
    other = jnp.concatenate(
        [jnp.full((16,), MEMBERS, jnp.int32), partners.T.reshape(64), jnp.zeros((48,), jnp.int32)]
    )
    other = jnp.broadcast_to(other[:, None], (128, 128))
    cotangent = lax.dynamic_slice_in_dim(cotangent, lax.axis_index("dp"), 1, 0)[0]
    cotangent = jnp.broadcast_to(cotangent[:, None], (NBANDS, 128))
    cotangent, other = lax.optimization_barrier((cotangent, other))
    to_full, to_half, from_full, from_half, to_mixing = prepare(
        place, by_order, full, half, other
    )
    share = np.zeros((8, 128), np.float32)
    share[:, :16] = 1.0 / MEMBERS
    share[:, 16:80] = -1.0 / (2.0 * MEMBERS * PARTNERS)
    stacked, observed, sums = spectra(place, rows, to_full, to_half, other, targets)
    sums = exchange(sums.reshape(128, 5, 2, 128), EVERY).reshape(32, 40, 128)
    back, grads, loss = gradient(
        stacked, observed, sums, cotangent, jnp.asarray(share), to_mixing, from_full, from_half
    )
    returned = travel(back)
    loss = loss[:, 0]
    loss_bands = loss + lax.ppermute(loss, "dp", [(0, 1), (1, 0)])
    weight = weights(place, rows, grads, full, half)
    beside = lax.ppermute(weight[1], "dp", [(0, 1), (1, 0)])
    weight = (weight[0].astype(F32) + beside.astype(F32)).astype(BF)
    near = swap([weight[k] for k in range(8)], (1, 2))
    *far, near[0], near[1] = lax.optimization_barrier((*[weight[k] for k in range(3, 8)], *near))
    far = swap([weight[0]] * 3 + far, range(3, 8))
    native_grad, grad_analysis = unpack(place, returned, [weight[0]] + near + far)
    native_grad = native_grad.reshape(20, 320, 2, 128)
    grad_fourier = jnp.transpose(native_grad, (2, 0, 1, 3)).reshape(1, 2, 20, 40960)
    return (grad_fourier, grad_analysis, loss_bands)


def solution(mesh):
    torus = Mesh(
        mesh.devices.reshape(mesh.shape["dp"], 4, 4, 2, 4),
        ("dp", "order_0", "order_1", "ens_0", "ens_1"),
    )
    in_specs = (
        P("dp", ENS, ORDER, None),
        P(None, ORDER, None),
        P("dp", ENS, ORDER),
        P(ENS, ORDER),
        P(),
        P(),
    )
    out_specs = (P("dp", ENS, ORDER, None), P(DP_ENS, ORDER, None), P())
    return jax.shard_map(body, mesh=torus, in_specs=in_specs, out_specs=out_specs, check_vma=False)
```

```python
import functools

import jax
import jax.numpy as jnp
import numpy as np
from jax import lax
from jax.experimental import pallas as pl
from jax.experimental.pallas import tpu as pltpu
from jax.sharding import Mesh
from jax.sharding import PartitionSpec as P

MEMBERS = 16
NLAT = 320
L = 320
NBANDS = 16
PARTNERS = 4
JJ = MEMBERS + 1
ORDER = ("order_0", "order_1")
ENS = ("ens_0", "ens_1")
DP_ENS = ("dp", "ens_0", "ens_1")
EVERY = ORDER + ENS
EPSILON = 1e-06
WEIGHT_RATIO = 1.0 / 64.0
BF = jnp.bfloat16
F32 = jnp.float32
GROUP = 16
NGROUPS = L // GROUP
WIDE = 384
MIB = 1024 * 1024
VMEM = pl.BlockSpec(memory_space=pltpu.VMEM)
SMEM = pl.BlockSpec(memory_space=pltpu.SMEM)
HBM = pl.BlockSpec(memory_space=pltpu.HBM)


def selections():
    full = np.zeros((NLAT, 640), np.float32)
    half = np.zeros((2, NLAT, WIDE), np.float32)
    for t in range(NLAT):
        full[t, 2 * t : 2 * t + 2] = 1.0
        o, rest = divmod(t, 20)
        h, s = divmod(rest, 10)
        half[h, t, 24 * o + 2 * s : 24 * o + 2 * s + 2] = 1.0
    return full, half


def orderings():
    whole = np.zeros((64, 64), np.float32)
    half = np.zeros((2, 96, 160), np.float32)
    for i in range(2):
        for t in range(4):
            for e in range(8):
                whole[8 * e + 2 * t + i, 16 * t + 2 * e + i] = 1.0
        for t in range(20):
            h, s = divmod(t, 10)
            for p in range(4):
                half[h, 24 * p + 2 * s + i, 8 * t + 2 * p + i] = 1.0
    return whole, half


FULL, HALF = selections()
WHOLE_ORDER, HALF_ORDER = orderings()


def dot(a, b, ca=1, cb=0):
    return lax.dot_general(a, b, (((ca,), (cb,)), ((), ())), preferred_element_type=F32)


def iota(shape, dim):
    return lax.broadcasted_iota(jnp.int32, shape, dim)


def swap_halves(x):
    return pltpu.roll(x, 64, x.ndim - 1)


def split2(x):
    high = x.astype(BF)
    return high, (x - high.astype(F32)).astype(BF)


def split3(x):
    high = x.astype(BF)
    rest = x - high.astype(F32)
    mid = rest.astype(BF)
    return high, mid, (rest - mid.astype(F32)).astype(BF)


STEP = 4


def pack_step(x_ref, whole_ref, half_ref, o_ref):
    def block(rows, columns):
        return x_ref[rows, columns, :].astype(F32).reshape(-1, 128).astype(BF)

    for k in range(STEP):
        for slot in range(2):
            start = 40 * k + 16 * slot
            parts = [block(slice(4 * c, 4 * c + 4), slice(start, start + 16)) for c in range(5)]
            moved = dot(whole_ref[...], jnp.concatenate(parts, axis=1))
            moved = [moved[:, 128 * c : 128 * c + 128].reshape(8, 8, 128) for c in range(5)]
            moved = jnp.concatenate(moved, axis=1).astype(BF)
            o_ref[k, :, 40 * slot : 40 * slot + 40, :] = moved
    parts = [block(slice(0, 20), slice(40 * k + 32, 40 * k + 40)) for k in range(STEP)]
    values = jnp.concatenate(parts, axis=1)
    firsts = dot(half_ref[0], values)
    seconds = dot(half_ref[1], values)
    low = iota((96, 128), 1) < 64
    for k in range(STEP):
        first = firsts[:, 128 * k : 128 * k + 128]
        second = seconds[:, 128 * k : 128 * k + 128]
        real = jnp.where(low, first, swap_halves(second)).astype(BF)
        imaginary = jnp.where(low, swap_halves(first), second).astype(BF)
        for p in range(4):
            o_ref[k, 2 * p, 80:104, :] = real[24 * p : 24 * p + 24]
            o_ref[k, 2 * p + 1, 80:104, :] = imaginary[24 * p : 24 * p + 24]


def unpack_step(y_ref, whole_ref, half_ref, x_ref):
    for k in range(STEP):
        for slot in range(2):
            rows = y_ref[k, :, 40 * slot : 40 * slot + 40, :].astype(F32)
            parts = [rows[:, 8 * c : 8 * c + 8].reshape(64, 128).astype(BF) for c in range(5)]
            moved = dot(whole_ref[...], jnp.concatenate(parts, axis=1))
            moved = [moved[:, 128 * c : 128 * c + 128].reshape(4, 16, 128) for c in range(5)]
            start = 40 * k + 16 * slot
            x_ref[:, start : start + 16, :] = jnp.concatenate(moved, axis=0).astype(BF)
    low = iota((96, 128), 1) < 64
    firsts, seconds = [], []
    for k in range(STEP):
        real, imaginary = [
            jnp.concatenate([y_ref[k, 2 * p + r, 80:104, :].astype(F32) for p in range(4)], axis=0)
            for r in range(2)
        ]
        firsts.append(jnp.where(low, real, swap_halves(imaginary)).astype(BF))
        seconds.append(jnp.where(low, swap_halves(real), imaginary).astype(BF))
    moved = dot(half_ref[0], jnp.concatenate(firsts, axis=1))
    moved = moved + dot(half_ref[1], jnp.concatenate(seconds, axis=1))
    for k in range(STEP):
        part = moved[:, 128 * k : 128 * k + 128].reshape(20, 8, 128).astype(BF)
        x_ref[:, 40 * k + 32 : 40 * k + 40, :] = part


def in_steps(step, place_in, place_out, in_hbm, whole_ref, half_ref, out_hbm, *refs, between=None):
    in_ref, out_ref, in_sem, out_sem = refs

    def load(g):
        return pltpu.make_async_copy(place_in(in_hbm, g), in_ref.at[g], in_sem.at[g])

    def store(g):
        return pltpu.make_async_copy(out_ref.at[g], place_out(out_hbm, g), out_sem.at[g])

    for g in range(16 // STEP):
        load(g).start()

    def one(g, carry):
        load(g).wait()
        step(in_ref.at[g], whole_ref, half_ref, out_ref.at[g])
        store(g).start()
        return carry

    lax.fori_loop(0, 8 // STEP, one, 0)
    if between is not None:
        between()
    lax.fori_loop(8 // STEP, 16 // STEP, one, 0)
    for g in range(16 // STEP):
        store(g).wait()


def unpack_kernel(place_ref, in_hbm, whole_ref, half_ref, *refs):
    r_refs, (out_hbm, weight_hbm), rest = refs[:8], refs[8:10], refs[10:]
    *step_refs, order_ref, weight_ref, r_sem, weight_sem = rest
    loads = [
        pltpu.make_async_copy(
            r_refs[k], order_ref.at[jnp.bitwise_xor(place_ref[1], k)], r_sem.at[k]
        )
        for k in range(8)
    ]
    out = pltpu.make_async_copy(weight_ref, weight_hbm, weight_sem)

    def finish():
        for copy in loads:
            copy.wait()
        for e in range(8):
            weight_ref[:, e, :] = order_ref[e, 0].astype(F32)
            weight_ref[:, 8 + e, :] = order_ref[e, 1].astype(F32)
        for p in range(4):
            both = order_ref[2 * p, 2].astype(F32) + order_ref[2 * p + 1, 2].astype(F32)
            weight_ref[:, 16 + p, :] = both
        out.start()

    for copy in loads:
        copy.start()
    in_steps(
        unpack_step, packed_at, native_at, in_hbm, whole_ref, half_ref, out_hbm, *step_refs,
        between=finish,
    )
    out.wait()


def native_at(ref, g):
    return ref.at[:, pl.ds(40 * STEP * g, 40 * STEP)]


def packed_at(ref, g):
    return ref.at[pl.ds(STEP * g, STEP)]


NATIVE = pltpu.VMEM((16 // STEP, 20, 40 * STEP, 128), BF)
PACKED = pltpu.VMEM((16 // STEP, STEP, 8, 104, 128), BF)
SEMS = [pltpu.SemaphoreType.DMA((16 // STEP,))] * 2


def pack(x):
    return pl.pallas_call(
        functools.partial(in_steps, pack_step, native_at, packed_at),
        out_shape=jax.ShapeDtypeStruct((16, 8, 104, 128), BF),
        in_specs=[HBM, VMEM, VMEM],
        out_specs=HBM,
        scratch_shapes=[NATIVE, PACKED] + SEMS,
        compiler_params=pltpu.CompilerParams(vmem_limit_bytes=63 * MIB),
        name="pack",
    )(x, jnp.asarray(WHOLE_ORDER, BF), jnp.asarray(HALF_ORDER, BF))


def unpack(place, y, received):
    return pl.pallas_call(
        unpack_kernel,
        out_shape=[
            jax.ShapeDtypeStruct((20, 640, 128), BF),
            jax.ShapeDtypeStruct((20, 20, L), F32),
        ],
        in_specs=[SMEM, HBM, VMEM, VMEM] + [HBM] * 8,
        out_specs=[HBM, HBM],
        scratch_shapes=[PACKED, NATIVE]
        + SEMS
        + [
            pltpu.VMEM((8, 3, 20, L), BF),
            pltpu.VMEM((20, 20, L), F32),
            pltpu.SemaphoreType.DMA((8,)),
            pltpu.SemaphoreType.DMA(()),
        ],
        compiler_params=pltpu.CompilerParams(vmem_limit_bytes=63 * MIB),
        name="unpack",
    )(
        place, y, jnp.asarray(WHOLE_ORDER.T, BF), jnp.asarray(HALF_ORDER.transpose(0, 2, 1), BF),
        *received,
    )


def target_kernel(place_ref, t_ref, band_ref, *refs):
    *o_refs, held_ref, sem = refs
    bands = jnp.broadcast_to(band_ref[:, 0:1].astype(F32), (40, 128))
    low = iota((40, 128), 1) < 64
    for k in range(8):
        e = jnp.bitwise_xor(place_ref[1], k)

        def lanes(start):
            return t_ref[:, pl.ds(pl.multiple_of(start, 128), 128)]

        middle = lanes(2048 + 128 * (e // 2)).astype(F32)
        held_ref[k, :, 0:128] = lanes(128 * e)
        held_ref[k, :, 128:256] = lanes(1024 + 128 * e)
        odd = jnp.broadcast_to(e % 2, (40, 128)) == 1
        part = jnp.where(odd, swap_halves(middle), middle)
        held_ref[k, :, 256:384] = jnp.where(low, part, bands).astype(BF)
    copies = [pltpu.make_async_copy(held_ref.at[k], o_refs[k], sem.at[k]) for k in range(8)]
    for copy in copies:
        copy.start()
    for copy in copies:
        copy.wait()


def target_blocks(place, target, bands):
    return pl.pallas_call(
        target_kernel,
        out_shape=[jax.ShapeDtypeStruct((40, WIDE), BF)] * 8,
        in_specs=[SMEM, VMEM, VMEM],
        out_specs=[HBM] * 8,
        scratch_shapes=[pltpu.VMEM((8, 40, WIDE), BF), pltpu.SemaphoreType.DMA((8,))],
        compiler_params=pltpu.CompilerParams(vmem_limit_bytes=63 * MIB),
        name="target_blocks",
    )(place, target, bands)


def own_orders(place_ref):
    ens = place_ref[1]
    return ens, 8 + ens, 16 + ens // 2


def fetches(place_ref, analysis_ref, own_ref, sem):
    return [
        pltpu.make_async_copy(analysis_ref.at[m], own_ref.at[k], sem.at[k])
        for k, m in enumerate(own_orders(place_ref))
    ]


def halves(x):
    return [x[:, 128 * k : 128 * k + 128] for k in range(2)]


STARTS = (0, 40, 80)
COUNTS = (40, 40, 24)


def two_rows_of(rows_ref, g, slot):
    start, count = STARTS[slot], COUNTS[slot]
    parts = [
        rows_ref[:, 2 * g + k, start : start + count, :]
        .astype(F32)
        .reshape(16 * count, 128)
        .astype(BF)
        for k in range(2)
    ]
    return jnp.concatenate(parts, axis=1)


def band_column(target_ref, start, count):
    return target_ref[pl.ds(start, count), 256:384].astype(F32)[:, 64:65]


def prepare_kernel(
    place_ref, analysis_ref, full_ref, half_ref, other_column_ref,
    to_full_ref, to_half_ref, from_full_ref, from_half_ref, to_mixing_ref, own_ref, sem,
):
    copies = fetches(place_ref, analysis_ref, own_ref, sem)
    for copy in copies:
        copy.start()
    row, j = iota((128, 128), 0), iota((128, 128), 1)
    who, other = row & 15, other_column_ref[...]
    pair = (row >= 16) & (row < 80)
    for i in range(MEMBERS):
        own = (j == i).astype(F32)
        value = jnp.where(pair & (who == i), (other == j).astype(F32) - own, 0.0)
        value = value + jnp.where(pair & (other == i), (who == j).astype(F32) - own, 0.0)
        value = value + jnp.where((row < 16) & (who == i), own, 0.0)
        to_mixing_ref[:, 128 * i : 128 * i + 128] = value.astype(BF)
    for copy in copies:
        copy.wait()
    for n in range(4):
        choose = full_ref[...] if n < 2 else half_ref[n - 2]
        own = own_ref[min(n, 2)]
        to_ref = to_full_ref.at[n] if n < 2 else to_half_ref.at[n - 2]
        from_ref = from_full_ref.at[n] if n < 2 else from_half_ref.at[n - 2]
        from_ref[...] = jnp.zeros_like(from_ref)
        spread = dot(own, choose, 0, 0)
        member = iota(spread.shape, 1) % 2
        for i in range(2):
            to_ref[i] = jnp.where(member == i, spread, 0.0).astype(BF)
        spread = dot(choose, own, 0, 0)
        member = iota(spread.shape, 0) % 2
        for i in range(2):
            from_ref[:, WIDE * i : WIDE * i + L] = jnp.where(member == i, spread, 0.0).astype(BF)


def prepare(place, analysis, full, half, other):
    return pl.pallas_call(
        prepare_kernel,
        out_shape=[
            jax.ShapeDtypeStruct((2, 2, L, 640), BF),
            jax.ShapeDtypeStruct((2, 2, L, WIDE), BF),
            jax.ShapeDtypeStruct((2, 640, WIDE + L), BF),
            jax.ShapeDtypeStruct((2, WIDE, WIDE + L), BF),
            jax.ShapeDtypeStruct((128, MEMBERS * 128), BF),
        ],
        in_specs=[SMEM, HBM, VMEM, VMEM, VMEM],
        out_specs=[VMEM] * 5,
        scratch_shapes=[pltpu.VMEM((3, NLAT, L), BF), pltpu.SemaphoreType.DMA((3,))],
        compiler_params=pltpu.CompilerParams(vmem_limit_bytes=63 * MIB),
        name="prepare",
    )(place, analysis, full, half, other)


def block_mask(size, kind, lanes=None):
    shape = (size, lanes or size)
    row, lane = iota(shape, 0), iota(shape, 1)
    same = (row >> 4) == (lane >> 4) if kind == "block" else (row & 15) == (lane & 15)
    return same.astype(F32).astype(BF)


def pick_bands(bands, mask):
    shape = (GROUP, 128)
    one_hot = jnp.broadcast_to(bands, shape) == (iota(shape, 1) & 15).astype(F32)
    tile = jnp.concatenate([one_hot.astype(F32).astype(BF)] * MEMBERS, axis=0)
    return jnp.concatenate([tile, tile], axis=1) * mask


def fold(x):
    x = x[:, :128] + x[:, 128:]
    for shift in (64, 32, 16):
        x = x + pltpu.roll(x, shift, 1)
    return x


def compact(x):
    top, rest = x[:8], x[8:]
    lane = iota((8, 128), 1)
    first = jnp.where(lane < 80, top, pltpu.roll(rest, 80, 1))
    left = pltpu.roll(rest, 80, 1)
    lane = iota((1, 128), 1)
    tails = []
    for n in range(2):
        tail = jnp.zeros((1, 128), F32)
        for r in range(4):
            row = pltpu.roll(left[4 * n + r : 4 * n + r + 1], 32 * r, 1)
            tail = jnp.where((lane >= 32 * r) & (lane < 32 * r + 32), row, tail)
        tails.append(tail)
    return jnp.concatenate([first] + tails, axis=0)


def expand(x):
    first = x[:8]
    lane = iota((8, 128), 1)
    top = jnp.where(lane < 80, first, 0.0)
    rows = []
    for n in range(2):
        for r in range(4):
            rows.append(pltpu.roll(x[8 + n : 9 + n], (48 - 32 * r) % 128, 1))
    rest = jnp.where(lane < 48, pltpu.roll(first, 48, 1), jnp.concatenate(rows, axis=0))
    return jnp.concatenate([top, jnp.where(lane < 80, rest, 0.0)], axis=0)


def spectra_kernel(place_ref, rows_hbm, to_full_hbm, to_half_hbm, other_ref, *refs):
    target_refs = refs[:8]
    stacked_hbm, target_hbm, sums_hbm = refs[8:11]
    to_full_ref, to_half_ref, stacked_ref, target_ref, sums_ref = refs[11:16]
    rows_ref, mask_ref, order_ref, in_sem, rows_sem, target_sem, out_sem = refs[16:]

    def load_rows(g):
        where = pl.ds(2 * g, 2)
        return pltpu.make_async_copy(rows_hbm.at[:, where], rows_ref.at[:, where], rows_sem.at[g])

    load_rows(0).start()
    loads = [
        pltpu.make_async_copy(to_full_hbm.at[n], to_full_ref.at[n], in_sem.at[n]) for n in range(2)
    ]
    loads.append(pltpu.make_async_copy(to_half_hbm, to_half_ref, in_sem.at[2]))
    for k in range(8):
        there = order_ref.at[jnp.bitwise_xor(place_ref[1], k)]
        loads.append(pltpu.make_async_copy(target_refs[k], there, target_sem.at[k]))
    for copy in loads[:3]:
        copy.start()
    for g in range(1, 4):
        load_rows(g).start()
    for copy in loads[3:]:
        copy.start()
    mask_ref[...] = block_mask(256, "block")
    base = place_ref[0] * 20
    orders = [base + m for m in own_orders(place_ref)]
    degree = iota((L, 128), 0)
    low = iota((L, 128), 1) < 64
    keeps = [degree >= orders[0], degree >= orders[1], (degree >= orders[2]) & low]

    def transform(g, carry, operators=None):
        load_rows(g).wait()
        for slot in range(3):
            if operators:
                operators[slot].wait()
            values = two_rows_of(rows_ref, g, slot)
            for i in range(2):
                if slot < 2:
                    parts = halves(dot(to_full_ref[slot, i], values))
                else:
                    parts = halves(dot(to_half_ref[0, i], values))
                    other = halves(dot(to_half_ref[1, i], values))
                    parts = [parts[k] + swap_halves(other[k]) for k in range(2)]
                for k in range(2):
                    stacked_ref[4 * g + 2 * k + i, :, 128 * slot : 128 * slot + 128] = jnp.where(
                        keeps[slot], parts[k], 0.0
                    ).astype(BF)
        store(g).start()
        return carry

    def store(g):
        where = pl.ds(4 * g, 4)
        return pltpu.make_async_copy(stacked_ref.at[where], stacked_hbm.at[where], out_sem.at[g])

    transform(0, 0, loads[:3])
    lax.fori_loop(1, 4, transform, 0)
    for copy in loads[3:]:
        copy.wait()
    target_ref[...] = order_ref[...].astype(F32).reshape(L, WIDE).astype(BF)
    stores = [pltpu.make_async_copy(target_ref, target_hbm, out_sem.at[4])]
    for slot in range(3):
        lanes = slice(128 * slot, 128 * slot + 128)
        observed = jnp.where(keeps[slot], target_ref[:, lanes].astype(F32), 0.0)
        stacked_ref[MEMBERS, :, lanes] = observed.astype(BF)
    last = stacked_hbm.at[MEMBERS]
    stores.append(pltpu.make_async_copy(stacked_ref.at[MEMBERS], last, out_sem.at[5]))
    for copy in stores:
        copy.start()

    size = MEMBERS * GROUP
    same = (iota((JJ * GROUP, size), 0) & 15) == (iota((JJ * GROUP, size), 1) & 15)
    empty = jnp.zeros((32 - JJ, size), F32)

    def gram(g, carry):
        totals, last = carry
        start = pl.multiple_of(g * GROUP, GROUP)
        block = stacked_ref[:, pl.ds(start, GROUP), :].reshape(JJ * GROUP, WIDE)
        products = jnp.where(same, dot(block, block[:size], 1, 1), 0.0)
        products = jnp.sum(products.reshape(JJ, GROUP, size), axis=1)
        parts = split3(jnp.concatenate([products, empty], axis=0))
        bands = band_column(target_ref, start, GROUP)
        moved = dot(jnp.concatenate(parts, axis=0), pick_bands(bands, mask_ref[...]))
        totals = totals + (moved[:32] + moved[32:64] + moved[64:])
        own = block[size:].astype(F32)
        power = jnp.sum(own * own, axis=1, keepdims=True)
        lane = (iota((GROUP, 128), 1) & 15).astype(F32)
        power = jnp.where(jnp.broadcast_to(bands, (GROUP, 128)) == lane, power, 0.0)
        return totals, last + jnp.sum(power, axis=0, keepdims=True)

    start = (jnp.zeros((32, size), F32), jnp.zeros((1, 128), F32))
    totals, last = lax.fori_loop(0, NGROUPS, gram, start, unroll=2)

    grams = totals[:MEMBERS]
    member = iota((MEMBERS, size), 1) >> 4
    diagonal = jnp.where(iota((MEMBERS, size), 0) == member, grams, 0.0)
    powers = jnp.sum(diagonal, axis=0, keepdims=True)
    own_power = fold(diagonal)
    squares = jnp.concatenate([own_power, own_power], axis=1) + powers - 2.0 * grams
    beside = powers + jnp.concatenate([last, last], axis=1) - 2.0 * totals[MEMBERS : MEMBERS + 1]
    beside = jnp.broadcast_to(beside, (MEMBERS, size))
    chosen = fold(jnp.where(iota((MEMBERS, size), 0) == member, beside, 0.0))
    kind = iota((MEMBERS, 128), 1) >> 4
    wanted = jnp.where(kind == 0, chosen, 0.0)
    for p in range(PARTNERS):
        other = other_ref[GROUP * (p + 1) : GROUP * (p + 2), :]
        other = jnp.concatenate([other, other], axis=1)
        chosen = fold(jnp.where(member == other, squares, 0.0))
        wanted = wanted + jnp.where(kind == p + 1, chosen, 0.0)
    wanted = jnp.concatenate([wanted, jnp.zeros((112, 128), F32)], axis=0).T
    squares = wanted[:NBANDS]
    for c in range(1, PARTNERS + 1):
        squares = squares + pltpu.roll(wanted[16 * c : 16 * c + 16], 16 * c, 1)
    sums = compact(squares)
    sums = jnp.concatenate([sums] * 4, axis=0)
    sums_ref[...] = jnp.broadcast_to(sums[None], (32, 40, 128))
    stores.append(pltpu.make_async_copy(sums_ref, sums_hbm, out_sem.at[6]))
    stores[2].start()
    for copy in stores:
        copy.wait()
    for g in range(4):
        store(g).wait()


def spectra(place, rows, to_full, to_half, other, targets):
    return pl.pallas_call(
        spectra_kernel,
        out_shape=[
            jax.ShapeDtypeStruct((JJ, L, WIDE), BF),
            jax.ShapeDtypeStruct((L, WIDE), BF),
            jax.ShapeDtypeStruct((32, 40, 128), F32),
        ],
        in_specs=[SMEM] + [HBM] * 3 + [VMEM] + [HBM] * 8,
        out_specs=[HBM] * 3,
        scratch_shapes=[
            pltpu.VMEM((2, 2, L, 640), BF),
            pltpu.VMEM((2, 2, L, WIDE), BF),
            pltpu.VMEM((JJ, L, WIDE), BF),
            pltpu.VMEM((L, WIDE), BF),
            pltpu.VMEM((32, 40, 128), F32),
            pltpu.VMEM((16, 8, 104, 128), BF),
            pltpu.VMEM((256, 256), BF),
            pltpu.VMEM((8, 40, WIDE), BF),
            pltpu.SemaphoreType.DMA((3,)),
            pltpu.SemaphoreType.DMA((4,)),
            pltpu.SemaphoreType.DMA((8,)),
            pltpu.SemaphoreType.DMA((7,)),
        ],
        compiler_params=pltpu.CompilerParams(vmem_limit_bytes=60 * MIB),
        cost_estimate=pl.CostEstimate(
            flops=10_000_000_000, bytes_accessed=12_000_000, transcendentals=0
        ),
        name="spectra",
    )(place, rows, to_full, to_half, other, *targets)


def gradient_kernel(
    stacked_hbm, target_hbm, sums_hbm, cotangent_ref, share_ref, to_mixing_hbm,
    from_full_hbm, from_half_hbm,
    back_ref, grad_hbm, loss_ref,
    stacked_ref, target_ref, to_mixing_ref, from_full_ref, from_half_ref, grad_ref,
    held_ref, member_ref, degree_ref, sums_ref, in_sem, stacked_sem, sem,
):
    loads = [
        pltpu.make_async_copy(there, here, in_sem.at[n])
        for n, (there, here) in enumerate(
            (
                (to_mixing_hbm, to_mixing_ref),
                (target_hbm, target_ref),
                (from_full_hbm, from_full_ref),
                (from_half_hbm, from_half_ref),
                (sums_hbm, sums_ref),
            )
        )
    ]
    loads[4].start()
    piece = L // 4

    def load_piece(n):
        where = pl.ds(piece * n, piece)
        return pltpu.make_async_copy(
            stacked_hbm.at[:, where], stacked_ref.at[:, where], stacked_sem.at[n]
        )

    def keep_piece(n):
        where = pl.ds(piece * n, piece)
        return pltpu.make_async_copy(grad_ref.at[:, where], grad_hbm.at[:, where], sem.at[4 + n])

    for copy in loads[:2]:
        copy.start()
    for n in range(4):
        load_piece(n).start()
    for copy in loads[2:4]:
        copy.start()
    member_ref[...] = block_mask(256, "block")
    degree_ref[...] = block_mask(256, "inside")
    loads[4].wait()
    sums = jnp.sum(sums_ref[...], axis=0)
    sums = sum(sums[10 * n : 10 * n + 10] for n in range(4))
    lane = iota((NBANDS, 128), 1)
    distance = jnp.sqrt(jnp.maximum(expand(sums), 0.0) + EPSILON)
    cotangent = cotangent_ref[...]
    share = share_ref[0:1, :]
    score = jnp.sum(distance * share, axis=1, keepdims=True)
    loss_ref[...] = score * cotangent
    weight = cotangent * (16.0 * MEMBERS * NLAT) * jnp.abs(share) / distance
    beside = jnp.where(lane < MEMBERS, -weight, 0.0)
    loads[0].wait()
    mixing = dot(jnp.concatenate(split3(weight), axis=0), to_mixing_ref[...])
    mixing = mixing[:16] + mixing[16:32] + mixing[32:]
    mixing = [mixing[:, 128 * i : 128 * i + 128] for i in range(MEMBERS)]

    size = MEMBERS * GROUP
    widen = (iota((128, size), 0) == (iota((128, size), 1) >> 4)).astype(F32).astype(BF)
    mix_high, mix_low = split2(jnp.concatenate(mixing, axis=0))
    mix_high = dot(mix_high, widen).astype(BF)
    mix_low = dot(mix_low, widen).astype(BF)
    beside_both = jnp.concatenate(
        [part.astype(F32) for part in split2(beside)] + [jnp.zeros((96, 128), F32)], axis=0
    ).astype(BF)
    band_of_lane = (iota((GROUP, 128), 1) & 15).astype(F32)

    def mix(g, carry):
        start = pl.multiple_of(g * GROUP, GROUP)
        bands = band_column(target_ref, start, GROUP)
        pick = pick_bands(bands, member_ref[...])
        degree = degree_ref[...]
        high = dot(pick, mix_high).astype(BF) * degree
        low = dot(pick, mix_low).astype(BF) * degree
        one_hot = (jnp.broadcast_to(bands, (GROUP, 128)) == band_of_lane).astype(F32).astype(BF)
        weights = dot(one_hot, beside_both)
        weights = jnp.concatenate(
            [jnp.broadcast_to(weights[:, i : i + 1], (GROUP, 128)) for i in range(MEMBERS)], axis=0
        )
        block = stacked_ref[0:MEMBERS, pl.ds(start, GROUP), :].reshape(size, WIDE)
        own = stacked_ref[MEMBERS, pl.ds(start, GROUP), :].astype(F32)
        grad = dot(high, block) + dot(low, block)
        for slot in range(3):
            lanes = slice(128 * slot, 128 * slot + 128)
            part = grad[:, lanes] + weights * jnp.concatenate([own[:, lanes]] * MEMBERS, axis=0)
            grad_ref[:, pl.ds(start, GROUP), lanes] = part.astype(BF).reshape(MEMBERS, GROUP, 128)
        return carry

    loads[1].wait()
    for n in range(4):
        load_piece(n).wait()
        lax.fori_loop(5 * n, 5 * n + 5, mix, 0, unroll=5)
        keep_piece(n).start()
    for copy in loads[2:4]:
        copy.wait()
    def inverse(g, carry):
        for slot in range(3):
            grads = [jnp.concatenate(grads_of(grad_ref, g, i, slot), axis=1) for i in range(2)]
            grads = jnp.concatenate([grads[0], jnp.zeros((WIDE - L, 256), BF), grads[1]], axis=0)
            parts = halves(dot(from_full_ref[slot] if slot < 2 else from_half_ref[0], grads))
            if slot == 2:
                other = halves(dot(from_half_ref[1], grads))
                parts = [parts[k] + swap_halves(other[k]) for k in range(2)]
            start, count = STARTS[slot], COUNTS[slot]
            for k in range(2):
                part = parts[k].reshape(16, count, 128).astype(BF)
                held_ref[:, 2 * g + k, start : start + count, :] = part
        send(g).start()
        return carry

    def send(g):
        where = pl.ds(2 * g, 2)
        return pltpu.make_async_copy(held_ref.at[:, where], back_ref.at[:, where], sem.at[g])

    lax.fori_loop(0, 4, inverse, 0)
    for g in range(4):
        send(g).wait()
        keep_piece(g).wait()


def grads_of(grad_ref, g, i, slot):
    lanes = slice(128 * slot, 128 * slot + 128)
    return [grad_ref[4 * g + 2 * k + i, :, lanes] for k in range(2)]


def gradient(stacked, target, sums, cotangent, share, to_mixing, from_full, from_half):
    return pl.pallas_call(
        gradient_kernel,
        out_shape=[
            jax.ShapeDtypeStruct((16, 8, 104, 128), BF),
            jax.ShapeDtypeStruct((MEMBERS, L, WIDE), BF),
            jax.ShapeDtypeStruct((NBANDS, 128), F32),
        ],
        in_specs=[HBM, HBM, HBM, VMEM, VMEM, HBM, HBM, HBM],
        out_specs=[HBM, HBM, VMEM],
        scratch_shapes=[
            pltpu.VMEM((JJ, L, WIDE), BF),
            pltpu.VMEM((L, WIDE), BF),
            pltpu.VMEM((128, MEMBERS * 128), BF),
            pltpu.VMEM((2, 640, WIDE + L), BF),
            pltpu.VMEM((2, WIDE, WIDE + L), BF),
            pltpu.VMEM((MEMBERS, L, WIDE), BF),
            pltpu.VMEM((16, 8, 104, 128), BF),
            pltpu.VMEM((256, 256), BF),
            pltpu.VMEM((256, 256), BF),
            pltpu.VMEM((32, 40, 128), F32),
            pltpu.SemaphoreType.DMA((5,)),
            pltpu.SemaphoreType.DMA((4,)),
            pltpu.SemaphoreType.DMA((8,)),
        ],
        compiler_params=pltpu.CompilerParams(vmem_limit_bytes=63 * MIB),
        cost_estimate=pl.CostEstimate(
            flops=10_000_000_000, bytes_accessed=12_000_000, transcendentals=0
        ),
        name="gradient",
    )(stacked, target, sums, cotangent, share, to_mixing, from_full, from_half)


def weight_kernel(
    place_ref, rows_ref, grad_ref, full_ref, half_ref, weight_ref, full_sum_ref, half_sum_ref
):
    full_sum_ref[...] = jnp.zeros_like(full_sum_ref)
    half_sum_ref[...] = jnp.zeros_like(half_sum_ref)

    def step(g, carry):
        for slot in range(3):
            values = two_rows_of(rows_ref, g, slot)
            member = iota((values.shape[0], L), 0) % 2
            sides = [[grads_of(grad_ref, g, i, slot) for i in range(2)]]
            if slot == 2:
                sides.append(
                    [[swap_halves(x.astype(F32)).astype(BF) for x in pair] for pair in sides[0]]
                )
            for h, side in enumerate(sides):
                grads = [jnp.concatenate(side[i], axis=1) for i in range(2)]
                terms = jnp.where(
                    member == 0, dot(values, grads[0], 1, 1), dot(values, grads[1], 1, 1)
                )
                if slot < 2:
                    full_sum_ref[slot] += terms
                else:
                    half_sum_ref[h] += terms
        return carry

    lax.fori_loop(0, 4, step, 0)
    for slot in range(3):
        if slot < 2:
            parts = split2(full_sum_ref[slot])
            weight = dot(full_ref[...], parts[0]) + dot(full_ref[...], parts[1])
        else:
            weight = jnp.zeros((NLAT, L), F32)
            for h in range(2):
                parts = split2(half_sum_ref[h])
                weight = weight + dot(half_ref[h], parts[0]) + dot(half_ref[h], parts[1])
        weight = weight * WEIGHT_RATIO
        for c in range(16):
            other = jnp.bitwise_xor(place_ref[2], c // 8)
            step_to = jnp.bitwise_xor(place_ref[1], c % 8)
            weight_ref[other, step_to, slot] = weight[20 * c : 20 * c + 20].astype(BF)


def weights(place, rows, grads, full, half):
    return pl.pallas_call(
        weight_kernel,
        out_shape=jax.ShapeDtypeStruct((2, 8, 3, 20, L), BF),
        in_specs=[SMEM] + [VMEM] * 4,
        out_specs=VMEM,
        scratch_shapes=[
            pltpu.VMEM((2, 640, L), F32),
            pltpu.VMEM((2, WIDE, L), F32),
        ],
        compiler_params=pltpu.CompilerParams(vmem_limit_bytes=63 * MIB),
        cost_estimate=pl.CostEstimate(
            flops=5_000_000_000, bytes_accessed=8_000_000, transcendentals=0
        ),
        name="weights",
    )(place, rows, grads, full, half)


def exchange(x, axes):
    return lax.all_to_all(x, axes, split_axis=0, concat_axis=0, tiled=True)


def swap(blocks, kinds):
    return [lax.ppermute(blocks[k], ENS, [(e, e ^ k) for e in range(8)]) for k in kinds]


def travel(x):
    moved = exchange(x.reshape(128, 52, 2, 128), EVERY)
    return moved.reshape(16, 8, 104, 128)


def body(fourier, analysis, target, band_ids, partners, band_cotangent):
    place = jnp.stack([lax.axis_index(ORDER), lax.axis_index(ENS), lax.axis_index("dp")])
    place = place.astype(jnp.int32)
    full = jnp.asarray(FULL, BF)
    half = jnp.asarray(HALF, BF)
    by_order = jnp.transpose(analysis, (1, 0, 2))
    native = jnp.transpose(fourier[0].reshape(2, 20, 320, 128), (1, 2, 0, 3)).reshape(20, 640, 128)
    packed = pack(native)
    target_in, partners, full, cotangent, packed = lax.optimization_barrier(
        (target[0], partners, full, band_cotangent, packed)
    )
    rows = travel(packed)
    blocks = list(target_blocks(place, target_in, band_ids))
    far = swap(blocks, range(4, 8))
    near = swap(blocks, (3,))
    for k in (2, 1):
        blocks[k], near[0] = lax.optimization_barrier((blocks[k], near[0]))
        near = swap(blocks, (k,)) + near
    targets = [blocks[0]] + near + far
    other = jnp.concatenate(
        [jnp.full((16,), MEMBERS, jnp.int32), partners.T.reshape(64), jnp.zeros((48,), jnp.int32)]
    )
    other = jnp.broadcast_to(other[:, None], (128, 128))
    cotangent = lax.dynamic_slice_in_dim(cotangent, lax.axis_index("dp"), 1, 0)[0]
    cotangent = jnp.broadcast_to(cotangent[:, None], (NBANDS, 128))
    cotangent, other = lax.optimization_barrier((cotangent, other))
    to_full, to_half, from_full, from_half, to_mixing = prepare(
        place, by_order, full, half, other
    )
    share = np.zeros((8, 128), np.float32)
    share[:, :16] = 1.0 / MEMBERS
    share[:, 16:80] = -1.0 / (2.0 * MEMBERS * PARTNERS)
    stacked, observed, sums = spectra(place, rows, to_full, to_half, other, targets)
    sums = exchange(sums.reshape(128, 5, 2, 128), EVERY).reshape(32, 40, 128)
    back, grads, loss = gradient(
        stacked, observed, sums, cotangent, jnp.asarray(share), to_mixing, from_full, from_half
    )
    returned = travel(back)
    loss = loss[:, 0]
    loss_bands = loss + lax.ppermute(loss, "dp", [(0, 1), (1, 0)])
    weight = weights(place, rows, grads, full, half)
    beside = lax.ppermute(weight[1], "dp", [(0, 1), (1, 0)])
    weight = (weight[0].astype(F32) + beside.astype(F32)).astype(BF)
    pieces = [weight[k] for k in range(8)]
    far = swap(pieces, range(4, 8))
    near = swap(pieces, (3,))
    for k in (2, 1):
        pieces[k], near[0] = lax.optimization_barrier((pieces[k], near[0]))
        near = swap(pieces, (k,)) + near
    native_grad, grad_analysis = unpack(place, returned, [pieces[0]] + near + far)
    native_grad = native_grad.reshape(20, 320, 2, 128)
    grad_fourier = jnp.transpose(native_grad, (2, 0, 1, 3)).reshape(1, 2, 20, 40960)
    return (grad_fourier, grad_analysis, loss_bands)


def solution(mesh):
    torus = Mesh(
        mesh.devices.reshape(mesh.shape["dp"], 4, 4, 2, 4),
        ("dp", "order_0", "order_1", "ens_0", "ens_1"),
    )
    in_specs = (
        P("dp", ENS, ORDER, None),
        P(None, ORDER, None),
        P("dp", ENS, ORDER),
        P(ENS, ORDER),
        P(),
        P(),
    )
    out_specs = (P("dp", ENS, ORDER, None), P(DP_ENS, ORDER, None), P())
    return jax.shard_map(body, mesh=torus, in_specs=in_specs, out_specs=out_specs, check_vma=False)
```

```python
import functools

import jax
import jax.numpy as jnp
import numpy as np
from jax import lax
from jax.experimental import pallas as pl
from jax.experimental.pallas import tpu as pltpu
from jax.sharding import Mesh
from jax.sharding import PartitionSpec as P

MEMBERS = 16
NLAT = 320
L = 320
NBANDS = 16
PARTNERS = 4
JJ = MEMBERS + 1
ORDER = ("order_0", "order_1")
ENS = ("ens_0", "ens_1")
DP_ENS = ("dp", "ens_0", "ens_1")
EVERY = ORDER + ENS
EPSILON = 1e-06
WEIGHT_RATIO = 1.0 / 64.0
BF = jnp.bfloat16
F32 = jnp.float32
GROUP = 16
NGROUPS = L // GROUP
WIDE = 384
MIB = 1024 * 1024
VMEM = pl.BlockSpec(memory_space=pltpu.VMEM)
SMEM = pl.BlockSpec(memory_space=pltpu.SMEM)
HBM = pl.BlockSpec(memory_space=pltpu.HBM)


def selections():
    full = np.zeros((NLAT, 640), np.float32)
    half = np.zeros((2, NLAT, WIDE), np.float32)
    for t in range(NLAT):
        full[t, 2 * t : 2 * t + 2] = 1.0
        o, rest = divmod(t, 20)
        h, s = divmod(rest, 10)
        half[h, t, 24 * o + 2 * s : 24 * o + 2 * s + 2] = 1.0
    return full, half


def orderings():
    whole = np.zeros((64, 64), np.float32)
    half = np.zeros((2, 96, 160), np.float32)
    for i in range(2):
        for t in range(4):
            for e in range(8):
                whole[8 * e + 2 * t + i, 16 * t + 2 * e + i] = 1.0
        for t in range(20):
            h, s = divmod(t, 10)
            for p in range(4):
                half[h, 24 * p + 2 * s + i, 8 * t + 2 * p + i] = 1.0
    return whole, half


FULL, HALF = selections()
WHOLE_ORDER, HALF_ORDER = orderings()


def dot(a, b, ca=1, cb=0):
    return lax.dot_general(a, b, (((ca,), (cb,)), ((), ())), preferred_element_type=F32)


def iota(shape, dim):
    return lax.broadcasted_iota(jnp.int32, shape, dim)


def swap_halves(x):
    return pltpu.roll(x, 64, x.ndim - 1)


def split2(x):
    high = x.astype(BF)
    return high, (x - high.astype(F32)).astype(BF)


def split3(x):
    high = x.astype(BF)
    rest = x - high.astype(F32)
    mid = rest.astype(BF)
    return high, mid, (rest - mid.astype(F32)).astype(BF)


STEP = 4


def pack_step(x_ref, whole_ref, half_ref, o_ref):
    def block(rows, columns):
        return x_ref[rows, columns, :].astype(F32).reshape(-1, 128).astype(BF)

    for k in range(STEP):
        for slot in range(2):
            start = 40 * k + 16 * slot
            parts = [block(slice(4 * c, 4 * c + 4), slice(start, start + 16)) for c in range(5)]
            moved = dot(whole_ref[...], jnp.concatenate(parts, axis=1))
            moved = [moved[:, 128 * c : 128 * c + 128].reshape(8, 8, 128) for c in range(5)]
            moved = jnp.concatenate(moved, axis=1).astype(BF)
            o_ref[k, :, 40 * slot : 40 * slot + 40, :] = moved
    parts = [block(slice(0, 20), slice(40 * k + 32, 40 * k + 40)) for k in range(STEP)]
    values = jnp.concatenate(parts, axis=1)
    firsts = dot(half_ref[0], values)
    seconds = dot(half_ref[1], values)
    low = iota((96, 128), 1) < 64
    for k in range(STEP):
        first = firsts[:, 128 * k : 128 * k + 128]
        second = seconds[:, 128 * k : 128 * k + 128]
        real = jnp.where(low, first, swap_halves(second)).astype(BF)
        imaginary = jnp.where(low, swap_halves(first), second).astype(BF)
        for p in range(4):
            o_ref[k, 2 * p, 80:104, :] = real[24 * p : 24 * p + 24]
            o_ref[k, 2 * p + 1, 80:104, :] = imaginary[24 * p : 24 * p + 24]


def unpack_step(y_ref, whole_ref, half_ref, x_ref):
    for k in range(STEP):
        for slot in range(2):
            rows = y_ref[k, :, 40 * slot : 40 * slot + 40, :].astype(F32)
            parts = [rows[:, 8 * c : 8 * c + 8].reshape(64, 128).astype(BF) for c in range(5)]
            moved = dot(whole_ref[...], jnp.concatenate(parts, axis=1))
            moved = [moved[:, 128 * c : 128 * c + 128].reshape(4, 16, 128) for c in range(5)]
            start = 40 * k + 16 * slot
            x_ref[:, start : start + 16, :] = jnp.concatenate(moved, axis=0).astype(BF)
    low = iota((96, 128), 1) < 64
    firsts, seconds = [], []
    for k in range(STEP):
        real, imaginary = [
            jnp.concatenate([y_ref[k, 2 * p + r, 80:104, :].astype(F32) for p in range(4)], axis=0)
            for r in range(2)
        ]
        firsts.append(jnp.where(low, real, swap_halves(imaginary)).astype(BF))
        seconds.append(jnp.where(low, swap_halves(real), imaginary).astype(BF))
    moved = dot(half_ref[0], jnp.concatenate(firsts, axis=1))
    moved = moved + dot(half_ref[1], jnp.concatenate(seconds, axis=1))
    for k in range(STEP):
        part = moved[:, 128 * k : 128 * k + 128].reshape(20, 8, 128).astype(BF)
        x_ref[:, 40 * k + 32 : 40 * k + 40, :] = part


def in_steps(step, place_in, place_out, in_hbm, whole_ref, half_ref, out_hbm, *refs, between=None):
    in_ref, out_ref, in_sem, out_sem = refs

    def load(g):
        return pltpu.make_async_copy(place_in(in_hbm, g), in_ref.at[g], in_sem.at[g])

    def store(g):
        return pltpu.make_async_copy(out_ref.at[g], place_out(out_hbm, g), out_sem.at[g])

    for g in range(16 // STEP):
        load(g).start()

    def one(g, carry):
        load(g).wait()
        step(in_ref.at[g], whole_ref, half_ref, out_ref.at[g])
        store(g).start()
        return carry

    lax.fori_loop(0, 8 // STEP, one, 0)
    if between is not None:
        between()
    lax.fori_loop(8 // STEP, 16 // STEP, one, 0)
    for g in range(16 // STEP):
        store(g).wait()


def unpack_kernel(place_ref, in_hbm, whole_ref, half_ref, *refs):
    r_refs, (out_hbm, weight_hbm), rest = refs[:8], refs[8:10], refs[10:]
    *step_refs, order_ref, weight_ref, r_sem, weight_sem = rest
    loads = [
        pltpu.make_async_copy(
            r_refs[k], order_ref.at[jnp.bitwise_xor(place_ref[1], k)], r_sem.at[k]
        )
        for k in range(8)
    ]
    out = pltpu.make_async_copy(weight_ref, weight_hbm, weight_sem)

    def finish():
        for copy in loads:
            copy.wait()
        for e in range(8):
            weight_ref[:, e, :] = order_ref[e, 0].astype(F32)
            weight_ref[:, 8 + e, :] = order_ref[e, 1].astype(F32)
        for p in range(4):
            both = order_ref[2 * p, 2].astype(F32) + order_ref[2 * p + 1, 2].astype(F32)
            weight_ref[:, 16 + p, :] = both
        out.start()

    for copy in loads:
        copy.start()
    in_steps(
        unpack_step, packed_at, native_at, in_hbm, whole_ref, half_ref, out_hbm, *step_refs,
        between=finish,
    )
    out.wait()


def native_at(ref, g):
    return ref.at[:, pl.ds(40 * STEP * g, 40 * STEP)]


def packed_at(ref, g):
    return ref.at[pl.ds(STEP * g, STEP)]


NATIVE = pltpu.VMEM((16 // STEP, 20, 40 * STEP, 128), BF)
PACKED = pltpu.VMEM((16 // STEP, STEP, 8, 104, 128), BF)
SEMS = [pltpu.SemaphoreType.DMA((16 // STEP,))] * 2


def pack(x):
    return pl.pallas_call(
        functools.partial(in_steps, pack_step, native_at, packed_at),
        out_shape=jax.ShapeDtypeStruct((16, 8, 104, 128), BF),
        in_specs=[HBM, VMEM, VMEM],
        out_specs=HBM,
        scratch_shapes=[NATIVE, PACKED] + SEMS,
        compiler_params=pltpu.CompilerParams(vmem_limit_bytes=63 * MIB),
        name="pack",
    )(x, jnp.asarray(WHOLE_ORDER, BF), jnp.asarray(HALF_ORDER, BF))


def unpack(place, y, received):
    return pl.pallas_call(
        unpack_kernel,
        out_shape=[
            jax.ShapeDtypeStruct((20, 640, 128), BF),
            jax.ShapeDtypeStruct((20, 20, L), F32),
        ],
        in_specs=[SMEM, HBM, VMEM, VMEM] + [HBM] * 8,
        out_specs=[HBM, HBM],
        scratch_shapes=[PACKED, NATIVE]
        + SEMS
        + [
            pltpu.VMEM((8, 3, 20, L), BF),
            pltpu.VMEM((20, 20, L), F32),
            pltpu.SemaphoreType.DMA((8,)),
            pltpu.SemaphoreType.DMA(()),
        ],
        compiler_params=pltpu.CompilerParams(vmem_limit_bytes=63 * MIB),
        name="unpack",
    )(
        place, y, jnp.asarray(WHOLE_ORDER.T, BF), jnp.asarray(HALF_ORDER.transpose(0, 2, 1), BF),
        *received,
    )


def target_kernel(place_ref, t_ref, band_ref, *refs):
    *o_refs, held_ref, sem = refs
    bands = jnp.broadcast_to(band_ref[:, 0:1].astype(F32), (40, 128))
    low = iota((40, 128), 1) < 64
    for k in range(8):
        e = jnp.bitwise_xor(place_ref[1], k)

        def lanes(start):
            return t_ref[:, pl.ds(pl.multiple_of(start, 128), 128)]

        middle = lanes(2048 + 128 * (e // 2)).astype(F32)
        held_ref[k, :, 0:128] = lanes(128 * e)
        held_ref[k, :, 128:256] = lanes(1024 + 128 * e)
        odd = jnp.broadcast_to(e % 2, (40, 128)) == 1
        part = jnp.where(odd, swap_halves(middle), middle)
        held_ref[k, :, 256:384] = jnp.where(low, part, bands).astype(BF)
    copies = [pltpu.make_async_copy(held_ref.at[k], o_refs[k], sem.at[k]) for k in range(8)]
    for copy in copies:
        copy.start()
    for copy in copies:
        copy.wait()


def target_blocks(place, target, bands):
    return pl.pallas_call(
        target_kernel,
        out_shape=[jax.ShapeDtypeStruct((40, WIDE), BF)] * 8,
        in_specs=[SMEM, VMEM, VMEM],
        out_specs=[HBM] * 8,
        scratch_shapes=[pltpu.VMEM((8, 40, WIDE), BF), pltpu.SemaphoreType.DMA((8,))],
        compiler_params=pltpu.CompilerParams(vmem_limit_bytes=63 * MIB),
        name="target_blocks",
    )(place, target, bands)


def own_orders(place_ref):
    ens = place_ref[1]
    return ens, 8 + ens, 16 + ens // 2


def fetches(place_ref, analysis_ref, own_ref, sem):
    return [
        pltpu.make_async_copy(analysis_ref.at[m], own_ref.at[k], sem.at[k])
        for k, m in enumerate(own_orders(place_ref))
    ]


def halves(x):
    return [x[:, 128 * k : 128 * k + 128] for k in range(2)]


STARTS = (0, 40, 80)
COUNTS = (40, 40, 24)


def two_rows_of(rows_ref, g, slot):
    start, count = STARTS[slot], COUNTS[slot]
    parts = [
        rows_ref[:, 2 * g + k, start : start + count, :]
        .astype(F32)
        .reshape(16 * count, 128)
        .astype(BF)
        for k in range(2)
    ]
    return jnp.concatenate(parts, axis=1)


def band_column(target_ref, start, count):
    return target_ref[pl.ds(start, count), 256:384].astype(F32)[:, 64:65]


def prepare_kernel(
    place_ref, analysis_ref, full_ref, half_ref, other_column_ref,
    to_full_ref, to_half_ref, from_full_ref, from_half_ref, to_mixing_ref, own_ref, sem,
):
    copies = fetches(place_ref, analysis_ref, own_ref, sem)
    for copy in copies:
        copy.start()
    row, j = iota((128, 128), 0), iota((128, 128), 1)
    who, other = row & 15, other_column_ref[...]
    pair = (row >= 16) & (row < 80)
    for i in range(MEMBERS):
        own = (j == i).astype(F32)
        value = jnp.where(pair & (who == i), (other == j).astype(F32) - own, 0.0)
        value = value + jnp.where(pair & (other == i), (who == j).astype(F32) - own, 0.0)
        value = value + jnp.where((row < 16) & (who == i), own, 0.0)
        to_mixing_ref[:, 128 * i : 128 * i + 128] = value.astype(BF)
    for copy in copies:
        copy.wait()
    for n in range(4):
        choose = full_ref[...] if n < 2 else half_ref[n - 2]
        own = own_ref[min(n, 2)]
        to_ref = to_full_ref.at[n] if n < 2 else to_half_ref.at[n - 2]
        from_ref = from_full_ref.at[n] if n < 2 else from_half_ref.at[n - 2]
        from_ref[...] = jnp.zeros_like(from_ref)
        spread = dot(own, choose, 0, 0)
        member = iota(spread.shape, 1) % 2
        for i in range(2):
            to_ref[i] = jnp.where(member == i, spread, 0.0).astype(BF)
        spread = dot(choose, own, 0, 0)
        member = iota(spread.shape, 0) % 2
        for i in range(2):
            from_ref[:, WIDE * i : WIDE * i + L] = jnp.where(member == i, spread, 0.0).astype(BF)


def prepare(place, analysis, full, half, other):
    return pl.pallas_call(
        prepare_kernel,
        out_shape=[
            jax.ShapeDtypeStruct((2, 2, L, 640), BF),
            jax.ShapeDtypeStruct((2, 2, L, WIDE), BF),
            jax.ShapeDtypeStruct((2, 640, WIDE + L), BF),
            jax.ShapeDtypeStruct((2, WIDE, WIDE + L), BF),
            jax.ShapeDtypeStruct((128, MEMBERS * 128), BF),
        ],
        in_specs=[SMEM, HBM, VMEM, VMEM, VMEM],
        out_specs=[VMEM] * 5,
        scratch_shapes=[pltpu.VMEM((3, NLAT, L), BF), pltpu.SemaphoreType.DMA((3,))],
        compiler_params=pltpu.CompilerParams(vmem_limit_bytes=63 * MIB),
        name="prepare",
    )(place, analysis, full, half, other)


def block_mask(size, kind, lanes=None):
    shape = (size, lanes or size)
    row, lane = iota(shape, 0), iota(shape, 1)
    same = (row >> 4) == (lane >> 4) if kind == "block" else (row & 15) == (lane & 15)
    return same.astype(F32).astype(BF)


def pick_bands(bands, mask):
    shape = (GROUP, 128)
    one_hot = jnp.broadcast_to(bands, shape) == (iota(shape, 1) & 15).astype(F32)
    tile = jnp.concatenate([one_hot.astype(F32).astype(BF)] * MEMBERS, axis=0)
    return jnp.concatenate([tile, tile], axis=1) * mask


def fold(x):
    x = x[:, :128] + x[:, 128:]
    for shift in (64, 32, 16):
        x = x + pltpu.roll(x, shift, 1)
    return x


def compact(x):
    top, rest = x[:8], x[8:]
    lane = iota((8, 128), 1)
    first = jnp.where(lane < 80, top, pltpu.roll(rest, 80, 1))
    left = pltpu.roll(rest, 80, 1)
    lane = iota((1, 128), 1)
    tails = []
    for n in range(2):
        tail = jnp.zeros((1, 128), F32)
        for r in range(4):
            row = pltpu.roll(left[4 * n + r : 4 * n + r + 1], 32 * r, 1)
            tail = jnp.where((lane >= 32 * r) & (lane < 32 * r + 32), row, tail)
        tails.append(tail)
    return jnp.concatenate([first] + tails, axis=0)


def expand(x):
    first = x[:8]
    lane = iota((8, 128), 1)
    top = jnp.where(lane < 80, first, 0.0)
    rows = []
    for n in range(2):
        for r in range(4):
            rows.append(pltpu.roll(x[8 + n : 9 + n], (48 - 32 * r) % 128, 1))
    rest = jnp.where(lane < 48, pltpu.roll(first, 48, 1), jnp.concatenate(rows, axis=0))
    return jnp.concatenate([top, jnp.where(lane < 80, rest, 0.0)], axis=0)


def spectra_kernel(place_ref, rows_hbm, to_full_hbm, to_half_hbm, other_ref, *refs):
    target_refs = refs[:8]
    stacked_hbm, target_hbm, sums_hbm = refs[8:11]
    to_full_ref, to_half_ref, stacked_ref, target_ref, sums_ref = refs[11:16]
    rows_ref, mask_ref, order_ref, in_sem, rows_sem, target_sem, out_sem = refs[16:]

    def load_rows(g):
        where = pl.ds(2 * g, 2)
        return pltpu.make_async_copy(rows_hbm.at[:, where], rows_ref.at[:, where], rows_sem.at[g])

    load_rows(0).start()
    loads = [
        pltpu.make_async_copy(to_full_hbm.at[n], to_full_ref.at[n], in_sem.at[n]) for n in range(2)
    ]
    loads.append(pltpu.make_async_copy(to_half_hbm, to_half_ref, in_sem.at[2]))
    for k in range(8):
        there = order_ref.at[jnp.bitwise_xor(place_ref[1], k)]
        loads.append(pltpu.make_async_copy(target_refs[k], there, target_sem.at[k]))
    for copy in loads[:3]:
        copy.start()
    for g in range(1, 4):
        load_rows(g).start()
    for copy in loads[3:]:
        copy.start()
    mask_ref[...] = block_mask(256, "block")
    base = place_ref[0] * 20
    orders = [base + m for m in own_orders(place_ref)]
    degree = iota((L, 128), 0)
    low = iota((L, 128), 1) < 64
    keeps = [degree >= orders[0], degree >= orders[1], (degree >= orders[2]) & low]

    def transform(g, carry, operators=None):
        load_rows(g).wait()
        for slot in range(3):
            if operators:
                operators[slot].wait()
            values = two_rows_of(rows_ref, g, slot)
            for i in range(2):
                if slot < 2:
                    parts = halves(dot(to_full_ref[slot, i], values))
                else:
                    parts = halves(dot(to_half_ref[0, i], values))
                    other = halves(dot(to_half_ref[1, i], values))
                    parts = [parts[k] + swap_halves(other[k]) for k in range(2)]
                for k in range(2):
                    stacked_ref[4 * g + 2 * k + i, :, 128 * slot : 128 * slot + 128] = jnp.where(
                        keeps[slot], parts[k], 0.0
                    ).astype(BF)
        store(g).start()
        return carry

    def store(g):
        where = pl.ds(4 * g, 4)
        return pltpu.make_async_copy(stacked_ref.at[where], stacked_hbm.at[where], out_sem.at[g])

    transform(0, 0, loads[:3])
    lax.fori_loop(1, 4, transform, 0)
    for copy in loads[3:]:
        copy.wait()
    target_ref[...] = order_ref[...].astype(F32).reshape(L, WIDE).astype(BF)
    stores = [pltpu.make_async_copy(target_ref, target_hbm, out_sem.at[4])]
    for slot in range(3):
        lanes = slice(128 * slot, 128 * slot + 128)
        observed = jnp.where(keeps[slot], target_ref[:, lanes].astype(F32), 0.0)
        stacked_ref[MEMBERS, :, lanes] = observed.astype(BF)
    last = stacked_hbm.at[MEMBERS]
    stores.append(pltpu.make_async_copy(stacked_ref.at[MEMBERS], last, out_sem.at[5]))
    for copy in stores:
        copy.start()

    size = MEMBERS * GROUP
    same = (iota((JJ * GROUP, size), 0) & 15) == (iota((JJ * GROUP, size), 1) & 15)
    empty = jnp.zeros((32 - JJ, size), F32)

    def gram(g, carry):
        totals, last = carry
        start = pl.multiple_of(g * GROUP, GROUP)
        block = stacked_ref[:, pl.ds(start, GROUP), :].reshape(JJ * GROUP, WIDE)
        products = jnp.where(same, dot(block, block[:size], 1, 1), 0.0)
        products = jnp.sum(products.reshape(JJ, GROUP, size), axis=1)
        parts = split3(jnp.concatenate([products, empty], axis=0))
        bands = band_column(target_ref, start, GROUP)
        moved = dot(jnp.concatenate(parts, axis=0), pick_bands(bands, mask_ref[...]))
        totals = totals + (moved[:32] + moved[32:64] + moved[64:])
        own = block[size:].astype(F32)
        power = jnp.sum(own * own, axis=1, keepdims=True)
        lane = (iota((GROUP, 128), 1) & 15).astype(F32)
        power = jnp.where(jnp.broadcast_to(bands, (GROUP, 128)) == lane, power, 0.0)
        return totals, last + jnp.sum(power, axis=0, keepdims=True)

    start = (jnp.zeros((32, size), F32), jnp.zeros((1, 128), F32))
    totals, last = lax.fori_loop(0, NGROUPS, gram, start, unroll=2)

    grams = totals[:MEMBERS]
    member = iota((MEMBERS, size), 1) >> 4
    diagonal = jnp.where(iota((MEMBERS, size), 0) == member, grams, 0.0)
    powers = jnp.sum(diagonal, axis=0, keepdims=True)
    own_power = fold(diagonal)
    squares = jnp.concatenate([own_power, own_power], axis=1) + powers - 2.0 * grams
    beside = powers + jnp.concatenate([last, last], axis=1) - 2.0 * totals[MEMBERS : MEMBERS + 1]
    beside = jnp.broadcast_to(beside, (MEMBERS, size))
    chosen = fold(jnp.where(iota((MEMBERS, size), 0) == member, beside, 0.0))
    kind = iota((MEMBERS, 128), 1) >> 4
    wanted = jnp.where(kind == 0, chosen, 0.0)
    for p in range(PARTNERS):
        other = other_ref[GROUP * (p + 1) : GROUP * (p + 2), :]
        other = jnp.concatenate([other, other], axis=1)
        chosen = fold(jnp.where(member == other, squares, 0.0))
        wanted = wanted + jnp.where(kind == p + 1, chosen, 0.0)
    wanted = jnp.concatenate([wanted, jnp.zeros((112, 128), F32)], axis=0).T
    squares = wanted[:NBANDS]
    for c in range(1, PARTNERS + 1):
        squares = squares + pltpu.roll(wanted[16 * c : 16 * c + 16], 16 * c, 1)
    sums = compact(squares)
    sums = jnp.concatenate([sums] * 4, axis=0)
    sums_ref[...] = jnp.broadcast_to(sums[None], (32, 40, 128))
    stores.append(pltpu.make_async_copy(sums_ref, sums_hbm, out_sem.at[6]))
    stores[2].start()
    for copy in stores:
        copy.wait()
    for g in range(4):
        store(g).wait()


def spectra(place, rows, to_full, to_half, other, targets):
    return pl.pallas_call(
        spectra_kernel,
        out_shape=[
            jax.ShapeDtypeStruct((JJ, L, WIDE), BF),
            jax.ShapeDtypeStruct((L, WIDE), BF),
            jax.ShapeDtypeStruct((32, 40, 128), F32),
        ],
        in_specs=[SMEM] + [HBM] * 3 + [VMEM] + [HBM] * 8,
        out_specs=[HBM] * 3,
        scratch_shapes=[
            pltpu.VMEM((2, 2, L, 640), BF),
            pltpu.VMEM((2, 2, L, WIDE), BF),
            pltpu.VMEM((JJ, L, WIDE), BF),
            pltpu.VMEM((L, WIDE), BF),
            pltpu.VMEM((32, 40, 128), F32),
            pltpu.VMEM((16, 8, 104, 128), BF),
            pltpu.VMEM((256, 256), BF),
            pltpu.VMEM((8, 40, WIDE), BF),
            pltpu.SemaphoreType.DMA((3,)),
            pltpu.SemaphoreType.DMA((4,)),
            pltpu.SemaphoreType.DMA((8,)),
            pltpu.SemaphoreType.DMA((7,)),
        ],
        compiler_params=pltpu.CompilerParams(vmem_limit_bytes=60 * MIB),
        cost_estimate=pl.CostEstimate(
            flops=10_000_000_000, bytes_accessed=12_000_000, transcendentals=0
        ),
        name="spectra",
    )(place, rows, to_full, to_half, other, *targets)


def gradient_kernel(
    stacked_hbm, target_hbm, sums_hbm, cotangent_ref, share_ref, to_mixing_hbm,
    from_full_hbm, from_half_hbm,
    back_ref, grad_hbm, loss_ref,
    stacked_ref, target_ref, to_mixing_ref, from_full_ref, from_half_ref, grad_ref,
    held_ref, member_ref, degree_ref, sums_ref, in_sem, stacked_sem, sem,
):
    loads = [
        pltpu.make_async_copy(there, here, in_sem.at[n])
        for n, (there, here) in enumerate(
            (
                (to_mixing_hbm, to_mixing_ref),
                (target_hbm, target_ref),
                (from_full_hbm, from_full_ref),
                (from_half_hbm, from_half_ref),
                (sums_hbm, sums_ref),
            )
        )
    ]
    loads[4].start()
    piece = L // 4

    def load_piece(n):
        where = pl.ds(piece * n, piece)
        return pltpu.make_async_copy(
            stacked_hbm.at[:, where], stacked_ref.at[:, where], stacked_sem.at[n]
        )

    def keep_piece(n):
        where = pl.ds(piece * n, piece)
        return pltpu.make_async_copy(grad_ref.at[:, where], grad_hbm.at[:, where], sem.at[4 + n])

    for copy in loads[:2]:
        copy.start()
    for n in range(4):
        load_piece(n).start()
    for copy in loads[2:4]:
        copy.start()
    member_ref[...] = block_mask(256, "block")
    degree_ref[...] = block_mask(256, "inside")
    loads[4].wait()
    sums = jnp.sum(sums_ref[...], axis=0)
    sums = sum(sums[10 * n : 10 * n + 10] for n in range(4))
    lane = iota((NBANDS, 128), 1)
    distance = jnp.sqrt(jnp.maximum(expand(sums), 0.0) + EPSILON)
    cotangent = cotangent_ref[...]
    share = share_ref[0:1, :]
    score = jnp.sum(distance * share, axis=1, keepdims=True)
    loss_ref[...] = score * cotangent
    weight = cotangent * (16.0 * MEMBERS * NLAT) * jnp.abs(share) / distance
    beside = jnp.where(lane < MEMBERS, -weight, 0.0)
    loads[0].wait()
    mixing = dot(jnp.concatenate(split3(weight), axis=0), to_mixing_ref[...])
    mixing = mixing[:16] + mixing[16:32] + mixing[32:]
    mixing = [mixing[:, 128 * i : 128 * i + 128] for i in range(MEMBERS)]

    size = MEMBERS * GROUP
    widen = (iota((128, size), 0) == (iota((128, size), 1) >> 4)).astype(F32).astype(BF)
    mix_high, mix_low = split2(jnp.concatenate(mixing, axis=0))
    mix_high = dot(mix_high, widen).astype(BF)
    mix_low = dot(mix_low, widen).astype(BF)
    beside_both = jnp.concatenate(
        [part.astype(F32) for part in split2(beside)] + [jnp.zeros((96, 128), F32)], axis=0
    ).astype(BF)
    band_of_lane = (iota((GROUP, 128), 1) & 15).astype(F32)

    def mix(g, carry):
        start = pl.multiple_of(g * GROUP, GROUP)
        bands = band_column(target_ref, start, GROUP)
        pick = pick_bands(bands, member_ref[...])
        degree = degree_ref[...]
        high = dot(pick, mix_high).astype(BF) * degree
        low = dot(pick, mix_low).astype(BF) * degree
        one_hot = (jnp.broadcast_to(bands, (GROUP, 128)) == band_of_lane).astype(F32).astype(BF)
        weights = dot(one_hot, beside_both)
        weights = jnp.concatenate(
            [jnp.broadcast_to(weights[:, i : i + 1], (GROUP, 128)) for i in range(MEMBERS)], axis=0
        )
        block = stacked_ref[0:MEMBERS, pl.ds(start, GROUP), :].reshape(size, WIDE)
        own = stacked_ref[MEMBERS, pl.ds(start, GROUP), :].astype(F32)
        grad = dot(high, block) + dot(low, block)
        for slot in range(3):
            lanes = slice(128 * slot, 128 * slot + 128)
            part = grad[:, lanes] + weights * jnp.concatenate([own[:, lanes]] * MEMBERS, axis=0)
            grad_ref[:, pl.ds(start, GROUP), lanes] = part.astype(BF).reshape(MEMBERS, GROUP, 128)
        return carry

    loads[1].wait()
    for n in range(4):
        load_piece(n).wait()
        lax.fori_loop(5 * n, 5 * n + 5, mix, 0, unroll=5)
        keep_piece(n).start()
    for copy in loads[2:4]:
        copy.wait()
    def inverse(g, carry):
        for slot in range(3):
            grads = [jnp.concatenate(grads_of(grad_ref, g, i, slot), axis=1) for i in range(2)]
            grads = jnp.concatenate([grads[0], jnp.zeros((WIDE - L, 256), BF), grads[1]], axis=0)
            parts = halves(dot(from_full_ref[slot] if slot < 2 else from_half_ref[0], grads))
            if slot == 2:
                other = halves(dot(from_half_ref[1], grads))
                parts = [parts[k] + swap_halves(other[k]) for k in range(2)]
            start, count = STARTS[slot], COUNTS[slot]
            for k in range(2):
                part = parts[k].reshape(16, count, 128).astype(BF)
                held_ref[:, 2 * g + k, start : start + count, :] = part
        send(g).start()
        return carry

    def send(g):
        where = pl.ds(2 * g, 2)
        return pltpu.make_async_copy(held_ref.at[:, where], back_ref.at[:, where], sem.at[g])

    lax.fori_loop(0, 4, inverse, 0, unroll=2)
    for g in range(4):
        send(g).wait()
        keep_piece(g).wait()


def grads_of(grad_ref, g, i, slot):
    lanes = slice(128 * slot, 128 * slot + 128)
    return [grad_ref[4 * g + 2 * k + i, :, lanes] for k in range(2)]


def gradient(stacked, target, sums, cotangent, share, to_mixing, from_full, from_half):
    return pl.pallas_call(
        gradient_kernel,
        out_shape=[
            jax.ShapeDtypeStruct((16, 8, 104, 128), BF),
            jax.ShapeDtypeStruct((MEMBERS, L, WIDE), BF),
            jax.ShapeDtypeStruct((NBANDS, 128), F32),
        ],
        in_specs=[HBM, HBM, HBM, VMEM, VMEM, HBM, HBM, HBM],
        out_specs=[HBM, HBM, VMEM],
        scratch_shapes=[
            pltpu.VMEM((JJ, L, WIDE), BF),
            pltpu.VMEM((L, WIDE), BF),
            pltpu.VMEM((128, MEMBERS * 128), BF),
            pltpu.VMEM((2, 640, WIDE + L), BF),
            pltpu.VMEM((2, WIDE, WIDE + L), BF),
            pltpu.VMEM((MEMBERS, L, WIDE), BF),
            pltpu.VMEM((16, 8, 104, 128), BF),
            pltpu.VMEM((256, 256), BF),
            pltpu.VMEM((256, 256), BF),
            pltpu.VMEM((32, 40, 128), F32),
            pltpu.SemaphoreType.DMA((5,)),
            pltpu.SemaphoreType.DMA((4,)),
            pltpu.SemaphoreType.DMA((8,)),
        ],
        compiler_params=pltpu.CompilerParams(vmem_limit_bytes=63 * MIB),
        cost_estimate=pl.CostEstimate(
            flops=10_000_000_000, bytes_accessed=12_000_000, transcendentals=0
        ),
        name="gradient",
    )(stacked, target, sums, cotangent, share, to_mixing, from_full, from_half)


def weight_kernel(
    place_ref, rows_ref, grad_ref, full_ref, half_ref, weight_ref, full_sum_ref, half_sum_ref
):
    full_sum_ref[...] = jnp.zeros_like(full_sum_ref)
    half_sum_ref[...] = jnp.zeros_like(half_sum_ref)

    def step(g, carry):
        for slot in range(3):
            values = two_rows_of(rows_ref, g, slot)
            member = iota((values.shape[0], L), 0) % 2
            sides = [[grads_of(grad_ref, g, i, slot) for i in range(2)]]
            if slot == 2:
                sides.append(
                    [[swap_halves(x.astype(F32)).astype(BF) for x in pair] for pair in sides[0]]
                )
            for h, side in enumerate(sides):
                grads = [jnp.concatenate(side[i], axis=1) for i in range(2)]
                terms = jnp.where(
                    member == 0, dot(values, grads[0], 1, 1), dot(values, grads[1], 1, 1)
                )
                if slot < 2:
                    full_sum_ref[slot] += terms
                else:
                    half_sum_ref[h] += terms
        return carry

    lax.fori_loop(0, 4, step, 0)
    for slot in range(3):
        if slot < 2:
            parts = split2(full_sum_ref[slot])
            weight = dot(full_ref[...], parts[0]) + dot(full_ref[...], parts[1])
        else:
            weight = jnp.zeros((NLAT, L), F32)
            for h in range(2):
                parts = split2(half_sum_ref[h])
                weight = weight + dot(half_ref[h], parts[0]) + dot(half_ref[h], parts[1])
        weight = weight * WEIGHT_RATIO
        for c in range(16):
            other = jnp.bitwise_xor(place_ref[2], c // 8)
            step_to = jnp.bitwise_xor(place_ref[1], c % 8)
            weight_ref[other, step_to, slot] = weight[20 * c : 20 * c + 20].astype(BF)


def weights(place, rows, grads, full, half):
    return pl.pallas_call(
        weight_kernel,
        out_shape=jax.ShapeDtypeStruct((2, 8, 3, 20, L), BF),
        in_specs=[SMEM] + [VMEM] * 4,
        out_specs=VMEM,
        scratch_shapes=[
            pltpu.VMEM((2, 640, L), F32),
            pltpu.VMEM((2, WIDE, L), F32),
        ],
        compiler_params=pltpu.CompilerParams(vmem_limit_bytes=63 * MIB),
        cost_estimate=pl.CostEstimate(
            flops=5_000_000_000, bytes_accessed=8_000_000, transcendentals=0
        ),
        name="weights",
    )(place, rows, grads, full, half)


def exchange(x, axes):
    return lax.all_to_all(x, axes, split_axis=0, concat_axis=0, tiled=True)


def swap(blocks, kinds):
    return [lax.ppermute(blocks[k], ENS, [(e, e ^ k) for e in range(8)]) for k in kinds]


def travel(x):
    moved = exchange(x.reshape(128, 52, 2, 128), EVERY)
    return moved.reshape(16, 8, 104, 128)


def body(fourier, analysis, target, band_ids, partners, band_cotangent):
    place = jnp.stack([lax.axis_index(ORDER), lax.axis_index(ENS), lax.axis_index("dp")])
    place = place.astype(jnp.int32)
    full = jnp.asarray(FULL, BF)
    half = jnp.asarray(HALF, BF)
    by_order = jnp.transpose(analysis, (1, 0, 2))
    native = jnp.transpose(fourier[0].reshape(2, 20, 320, 128), (1, 2, 0, 3)).reshape(20, 640, 128)
    packed = pack(native)
    target_in, partners, full, cotangent, packed = lax.optimization_barrier(
        (target[0], partners, full, band_cotangent, packed)
    )
    rows = travel(packed)
    blocks = list(target_blocks(place, target_in, band_ids))
    far = swap(blocks, range(4, 8))
    near = swap(blocks, (3,))
    for k in (2, 1):
        blocks[k], near[0] = lax.optimization_barrier((blocks[k], near[0]))
        near = swap(blocks, (k,)) + near
    targets = [blocks[0]] + near + far
    other = jnp.concatenate(
        [jnp.full((16,), MEMBERS, jnp.int32), partners.T.reshape(64), jnp.zeros((48,), jnp.int32)]
    )
    other = jnp.broadcast_to(other[:, None], (128, 128))
    cotangent = lax.dynamic_slice_in_dim(cotangent, lax.axis_index("dp"), 1, 0)[0]
    cotangent = jnp.broadcast_to(cotangent[:, None], (NBANDS, 128))
    cotangent, other = lax.optimization_barrier((cotangent, other))
    to_full, to_half, from_full, from_half, to_mixing = prepare(
        place, by_order, full, half, other
    )
    share = np.zeros((8, 128), np.float32)
    share[:, :16] = 1.0 / MEMBERS
    share[:, 16:80] = -1.0 / (2.0 * MEMBERS * PARTNERS)
    stacked, observed, sums = spectra(place, rows, to_full, to_half, other, targets)
    sums = exchange(sums.reshape(128, 5, 2, 128), EVERY).reshape(32, 40, 128)
    back, grads, loss = gradient(
        stacked, observed, sums, cotangent, jnp.asarray(share), to_mixing, from_full, from_half
    )
    returned = travel(back)
    loss = loss[:, 0]
    loss_bands = loss + lax.ppermute(loss, "dp", [(0, 1), (1, 0)])
    weight = weights(place, rows, grads, full, half)
    beside = lax.ppermute(weight[1], "dp", [(0, 1), (1, 0)])
    weight = (weight[0].astype(F32) + beside.astype(F32)).astype(BF)
    pieces = [weight[k] for k in range(8)]
    far = swap(pieces, range(4, 8))
    near = swap(pieces, (3,))
    for k in (2, 1):
        pieces[k], near[0] = lax.optimization_barrier((pieces[k], near[0]))
        near = swap(pieces, (k,)) + near
    native_grad, grad_analysis = unpack(place, returned, [pieces[0]] + near + far)
    native_grad = native_grad.reshape(20, 320, 2, 128)
    grad_fourier = jnp.transpose(native_grad, (2, 0, 1, 3)).reshape(1, 2, 20, 40960)
    return (grad_fourier, grad_analysis, loss_bands)


def solution(mesh):
    torus = Mesh(
        mesh.devices.reshape(mesh.shape["dp"], 4, 4, 2, 4),
        ("dp", "order_0", "order_1", "ens_0", "ens_1"),
    )
    in_specs = (
        P("dp", ENS, ORDER, None),
        P(None, ORDER, None),
        P("dp", ENS, ORDER),
        P(ENS, ORDER),
        P(),
        P(),
    )
    out_specs = (P("dp", ENS, ORDER, None), P(DP_ENS, ORDER, None), P())
    return jax.shard_map(body, mesh=torus, in_specs=in_specs, out_specs=out_specs, check_vma=False)
```
